32 devices in a mesh: row: 4 (over x, core), col: 8 (over z, y).
Axes of the slice: x: 2, y: 2, z: 4, core: 2. Of those that a mesh axis runs over, the one named last changes fastest.
Arguments:
- theta: bfloat16 [2048, 4, 4, 2048], P('row', None, None, 'col'), may hold values from -6 to 6
- gate: bfloat16 [4, 4, 4, 4], replicated, may hold values from -1.5 to 1.5
- warm_start: bfloat16 [8, 4, 2048, 512], P('row', None, 'col'), may hold values from -0.0625 to 0.0625
- slot_sector: int32 [8], replicated, may hold values from 0 to 7, each once
- kept: int32 [8], replicated, may hold values from 128 to 512
- block_offsets: int32 [4, 8], replicated, may hold values from 0 to 480, as said below
Outputs:
- left_factor: float32 [384, 8, 4, 512], P('col', 'row')
- right_factor: float32 [8, 4, 2048, 512], P('row', None, 'col')
The draws below stay inside these ranges and needn't reach their ends.
Inputs may be any that keep to these rules, and one draw needn't show every extreme that they name: `block_offsets`: each device's block lists the sectors in order; every sector has 32 to 96 states in every block, both ends reached; offsets start at 0 and the counts of a block add up to 512.
All inputs are finite; a program needn't handle non-finite values.
Results may differ from the reference program's by a relative error of at most 0.0042.
Values may be sent and summed in bfloat16 or wider, within the bound.
No kernel may reach another device: no remote copies, remote signals or barrier semaphores. Data moves between devices by JAX's collectives and lax.ppermute only.
A program may use at most 512 MiB of HBM per device.

```python
import jax
import jax.numpy as jnp
from jax import lax

MEANC = 64
SPG = 2
CB = 2048
KMAX = 512
NSEC = 8
ROW_DEV = 512
ROWS = 2048
NMAX = 96
SRC = 384


def draw_block_offsets(key, part):
    groups = NSEC // SPG
    pairs = NSEC // 2
    key_order, key_base, key_jitter = jax.random.split(jax.random.fold_in(key, 11), 3)
    order = jax.random.permutation(key_order, NSEC)
    base = jax.random.randint(key_base, (pairs,), 0, MEANC * 3 // 8 + 1)
    base = jnp.where(jnp.arange(pairs) == 0, MEANC // 2, base)
    jitter = jax.random.randint(key_jitter, (groups, pairs), 0, MEANC // 8 + 1)
    extra = jnp.minimum(base[None, :] + jitter, MEANC // 2)
    by_place = jnp.stack([MEANC + extra, MEANC - extra], axis=-1).reshape(groups, NSEC)
    inverse = jnp.argsort(order)
    counts = by_place[:, inverse]
    offsets = jnp.cumsum(counts, axis=1) - counts
    return offsets.astype(jnp.int32)


def place_ends(entries, rng, smallest, largest):
    longest = entries.shape.index(max(entries.shape))
    spots = []
    for shift in (0, 1):
        where = [jax.random.randint(jax.random.fold_in(rng, axis), (), 0, length) for axis, length in enumerate(entries.shape)]
        where[longest] = (where[longest] + shift) % entries.shape[longest]
        spots.append(tuple(where))
    return entries.at[spots[0]].set(smallest).at[spots[1]].set(largest)


def level_of(key, shape, cuts, low, high):
    factor_of, own = 1.0, jax.random.fold_in(key, 6)
    for axis_at, parts in cuts:
        steps = jnp.exp(jax.random.uniform(jax.random.fold_in(own, axis_at), (parts,), jnp.float32, low / len(cuts), high / len(cuts)))
        factor_of = factor_of * jnp.repeat(steps, shape[axis_at] // parts).reshape([-1 if axis == axis_at else 1 for axis in range(len(shape))])
    return factor_of


def gaussian(own_key, dims, spread, limit, cuts=(), held_as=jnp.bfloat16):
    drawn = spread * jax.random.normal(own_key, dims, jnp.float32)
    if cuts:
        drawn = drawn * level_of(own_key, dims, cuts, -0.22, 0.18)
    return jnp.clip(drawn, -limit, limit).astype(held_as)


def setup_inputs(seed: int = 0) -> dict:
    key_of = jax.random.split(jax.random.key(seed), 7)
    return {
        "theta": gaussian(key_of[0], (ROWS, 4, 4, CB), 1.0, 6.0, ((0, 4), (3, 8))),
        "gate": gaussian(key_of[1], (4, 4, 4, 4), 16 ** -0.5, 1.5),
        "warm_start": gaussian(key_of[2], (NSEC, 4, CB, KMAX), (4 * CB) ** -0.5, 0.0625, ((0, 4), (2, 8))),
        "slot_sector": jax.random.permutation(key_of[3], NSEC).astype(jnp.int32),
        "kept": place_ends(jax.random.randint(key_of[4], (NSEC,), KMAX // 4, KMAX + 1), jax.random.fold_in(key_of[4], 1), KMAX // 4, KMAX).astype(jnp.int32),
        "block_offsets": draw_block_offsets(jax.random.fold_in(key_of[6], 71), 0),
    }


damping = 0.25


def refine_step(gram_matrix, correlation, kept_rank):
    identity = jnp.eye(KMAX, dtype=jnp.float32)
    lambdas = jnp.diagonal(gram_matrix) / (jnp.diagonal(correlation) + 1e-6)
    resid = identity - correlation
    differ = lambdas[None, :] - lambdas[:, None]
    divisor = differ * differ + (damping * (lambdas[:, None] + lambdas[None, :])) ** 2 + 1e-6
    offdiag = (gram_matrix + lambdas[None, :] * resid) * differ / divisor
    indices = jnp.arange(KMAX)
    inside = (indices[:, None] < kept_rank) & (indices[None, :] < kept_rank)
    result = jnp.where(identity > 0.5, 0.5 * resid, offdiag)
    return jnp.where(inside, result, jnp.float32(0.0))


def reference(theta, gate, warm_start, slot_sector, kept, block_offsets):
    groups = NSEC // SPG
    closing = jnp.full((groups, 1), ROW_DEV, jnp.int32)
    counts = jnp.concatenate([block_offsets[:, 1:], closing], axis=1) - block_offsets
    places = jnp.arange(NMAX, dtype=jnp.int32)

    def one_slot(slot):
        sector = slot_sector[slot]
        starts = block_offsets[:, sector]
        amounts = counts[:, sector]
        row_index = jnp.minimum(starts[:, None] + places[None, :], ROW_DEV - 1)
        global_rows = (jnp.arange(groups, dtype=jnp.int32)[:, None] * ROW_DEV + row_index).reshape(-1)
        live_mask = (places[None, :] < amounts[:, None]).reshape(-1)
        picked = theta[global_rows]
        gated = jnp.einsum('abef,refc->rabc', gate.astype(jnp.float32), picked.astype(jnp.float32))
        gated = jnp.where(live_mask[:, None, None, None], gated, jnp.float32(0.0)).astype(jnp.bfloat16)
        a_rows = gated.reshape(SRC, 4, 4 * CB)
        vectors = warm_start[slot].reshape(4 * CB, KMAX)
        projected = jnp.einsum('rtn,nk->rtk', a_rows.astype(jnp.float32), vectors.astype(jnp.float32))
        correlation = jnp.dot(vectors.T, vectors, preferred_element_type=jnp.float32)
        projected_b = projected.astype(jnp.bfloat16)
        flattened = projected_b.reshape(SRC * 4, KMAX)
        gram_matrix = jnp.dot(flattened.T, flattened, preferred_element_type=jnp.float32)
        kept_rank = kept[sector]
        corr_b = refine_step(gram_matrix, correlation, kept_rank).astype(jnp.bfloat16)
        kept_mask = (jnp.arange(KMAX) < kept_rank).astype(jnp.float32)
        new_vectors = (vectors.astype(jnp.float32) + jnp.dot(vectors, corr_b, preferred_element_type=jnp.float32)) * kept_mask[None, :]
        left = projected + jnp.einsum('rtk,kl->rtl', projected_b.astype(jnp.float32), corr_b.astype(jnp.float32))
        left = left * kept_mask[None, None, :]
        return left, new_vectors.reshape(4, CB, KMAX)

    lefts, rights = lax.map(one_slot, jnp.arange(NSEC, dtype=jnp.int32))
    return jnp.transpose(lefts, (1, 0, 2, 3)), rights
```

```python
import functools

import jax
import jax.numpy as jnp
from jax import lax
from jax.experimental import pallas as pl
from jax.experimental.pallas import tpu as pltpu
from jax.sharding import PartitionSpec as P

NMAX = 96
CHUNK = 16
damping = 0.25


VMEM = pl.BlockSpec(memory_space=pltpu.VMEM)
SMEM = pl.BlockSpec(memory_space=pltpu.SMEM)
f32, bf16 = jnp.float32, jnp.bfloat16


def swap(value, axis, mask):
    count = lax.axis_size(axis)
    return lax.ppermute(value, axis, [(i, i ^ mask) for i in range(count)])


def product_body(halves, per_group, first_slot, first_far, count, ids, sectors_ref, offsets_ref, theta_hbm, gate_ref, *refs):
    vector_refs = refs[:count]
    sent_ref, kept_ref, theta, mixer, lhs, sem = refs[count:]
    slot, far_half = first_slot + pl.program_id(0), pl.program_id(1)
    block_rows = theta_hbm.shape[0]
    cols = theta.shape[3]
    size = CHUNK * CHUNK
    rows = NMAX // halves

    @pl.when((pl.program_id(0) == 0) & (far_half == 0))
    def _():
        copy = pltpu.make_async_copy(theta_hbm, theta.at[pl.ds(0, block_rows)], sem)
        copy.start()
        theta[pl.ds(block_rows, NMAX)] = jnp.zeros((NMAX,) + theta.shape[1:], theta.dtype)
        tall_row = lax.broadcasted_iota(jnp.int32, (size, CHUNK), 0)
        tall_col = lax.broadcasted_iota(jnp.int32, (size, CHUNK), 1)
        wide_row = lax.broadcasted_iota(jnp.int32, (CHUNK, size), 0)
        wide_col = lax.broadcasted_iota(jnp.int32, (CHUNK, size), 1)
        spread = ((tall_row % 4) * 4 + tall_row // (4 * CHUNK) == tall_col).astype(bf16)
        repeat = (wide_col % CHUNK == wide_row).astype(bf16)
        tall = jnp.dot(spread, gate_ref[...], preferred_element_type=f32).astype(bf16)
        full = jnp.dot(tall, repeat, preferred_element_type=f32)
        row = lax.broadcasted_iota(jnp.int32, (size, size), 0)
        col = lax.broadcasted_iota(jnp.int32, (size, size), 1)
        mixer[...] = jnp.where((row // 4) % CHUNK == col // CHUNK, full, 0.0).astype(bf16)
        copy.wait()

    block = ids[0]
    half = (ids[1] % halves) ^ (1 - far_half)
    for n in range(count):
        sector = sectors_ref[((first_far + n) ^ block) * per_group + slot]
        number = offsets_ref.shape[1]
        start = offsets_ref[block, sector]
        following = offsets_ref[block, jnp.minimum(sector + 1, number - 1)]
        end = jnp.where(sector + 1 < number, following, block_rows)
        start = start + half * rows
        live = jnp.clip(end - start, 0, rows)
        for part in range(rows // CHUNK):
            first = jnp.clip(start + part * CHUNK, 0, block_rows + NMAX - CHUNK)
            piece = theta[pl.ds(first, CHUNK)].reshape(size, cols)
            mixed = jnp.dot(mixer[...], piece, preferred_element_type=f32)
            place = part * CHUNK + lax.broadcasted_iota(jnp.int32, (4 * CHUNK, cols), 0) // 4
            for b in range(4):
                value = mixed[b * 4 * CHUNK : (b + 1) * 4 * CHUNK, :]
                value = jnp.where(place < live, value, 0.0).astype(bf16)
                lhs[pl.ds(part * 4 * CHUNK, 4 * CHUNK), pl.ds(b * cols, cols)] = value
        out = jnp.dot(lhs[...], vector_refs[n][0], preferred_element_type=f32)

        @pl.when(far_half == 0)
        def _():
            sent_ref[0, n] = out.astype(bf16)

        @pl.when(far_half == 1)
        def _():
            kept_ref[0, n] = out


def product(ids, slot_sector, block_offsets, theta, gate, vectors, first_slot, first_far, halves, per_group):
    block_rows, _, _, cols = theta.shape
    slots, depth, most = vectors[0].shape
    rows = NMAX // halves
    count = len(vectors)
    out_block = (1, count, 4 * rows, most)
    return pl.pallas_call(
        functools.partial(product_body, halves, per_group, first_slot, first_far, count),
        out_shape=(
            jax.ShapeDtypeStruct((slots,) + out_block[1:], bf16),
            jax.ShapeDtypeStruct((slots,) + out_block[1:], f32),
        ),
        grid_spec=pltpu.PrefetchScalarGridSpec(
            num_scalar_prefetch=3,
            grid=(slots, halves),
            in_specs=[
                pl.BlockSpec(memory_space=pl.ANY),
                pl.BlockSpec((CHUNK, CHUNK), lambda s, h, *_: (0, 0)),
            ]
            + [pl.BlockSpec((1, depth, most), lambda s, h, *_: (s, 0, 0))] * count,
            out_specs=(
                pl.BlockSpec(out_block, lambda s, h, *_: (s, 0, 0, 0)),
                pl.BlockSpec(out_block, lambda s, h, *_: (s, 0, 0, 0)),
            ),
            scratch_shapes=[
                pltpu.VMEM((block_rows + NMAX,) + theta.shape[1:], bf16),
                pltpu.VMEM((CHUNK * CHUNK, CHUNK * CHUNK), bf16),
                pltpu.VMEM((4 * rows, depth), bf16),
                pltpu.SemaphoreType.DMA,
            ],
        ),
        cost_estimate=pl.CostEstimate(
            flops=slots * count * 6 * 10**8, bytes_accessed=slots * count * 2**21, transcendentals=0
        ),
        name="product",
    )(ids, slot_sector, block_offsets, theta, gate, *vectors)


PACK = 16


def packed(diag):
    high = diag.astype(bf16)
    rest = diag - high.astype(f32)
    middle = rest.astype(bf16)
    low = (rest - middle.astype(f32)).astype(bf16)
    row = lax.broadcasted_iota(jnp.int32, (PACK, diag.shape[1]), 0)
    wide = [jnp.broadcast_to(x.astype(f32), row.shape) for x in (high, middle, low)]
    return jnp.where(row == 0, wide[0], jnp.where(row == 1, wide[1], jnp.where(row == 2, wide[2], 0.0))).astype(bf16)


def unpacked(block):
    return jnp.sum(block.astype(f32), axis=0, keepdims=True)


def gram_body(ids, kept_ref, taken_ref, projected_ref, sent_ref, stays_ref, diag_ref, gram):
    rows, most = stays_ref.shape[1:]
    projected = (kept_ref[...] + taken_ref[...].astype(f32)).astype(bf16)
    projected_ref[...] = projected
    gram[...] = lax.dot_general(projected, projected, (((0,), (0,)), ((), ())), preferred_element_type=f32)
    wide = projected.astype(f32)
    diag = jnp.sum(wide * wide, axis=0, keepdims=True)
    diag_ref[...] = diag
    count = stays_ref.shape[0]
    mine = ids[0] & 1
    for n in range(count):
        stays_ref[n] = gram[pl.ds(pl.multiple_of((2 * n + mine) * rows, rows), rows), :]
        other = gram[pl.ds(pl.multiple_of((2 * n + 1 - mine) * rows, rows), rows), :]
        sent_ref[pl.ds(n * rows, rows), :] = other.astype(bf16)
    sent_ref[pl.ds(count * rows, PACK), :] = packed(diag)


def gram_start(ids, kept, taken, groups):
    depth, most = kept.shape
    rows = most // groups
    count = groups // 2
    return pl.pallas_call(
        gram_body,
        out_shape=(
            jax.ShapeDtypeStruct((depth, most), bf16),
            jax.ShapeDtypeStruct((count * rows + PACK, most), bf16),
            jax.ShapeDtypeStruct((count, rows, most), f32),
            jax.ShapeDtypeStruct((1, most), f32),
        ),
        in_specs=[SMEM, VMEM, VMEM],
        out_specs=(VMEM,) * 4,
        scratch_shapes=[pltpu.VMEM((most, most), f32)],
        cost_estimate=pl.CostEstimate(flops=2 * depth * most * most, bytes_accessed=2**20, transcendentals=0),
        name="gram",
    )(ids, kept, taken)


def gram_step_body(shift, ids, stays_in, taken_ref, diag_in, sent_ref, stays_ref, diag_ref):
    count, rows, most = stays_ref.shape
    before = stays_in.shape[0]
    diag = diag_in[...] + unpacked(taken_ref[pl.ds(before * rows, PACK), :])
    diag_ref[...] = diag
    mine = (ids[0] >> shift) & 1
    for n in range(count):
        if before == count:
            total = stays_in[n] + taken_ref[pl.ds(n * rows, rows), :].astype(f32)
            stays_ref[n] = total
            sent_ref[pl.ds(n * rows, rows), :] = total.astype(bf16)
        else:
            for keep in (0, 1):
                at = 2 * n + jnp.where(keep == 1, mine, 1 - mine)
                total = stays_in[at] + taken_ref[pl.ds(pl.multiple_of(at * rows, rows), rows), :].astype(f32)
                if keep:
                    stays_ref[n] = total
                else:
                    sent_ref[pl.ds(n * rows, rows), :] = total.astype(bf16)
    sent_ref[pl.ds(count * rows, PACK), :] = packed(diag)


def gram_step(ids, stays, taken, diag, shift):
    before, rows, most = stays.shape
    count = max(before // 2, 1)
    return pl.pallas_call(
        functools.partial(gram_step_body, shift),
        out_shape=(
            jax.ShapeDtypeStruct((count * rows + PACK, most), bf16),
            jax.ShapeDtypeStruct((count, rows, most), f32),
            jax.ShapeDtypeStruct((1, most), f32),
        ),
        in_specs=[SMEM, VMEM, VMEM, VMEM],
        out_specs=(VMEM,) * 3,
        cost_estimate=pl.CostEstimate(flops=10**6, bytes_accessed=2**19, transcendentals=0),
        name="gram_step",
    )(ids, stays, taken, diag)


def refine_body(slot, halves, per_group, ids, sectors_ref, kept_ref, stays_ref, taken_ref, gdiag_ref, corr_ref, cdiag_ref, out_ref):
    rows, most = out_ref.shape
    block, col = ids[0], ids[1]
    first = block * rows
    rank = kept_ref[sectors_ref[(col // halves) * per_group + slot]]
    gram = stays_ref[0] + taken_ref[pl.ds(0, rows), :].astype(f32)
    gdiag = gdiag_ref[...] + unpacked(taken_ref[pl.ds(rows, PACK), :])
    cdiag = cdiag_ref[pl.ds(slot, 1), :]
    lam = gdiag / (cdiag + 1e-06)
    i = first + lax.broadcasted_iota(jnp.int32, (rows, most), 0)
    j = lax.broadcasted_iota(jnp.int32, (rows, most), 1)
    lam_j = jnp.broadcast_to(lam, (rows, most))
    lam_i = jnp.sum(jnp.where(i == j, lam_j, 0.0), axis=1, keepdims=True)
    differ = lam_j - lam_i
    total = damping * (lam_i + lam_j)
    divisor = differ * differ + total * total + 1e-06
    offdiag = (gram - lam_j * corr_ref[slot].astype(f32)) * differ / divisor
    result = jnp.where(i == j, 0.5 * (1.0 - cdiag), offdiag)
    inside = (i < rank) & (j < rank)
    out_ref[...] = jnp.where(inside, result, 0.0).astype(bf16)


def refine(slot, ids, slot_sector, kept, stays, taken, gdiag, corr, cdiag, halves, per_group):
    _, rows, most = stays.shape
    return pl.pallas_call(
        functools.partial(refine_body, slot, halves, per_group),
        out_shape=jax.ShapeDtypeStruct((rows, most), bf16),
        in_specs=[SMEM] * 3 + [VMEM] * 5,
        out_specs=VMEM,
        cost_estimate=pl.CostEstimate(flops=10**6, bytes_accessed=2**19, transcendentals=0),
        name="refine",
    )(ids, slot_sector, kept, stays, taken, gdiag, corr, cdiag)


def final_body(slot, per_group, halves, pieces, ids, sectors_ref, kept_ref, vectors_ref, left_ref, *refs):
    piece_refs = refs[:pieces]
    right_out, left_out, corr = refs[-3:]
    rows, most = piece_refs[0].shape
    rank = kept_ref[sectors_ref[ids[0] * per_group + slot]]

    def finish(narrow):
        out = narrow.astype(f32) + jnp.dot(narrow, corr[...], preferred_element_type=f32)
        j = lax.broadcasted_iota(jnp.int32, out.shape, 1)
        return jnp.where(j < rank, out, 0.0)

    @pl.when(pl.program_id(0) == 0)
    def _():
        for k, ref in enumerate(piece_refs):
            at = pl.multiple_of(((ids[1] // halves) ^ k) * rows, rows)
            corr[pl.ds(at, rows), :] = ref[...]
        out = finish(left_ref[...])
        left_out[:, 0] = out.reshape(out.shape[0] // 4, 4, most)

    right_out[0] = finish(vectors_ref[0])


def final(slot, ids, slot_sector, kept, vectors, left, pieces, carried, halves):
    per_group, depth, most = vectors.shape
    tile = depth // 4
    rows = left.shape[0] // 4
    whole = lambda shape: pl.BlockSpec(shape, lambda t, *_: (0,) * len(shape))
    right_shape = jax.ShapeDtypeStruct((per_group, depth, most), f32)
    left_shape = jax.ShapeDtypeStruct((rows, per_group, 4, most), f32)
    in_specs = [
        pl.BlockSpec((1, tile, most), lambda t, *_: (slot, t, 0)),
        whole(left.shape),
    ] + [whole(pieces[0].shape)] * len(pieces)
    operands = [vectors, left] + list(pieces)
    aliases = {}
    if carried is not None:
        aliases = {3 + len(operands): 0, 4 + len(operands): 1}
        in_specs += [pl.BlockSpec(memory_space=pl.ANY)] * 2
        operands += list(carried)
    return pl.pallas_call(
        functools.partial(final_body, slot, per_group, halves, len(pieces)),
        out_shape=(right_shape, left_shape),
        grid_spec=pltpu.PrefetchScalarGridSpec(
            num_scalar_prefetch=3,
            grid=(depth // tile,),
            in_specs=in_specs,
            out_specs=(
                pl.BlockSpec((1, tile, most), lambda t, *_: (slot, t, 0)),
                pl.BlockSpec((rows, 1, 4, most), lambda t, *_: (0, slot, 0, 0)),
            ),
            scratch_shapes=[pltpu.VMEM((most, most), bf16)],
        ),
        input_output_aliases=aliases,
        cost_estimate=pl.CostEstimate(flops=2 * 1216 * most * most, bytes_accessed=4 * 2**20, transcendentals=0),
        name="final",
    )(ids, slot_sector, kept, *operands)


def halve(low, high, axis, mask, choose_high):
    sent = jnp.where(choose_high, low, high).astype(bf16)
    stays = jnp.where(choose_high, high, low).astype(f32)
    return stays, swap(sent, axis, mask)


def shards(theta, gate, warm_start, slot_sector, kept, block_offsets):
    groups, cols = lax.axis_size("row"), lax.axis_size("col")
    block, col = lax.axis_index("row"), lax.axis_index("col")
    halves = cols // groups
    per_group, _, bond_cols, most = warm_start.shape
    group_bits = groups.bit_length() - 1
    ids = jnp.stack([block, col]).astype(jnp.int32)
    vectors = warm_start.reshape(per_group, 4 * bond_cols, most)
    group = col // halves
    gate_matrix = gate.reshape(CHUNK, CHUNK)

    partner = swap(vectors, "row", 1)
    across = []
    remaining = vectors
    for s in range(per_group):
        own = remaining[s : s + 1]
        own, remaining = lax.optimization_barrier((own, remaining))
        across.append({d: swap(own, "row", d) for d in range(2, groups, 2)})

    corr = jnp.einsum("snk,snl->skl", vectors, vectors, preferred_element_type=f32)
    cdiag = jnp.sum(jnp.square(vectors.astype(f32)), axis=1)
    corr = corr.reshape(per_group, groups, most // groups, most)
    for t in range(group_bits):
        parts = corr.reshape((per_group, corr.shape[1] // 2, 2) + corr.shape[2:])
        stays, taken = halve(parts[:, :, 0], parts[:, :, 1], "col", halves << t, (group >> t) & 1 != 0)
        corr = stays + taken.astype(f32)
        cdiag = cdiag + swap(cdiag, "col", halves << t)
    corr = corr.reshape(per_group, most // groups, most)
    for t in range(halves.bit_length() - 1):
        corr = corr + swap(corr.astype(bf16), "col", 1 << t).astype(f32)
        cdiag = cdiag + swap(cdiag, "col", 1 << t)

    def place(b, g, h):
        return b * cols + g * halves + h

    def turned(value, k=0):
        pairs = [
            (place(b, g, h), place(g, b ^ k, h))
            for b in range(groups)
            for g in range(groups)
            for h in range(halves)
        ]
        return lax.ppermute(value, ("row", "col"), pairs)

    corr, cdiag = turned(corr.astype(bf16)), turned(cdiag)

    def reduced(first_slot, first_far, operands):
        sent, stays = product(
            ids, slot_sector, block_offsets, theta, gate_matrix, operands, first_slot, first_far, halves, per_group
        )
        taken = swap(sent, "col", 1)
        value = stays + taken.astype(f32)
        for t in range(group_bits - 1):
            parts = value.reshape((value.shape[0], value.shape[1] // 2, 2) + value.shape[2:])
            wanted = ((group ^ block) >> t) & 1 != 0
            stays, taken = halve(parts[:, :, 0], parts[:, :, 1], "col", halves << t, wanted)
            value = stays + taken.astype(f32)
        return value[:, 0]

    near = [vectors, partner]
    for d in range(2, groups // 2, 2):
        arrived = jnp.concatenate([across[s][d] for s in range(per_group)])
        near += [arrived, swap(arrived, "row", 1)]
    near = reduced(0, 0, near)
    last = group_bits - 1
    carried = None
    for s in range(per_group):
        far = []
        for d in range(groups // 2, groups, 2):
            far += [across[s][d], swap(across[s][d], "row", 1)]
        far = reduced(s, groups // 2, far)[0]
        wanted = ((group ^ block) >> last) & 1 != 0
        stays, taken = halve(near[s], far, "col", halves << last, wanted)
        projected, sent, stays, diag = gram_start(ids, stays, taken, groups)
        for t in range(1, group_bits + 1):
            taken = swap(sent, "row", 1 << (t - 1))
            sent, stays, diag = gram_step(ids, stays, taken, diag, t)
        taken = swap(sent, "col", 1)
        step = refine(s, ids, slot_sector, kept, stays, taken, diag, corr, cdiag, halves, per_group)
        left = turned(projected)
        pieces = [turned(step, k) for k in range(groups)]
        carried = final(s, ids, slot_sector, kept, vectors, left, pieces, carried, halves)
    right, left = carried
    return left, right.reshape(warm_start.shape)


def solution(mesh):
    in_specs = (P("row", None, None, "col"), P(), P("row", None, "col", None), P(), P(), P())
    out_specs = (P("col", "row", None, None), P("row", None, "col", None))
    return jax.shard_map(shards, mesh=mesh, in_specs=in_specs, out_specs=out_specs, check_vma=False)
```

```python
import functools

import jax
import jax.numpy as jnp
from jax import lax
from jax.experimental import pallas as pl
from jax.experimental.pallas import tpu as pltpu
from jax.sharding import PartitionSpec as P


NMAX = 96
CHUNK = 16
MIB = 2**20
damping = 0.25


VMEM = pl.BlockSpec(memory_space=pltpu.VMEM)
SMEM = pl.BlockSpec(memory_space=pltpu.SMEM)
f32, bf16 = jnp.float32, jnp.bfloat16


def swap(value, axis, mask):
    count = lax.axis_size(axis)
    return lax.ppermute(value, axis, [(i, i ^ mask) for i in range(count)])


def window(ids, sectors_ref, offsets_ref, block_rows, far, slot, half, rows, per_group):
    block = ids[0]
    sector = sectors_ref[(far ^ block) * per_group + slot]
    number = offsets_ref.shape[1]
    start = offsets_ref[block, sector]
    following = offsets_ref[block, jnp.minimum(sector + 1, number - 1)]
    end = jnp.where(sector + 1 < number, following, block_rows)
    start = start + half * rows
    return start, jnp.clip(end - start, 0, rows)


def prepare(theta_hbm, gate_ref, theta, mixer, sem):
    block_rows = theta_hbm.shape[0]
    size = CHUNK * CHUNK
    copy = pltpu.make_async_copy(theta_hbm, theta.at[pl.ds(0, block_rows)], sem)
    copy.start()
    theta[pl.ds(block_rows, NMAX)] = jnp.zeros((NMAX,) + theta.shape[1:], theta.dtype)
    tall_row = lax.broadcasted_iota(jnp.int32, (size, CHUNK), 0)
    tall_col = lax.broadcasted_iota(jnp.int32, (size, CHUNK), 1)
    wide_row = lax.broadcasted_iota(jnp.int32, (CHUNK, size), 0)
    wide_col = lax.broadcasted_iota(jnp.int32, (CHUNK, size), 1)
    spread = ((tall_row % 4) * 4 + tall_row // (4 * CHUNK) == tall_col).astype(bf16)
    repeat = (wide_col % CHUNK == wide_row).astype(bf16)
    tall = jnp.dot(spread, gate_ref[...], preferred_element_type=f32).astype(bf16)
    full = jnp.dot(tall, repeat, preferred_element_type=f32)
    row = lax.broadcasted_iota(jnp.int32, (size, size), 0)
    col = lax.broadcasted_iota(jnp.int32, (size, size), 1)
    mixer[...] = jnp.where((row // 4) % CHUNK == col // CHUNK, full, 0.0).astype(bf16)
    copy.wait()


def gated_window(theta, mixer, start, live, rows, store):
    size = CHUNK * CHUNK
    cols = theta.shape[3]
    for part in range(rows // CHUNK):
        first = jnp.clip(start + part * CHUNK, 0, theta.shape[0] - CHUNK)
        piece = theta[pl.ds(first, CHUNK)].reshape(size, cols)
        mixed = jnp.dot(mixer[...], piece, preferred_element_type=f32)
        place = part * CHUNK + lax.broadcasted_iota(jnp.int32, (4 * CHUNK, cols), 0) // 4
        for b in range(4):
            value = mixed[b * 4 * CHUNK : (b + 1) * 4 * CHUNK, :]
            value = jnp.where(place < live, value, 0.0).astype(bf16)
            store(pl.ds(part * 4 * CHUNK, 4 * CHUNK), pl.ds(b * cols, cols), value)


def theta_scratch(theta):
    return [
        pltpu.VMEM((theta.shape[0] + NMAX,) + theta.shape[1:], bf16),
        pltpu.VMEM((CHUNK * CHUNK, CHUNK * CHUNK), bf16),
        pltpu.SemaphoreType.DMA,
    ]


def near_body(halves, per_group, count, ids, sectors_ref, offsets_ref, theta_hbm, gate_ref, *refs):
    vector_refs = refs[:count]
    sent_ref, kept_ref, theta, mixer, sem, lhs = refs[count:]
    slot = pl.program_id(0)
    rows = NMAX // halves

    @pl.when(slot == 0)
    def _():
        prepare(theta_hbm, gate_ref, theta, mixer, sem)

    for n in range(count):
        for far_half in (0, 1):
            half = (ids[1] % halves) ^ (1 - far_half)
            start, live = window(ids, sectors_ref, offsets_ref, theta_hbm.shape[0], n, slot, half, rows, per_group)

            def store(at, cols, value, base=far_half * 4 * rows):
                lhs[pl.ds(base + at.start, at.size), cols] = value

            gated_window(theta, mixer, start, live, rows, store)
        out = jnp.dot(lhs[...], vector_refs[n][0], preferred_element_type=f32)
        sent_ref[0, n] = out[: 4 * rows].astype(bf16)
        kept_ref[0, n] = out[4 * rows :]


def near_product(ids, slot_sector, block_offsets, theta, gate, vectors, halves, per_group):
    slots, depth, most = vectors[0].shape
    rows = NMAX // halves
    count = len(vectors)
    out_block = (1, count, 4 * rows, most)
    return pl.pallas_call(
        functools.partial(near_body, halves, per_group, count),
        out_shape=(
            jax.ShapeDtypeStruct((slots,) + out_block[1:], bf16),
            jax.ShapeDtypeStruct((slots,) + out_block[1:], f32),
        ),
        grid_spec=pltpu.PrefetchScalarGridSpec(
            num_scalar_prefetch=3,
            grid=(slots,),
            in_specs=[
                pl.BlockSpec(memory_space=pl.ANY),
                pl.BlockSpec((CHUNK, CHUNK), lambda s, *_: (0, 0)),
            ]
            + [pl.BlockSpec((1, depth, most), lambda s, *_: (s, 0, 0))] * count,
            out_specs=(
                pl.BlockSpec(out_block, lambda s, *_: (s, 0, 0, 0)),
                pl.BlockSpec(out_block, lambda s, *_: (s, 0, 0, 0)),
            ),
            scratch_shapes=theta_scratch(theta) + [pltpu.VMEM((halves * 4 * rows, depth), bf16)],
        ),
        cost_estimate=pl.CostEstimate(
            flops=slots * count * 12 * 10**8, bytes_accessed=slots * count * 2**21, transcendentals=0
        ),
        compiler_params=pltpu.CompilerParams(vmem_limit_bytes=24 * MIB),
        name="near",
    )(ids, slot_sector, block_offsets, theta, gate, *vectors)


def gate_body(halves, per_group, first_far, ids, sectors_ref, offsets_ref, theta_hbm, gate_ref, out_ref, theta, mixer, sem):
    slot, n = pl.program_id(0), pl.program_id(1)
    rows = NMAX // halves

    @pl.when((slot == 0) & (n == 0))
    def _():
        prepare(theta_hbm, gate_ref, theta, mixer, sem)

    for far_half in (0, 1):
        half = (ids[1] % halves) ^ (1 - far_half)
        start, live = window(
            ids, sectors_ref, offsets_ref, theta_hbm.shape[0], first_far + n, slot, half, rows, per_group
        )

        def store(at, cols, value, base=far_half * 4 * rows):
            out_ref[0, 0, pl.ds(base + at.start, at.size), cols] = value

        gated_window(theta, mixer, start, live, rows, store)


def gate_rows(ids, slot_sector, block_offsets, theta, gate, count, first_far, halves, per_group):
    rows, cols = NMAX // halves, theta.shape[3]
    block = (1, 1, halves * 4 * rows, 4 * cols)
    return pl.pallas_call(
        functools.partial(gate_body, halves, per_group, first_far),
        out_shape=jax.ShapeDtypeStruct((per_group, count) + block[2:], bf16),
        grid_spec=pltpu.PrefetchScalarGridSpec(
            num_scalar_prefetch=3,
            grid=(per_group, count),
            in_specs=[
                pl.BlockSpec(memory_space=pl.ANY),
                pl.BlockSpec((CHUNK, CHUNK), lambda s, n, *_: (0, 0)),
            ],
            out_specs=pl.BlockSpec(block, lambda s, n, *_: (s, n, 0, 0)),
            scratch_shapes=theta_scratch(theta),
        ),
        cost_estimate=pl.CostEstimate(flops=4 * 10**9, bytes_accessed=8 * 2**20, transcendentals=0),
        compiler_params=pltpu.CompilerParams(vmem_limit_bytes=12 * MIB),
        name="gate_rows",
    )(ids, slot_sector, block_offsets, theta, gate)


def far_body(count, lhs_ref, *refs):
    vector_refs = refs[:count]
    sent_ref, kept_ref = refs[count:]
    rows = sent_ref.shape[2]
    for n in range(count):
        out = jnp.dot(lhs_ref[0, n], vector_refs[n][0], preferred_element_type=f32)
        sent_ref[0, n] = out[:rows].astype(bf16)
        kept_ref[0, n] = out[rows:]


def far_product(slot, gated, vectors):
    _, count, rows, depth = gated.shape
    most = vectors[0].shape[2]
    out_block = (1, count, rows // 2, most)
    return pl.pallas_call(
        functools.partial(far_body, count),
        out_shape=(jax.ShapeDtypeStruct(out_block, bf16), jax.ShapeDtypeStruct(out_block, f32)),
        grid=(1,),
        in_specs=[pl.BlockSpec((1, count, rows, depth), lambda i: (slot, 0, 0, 0))]
        + [pl.BlockSpec((1, depth, most), lambda i: (0, 0, 0))] * count,
        out_specs=(pl.BlockSpec(out_block, lambda i: (0, 0, 0, 0)),) * 2,
        cost_estimate=pl.CostEstimate(flops=8 * 10**8, bytes_accessed=5 * 2**20, transcendentals=0),
        compiler_params=pltpu.CompilerParams(vmem_limit_bytes=16 * MIB),
        name="far",
    )(gated, *vectors)


PACK = 16


def packed(diag):
    high = diag.astype(bf16)
    rest = diag - high.astype(f32)
    middle = rest.astype(bf16)
    low = (rest - middle.astype(f32)).astype(bf16)
    row = lax.broadcasted_iota(jnp.int32, (PACK, diag.shape[1]), 0)
    wide = [jnp.broadcast_to(x.astype(f32), row.shape) for x in (high, middle, low)]
    return jnp.where(row == 0, wide[0], jnp.where(row == 1, wide[1], jnp.where(row == 2, wide[2], 0.0))).astype(bf16)


def unpacked(block):
    return jnp.sum(block.astype(f32), axis=0, keepdims=True)


def step_body(shift, halves, by_col, arrived, diagonal, ids, *refs):
    stays_in, refs = refs[0], refs[1:]
    if arrived:
        taken_ref, diag_in, refs = refs[0], refs[1], refs[2:]
    sent_ref, stays_ref, diag_ref = refs
    slots, count, rows, most = stays_ref.shape
    before = stays_in.shape[1]
    mine = ((ids[1] // halves if by_col else ids[0]) >> shift) & 1
    for s in range(slots):
        if diagonal:
            diag = jnp.zeros((1, most), f32)
            for n in range(before):
                i = n * rows + lax.broadcasted_iota(jnp.int32, (rows, most), 0)
                j = lax.broadcasted_iota(jnp.int32, (rows, most), 1)
                diag = diag + jnp.sum(jnp.where(i == j, stays_in[s, n], 0.0), axis=0, keepdims=True)
        else:
            diag = diag_in[s] + unpacked(taken_ref[s, pl.ds(before * rows, PACK), :])
        diag_ref[s] = diag

        def total(at):
            value = stays_in[s, at]
            if arrived:
                value = value + taken_ref[s, pl.ds(pl.multiple_of(at * rows, rows), rows), :].astype(f32)
            return value

        for n in range(count):
            if before == count:
                value = total(n)
                stays_ref[s, n] = value
            else:
                stays_ref[s, n] = total(2 * n + mine)
                value = total(2 * n + 1 - mine)
            sent_ref[s, pl.ds(n * rows, rows), :] = value.astype(bf16)
        sent_ref[s, pl.ds(count * rows, PACK), :] = packed(diag)


def step(ids, stays, taken, diag, shift, by_col, halves):
    slots, before, rows, most = stays.shape
    count = max(before // 2, 1)
    arrived = taken is not None
    operands = [stays] + ([taken, diag] if arrived else [])
    return pl.pallas_call(
        functools.partial(step_body, shift, halves, by_col, arrived, not arrived),
        out_shape=(
            jax.ShapeDtypeStruct((slots, count * rows + PACK, most), bf16),
            jax.ShapeDtypeStruct((slots, count, rows, most), f32),
            jax.ShapeDtypeStruct((slots, 1, most), f32),
        ),
        in_specs=[SMEM] + [VMEM] * len(operands),
        out_specs=(VMEM,) * 3,
        cost_estimate=pl.CostEstimate(flops=10**6, bytes_accessed=2**19, transcendentals=0),
        compiler_params=pltpu.CompilerParams(vmem_limit_bytes=8 * MIB),
    )(ids, *operands)


def gram_body(ids, stays_in, taken_ref, projected_ref, sent_ref, stays_ref, diag_ref, gram):
    _, count, rows, _ = stays_ref.shape
    projected = (stays_in[0, 0] + taken_ref[0, 0].astype(f32)).astype(bf16)
    projected_ref[...] = projected
    gram[...] = lax.dot_general(projected, projected, (((0,), (0,)), ((), ())), preferred_element_type=f32)
    wide = projected.astype(f32)
    diag = jnp.sum(wide * wide, axis=0, keepdims=True)
    diag_ref[0] = diag
    mine = ids[0] & 1
    for n in range(count):
        stays_ref[0, n] = gram[pl.ds(pl.multiple_of((2 * n + mine) * rows, rows), rows), :]
        other = gram[pl.ds(pl.multiple_of((2 * n + 1 - mine) * rows, rows), rows), :]
        sent_ref[0, pl.ds(n * rows, rows), :] = other.astype(bf16)
    sent_ref[0, pl.ds(count * rows, PACK), :] = packed(diag)


def gram_split(ids, stays, taken, groups):
    depth, most = stays.shape[2:]
    rows, count = most // groups, groups // 2
    return pl.pallas_call(
        gram_body,
        out_shape=(
            jax.ShapeDtypeStruct((depth, most), bf16),
            jax.ShapeDtypeStruct((1, count * rows + PACK, most), bf16),
            jax.ShapeDtypeStruct((1, count, rows, most), f32),
            jax.ShapeDtypeStruct((1, 1, most), f32),
        ),
        in_specs=[SMEM, VMEM, VMEM],
        out_specs=(VMEM,) * 4,
        scratch_shapes=[pltpu.VMEM((most, most), f32)],
        cost_estimate=pl.CostEstimate(flops=2 * depth * most * most, bytes_accessed=2**20, transcendentals=0),
        compiler_params=pltpu.CompilerParams(vmem_limit_bytes=6 * MIB),
        name="gram_split",
    )(ids, stays, taken)


def refine_body(slot, halves, per_group, ids, sectors_ref, kept_ref, stays_ref, taken_ref, gdiag_ref, corr_ref, out_ref):
    rows, most = out_ref.shape
    block, col = ids[0], ids[1]
    first = block * rows
    rank = kept_ref[sectors_ref[(col // halves) * per_group + slot]]
    gram = stays_ref[0, 0] + taken_ref[0, pl.ds(0, rows), :].astype(f32)
    gdiag = gdiag_ref[0] + unpacked(taken_ref[0, pl.ds(rows, PACK), :])
    cdiag = unpacked(corr_ref[slot, pl.ds(rows, PACK), :])
    lam = gdiag / (cdiag + 1e-06)
    i = first + lax.broadcasted_iota(jnp.int32, (rows, most), 0)
    j = lax.broadcasted_iota(jnp.int32, (rows, most), 1)
    lam_j = jnp.broadcast_to(lam, (rows, most))
    lam_i = jnp.sum(jnp.where(i == j, lam_j, 0.0), axis=1, keepdims=True)
    differ = lam_j - lam_i
    total = damping * (lam_i + lam_j)
    divisor = differ * differ + total * total + 1e-06
    offdiag = (gram - lam_j * corr_ref[slot, pl.ds(0, rows), :].astype(f32)) * differ / divisor
    result = jnp.where(i == j, 0.5 * (1.0 - cdiag), offdiag)
    inside = (i < rank) & (j < rank)
    out_ref[...] = jnp.where(inside, result, 0.0).astype(bf16)


def refine(slot, ids, slot_sector, kept, stays, taken, gdiag, corr, halves, per_group):
    _, _, rows, most = stays.shape
    return pl.pallas_call(
        functools.partial(refine_body, slot, halves, per_group),
        out_shape=jax.ShapeDtypeStruct((rows, most), bf16),
        in_specs=[SMEM] * 3 + [VMEM] * 4,
        out_specs=VMEM,
        cost_estimate=pl.CostEstimate(flops=10**6, bytes_accessed=2**19, transcendentals=0),
        compiler_params=pltpu.CompilerParams(vmem_limit_bytes=4 * MIB),
        name="refine",
    )(ids, slot_sector, kept, stays, taken, gdiag, corr)


def final_body(slot, per_group, halves, pieces, ids, sectors_ref, kept_ref, vectors_ref, left_ref, *refs):
    piece_refs = refs[:pieces]
    right_out, left_out, corr = refs[-3:]
    rows, most = piece_refs[0].shape
    rank = kept_ref[sectors_ref[ids[0] * per_group + slot]]

    def finish(narrow):
        out = narrow.astype(f32) + jnp.dot(narrow, corr[...], preferred_element_type=f32)
        j = lax.broadcasted_iota(jnp.int32, out.shape, 1)
        return jnp.where(j < rank, out, 0.0)

    @pl.when(pl.program_id(0) == 0)
    def _():
        for k, ref in enumerate(piece_refs):
            at = pl.multiple_of(((ids[1] // halves) ^ k) * rows, rows)
            corr[pl.ds(at, rows), :] = ref[...]
        out = finish(left_ref[...])
        left_out[:, 0] = out.reshape(out.shape[0] // 4, 4, most)

    right_out[0] = finish(vectors_ref[0])


def final(slot, ids, slot_sector, kept, vectors, left, pieces, carried, halves):
    per_group, depth, most = vectors.shape
    tile = depth // 2
    rows = left.shape[0] // 4
    whole = lambda shape: pl.BlockSpec(shape, lambda t, *_: (0,) * len(shape))
    right_shape = jax.ShapeDtypeStruct((per_group, depth, most), f32)
    left_shape = jax.ShapeDtypeStruct((rows, per_group, 4, most), f32)
    in_specs = [
        pl.BlockSpec((1, tile, most), lambda t, *_: (slot, t, 0)),
        whole(left.shape),
    ] + [whole(pieces[0].shape)] * len(pieces)
    operands = [vectors, left] + list(pieces)
    aliases = {}
    if carried is not None:
        aliases = {3 + len(operands): 0, 4 + len(operands): 1}
        in_specs += [pl.BlockSpec(memory_space=pl.ANY)] * 2
        operands += list(carried)
    return pl.pallas_call(
        functools.partial(final_body, slot, per_group, halves, len(pieces)),
        out_shape=(right_shape, left_shape),
        grid_spec=pltpu.PrefetchScalarGridSpec(
            num_scalar_prefetch=3,
            grid=(depth // tile,),
            in_specs=in_specs,
            out_specs=(
                pl.BlockSpec((1, tile, most), lambda t, *_: (slot, t, 0)),
                pl.BlockSpec((rows, 1, 4, most), lambda t, *_: (0, slot, 0, 0)),
            ),
            scratch_shapes=[pltpu.VMEM((most, most), bf16)],
        ),
        input_output_aliases=aliases,
        cost_estimate=pl.CostEstimate(flops=2 * 1216 * most * most, bytes_accessed=4 * 2**20, transcendentals=0),
        compiler_params=pltpu.CompilerParams(vmem_limit_bytes=12 * MIB),
        name="final",
    )(ids, slot_sector, kept, *operands)


def halve_body(shift, halves, slot, ids, stays_in, taken_in, *refs):
    other, (sent_ref, stays_ref) = refs[:-2], refs[-2:]
    want = (((ids[1] // halves) ^ ids[0]) >> shift) & 1
    for s in range(stays_ref.shape[0]):
        for n in range(stays_ref.shape[1]):
            if other:
                low = stays_in[slot, 0] + taken_in[slot, 0].astype(f32)
                high = other[0][0, 0] + other[1][0, 0].astype(f32)
                stays_ref[s, n] = jnp.where(want == 1, high, low)
                sent_ref[s, n] = jnp.where(want == 1, low, high).astype(bf16)
            else:
                at = 2 * n + want
                stays_ref[s, n] = stays_in[s, at] + taken_in[s, at].astype(f32)
                at = 2 * n + 1 - want
                sent_ref[s, n] = (stays_in[s, at] + taken_in[s, at].astype(f32)).astype(bf16)


def halve(ids, shift, halves, value, other=None, slot=0):
    slots, count, rows, most = value[0].shape
    shape = (1, 1, rows, most) if other else (slots, count // 2, rows, most)
    operands = list(value) + list(other or ())
    return pl.pallas_call(
        functools.partial(halve_body, shift, halves, slot),
        out_shape=(jax.ShapeDtypeStruct(shape, bf16), jax.ShapeDtypeStruct(shape, f32)),
        in_specs=[SMEM] + [VMEM] * len(operands),
        out_specs=(VMEM,) * 2,
        cost_estimate=pl.CostEstimate(flops=10**6, bytes_accessed=2**20, transcendentals=0),
        compiler_params=pltpu.CompilerParams(vmem_limit_bytes=8 * MIB),
    )(ids, *operands)


def work(theta, gate, warm_start, slot_sector, kept, block_offsets):
    groups, cols = lax.axis_size("row"), lax.axis_size("col")
    block, col = lax.axis_index("row"), lax.axis_index("col")
    halves = cols // groups
    per_group, _, bond_cols, most = warm_start.shape
    group_bits = groups.bit_length() - 1
    ids = jnp.stack([block, col]).astype(jnp.int32)
    vectors = warm_start.reshape(per_group, 4 * bond_cols, most)
    gate_matrix = gate.reshape(CHUNK, CHUNK)

    across = []
    remaining = vectors
    for s in range(per_group):
        own = remaining[s : s + 1]
        own, remaining = lax.optimization_barrier((own, remaining))
        across.append({d: swap(own, "row", d) for d in range(2, groups, 2)})
    partner = swap(vectors, "row", 1)

    def place(b, g, h):
        return b * cols + g * halves + h

    def turned(value, k=0):
        pairs = [
            (place(b, g, h), place(g, b ^ k, h))
            for b in range(groups)
            for g in range(groups)
            for h in range(halves)
        ]
        return lax.ppermute(value, ("row", "col"), pairs)

    corr = jnp.einsum("snk,snl->skl", vectors, vectors, preferred_element_type=f32)
    corr = corr.reshape(per_group, groups, most // groups, most)
    sent, stays, diag = step(ids, corr, None, None, 0, True, halves)
    for t in range(1, group_bits + 1):
        taken = swap(sent, "col", halves << (t - 1))
        sent, stays, diag = step(ids, stays, taken, diag, t, True, halves)
    taken = swap(sent, "col", 1)
    sent, _, _ = step(ids, stays, taken, diag, 0, True, halves)
    corr = turned(sent)

    def reduced(sent, stays):
        taken = swap(sent, "col", 1)
        for t in range(group_bits - 1):
            sent, stays = halve(ids, t, halves, (stays, taken))
            taken = swap(sent, "col", halves << t)
        return stays, taken

    near = [vectors, partner]
    for d in range(2, groups // 2, 2):
        arrived = jnp.concatenate([across[s][d] for s in range(per_group)])
        near += [arrived, swap(arrived, "row", 1)]
    near = near_product(ids, slot_sector, block_offsets, theta, gate_matrix, near, halves, per_group)
    near = reduced(*near)
    gated = gate_rows(ids, slot_sector, block_offsets, theta, gate_matrix, groups // 2, groups // 2, halves, per_group)
    last = group_bits - 1
    carried = None
    for s in range(per_group):
        far = []
        for d in range(groups // 2, groups, 2):
            far += [across[s][d], swap(across[s][d], "row", 1)]
        far = far_product(s, gated, far)
        far = reduced(*far)
        sent, stays = halve(ids, last, halves, near, far, s)
        taken = swap(sent, "col", halves << last)
        projected, sent, stays, diag = gram_split(ids, stays, taken, groups)
        left = turned(projected)
        for t in range(1, group_bits + 1):
            taken = swap(sent, "row", 1 << (t - 1))
            sent, stays, diag = step(ids, stays, taken, diag, t, False, halves)
        taken = swap(sent, "col", 1)
        piece = refine(s, ids, slot_sector, kept, stays, taken, diag, corr, halves, per_group)
        pieces = []
        for k in range(groups):
            pieces.append(turned(piece, k))
        carried = final(s, ids, slot_sector, kept, vectors, left, pieces, carried, halves)
    right, left = carried
    return left, right.reshape(warm_start.shape)


def solution(mesh):
    in_specs = (P("row", None, None, "col"), P(), P("row", None, "col", None), P(), P(), P())
    out_specs = (P("col", "row", None, None), P("row", None, "col", None))
    return jax.shard_map(work, mesh=mesh, in_specs=in_specs, out_specs=out_specs, check_vma=False)
```

```python
import functools

import jax
import jax.numpy as jnp
from jax import lax
from jax.experimental import pallas as pl
from jax.experimental.pallas import tpu as pltpu
from jax.sharding import PartitionSpec as P


NMAX = 96
CHUNK = 16
MIB = 2**20
damping = 0.25


VMEM = pl.BlockSpec(memory_space=pltpu.VMEM)
SMEM = pl.BlockSpec(memory_space=pltpu.SMEM)
f32, bf16 = jnp.float32, jnp.bfloat16


def swap(value, axis, mask):
    count = lax.axis_size(axis)
    return lax.ppermute(value, axis, [(i, i ^ mask) for i in range(count)])


def window(ids, sectors_ref, offsets_ref, block_rows, far, slot, half, rows, per_group):
    block = ids[0]
    sector = sectors_ref[(far ^ block) * per_group + slot]
    number = offsets_ref.shape[1]
    start = offsets_ref[block, sector]
    following = offsets_ref[block, jnp.minimum(sector + 1, number - 1)]
    end = jnp.where(sector + 1 < number, following, block_rows)
    start = start + half * rows
    return start, jnp.clip(end - start, 0, rows)


def prepare(theta_hbm, gate_ref, theta, mixer, sem):
    block_rows = theta_hbm.shape[0]
    size = CHUNK * CHUNK
    copy = pltpu.make_async_copy(theta_hbm, theta.at[pl.ds(0, block_rows)], sem)
    copy.start()
    theta[pl.ds(block_rows, NMAX)] = jnp.zeros((NMAX,) + theta.shape[1:], theta.dtype)
    tall_row = lax.broadcasted_iota(jnp.int32, (size, CHUNK), 0)
    tall_col = lax.broadcasted_iota(jnp.int32, (size, CHUNK), 1)
    wide_row = lax.broadcasted_iota(jnp.int32, (CHUNK, size), 0)
    wide_col = lax.broadcasted_iota(jnp.int32, (CHUNK, size), 1)
    spread = ((tall_row % 4) * 4 + tall_row // (4 * CHUNK) == tall_col).astype(bf16)
    repeat = (wide_col % CHUNK == wide_row).astype(bf16)
    tall = jnp.dot(spread, gate_ref[...], preferred_element_type=f32).astype(bf16)
    full = jnp.dot(tall, repeat, preferred_element_type=f32)
    row = lax.broadcasted_iota(jnp.int32, (size, size), 0)
    col = lax.broadcasted_iota(jnp.int32, (size, size), 1)
    mixer[...] = jnp.where((row // 4) % CHUNK == col // CHUNK, full, 0.0).astype(bf16)
    copy.wait()


def gated_window(theta, mixer, start, live, rows, store):
    size = CHUNK * CHUNK
    cols = theta.shape[3]
    for part in range(rows // CHUNK):
        first = jnp.clip(start + part * CHUNK, 0, theta.shape[0] - CHUNK)
        piece = theta[pl.ds(first, CHUNK)].reshape(size, cols)
        mixed = jnp.dot(mixer[...], piece, preferred_element_type=f32)
        place = part * CHUNK + lax.broadcasted_iota(jnp.int32, (4 * CHUNK, cols), 0) // 4
        for b in range(4):
            value = mixed[b * 4 * CHUNK : (b + 1) * 4 * CHUNK, :]
            value = jnp.where(place < live, value, 0.0).astype(bf16)
            store(pl.ds(part * 4 * CHUNK, 4 * CHUNK), pl.ds(b * cols, cols), value)


def theta_scratch(theta):
    return [
        pltpu.VMEM((theta.shape[0] + NMAX,) + theta.shape[1:], bf16),
        pltpu.VMEM((CHUNK * CHUNK, CHUNK * CHUNK), bf16),
        pltpu.SemaphoreType.DMA,
    ]


def near_body(halves, per_group, count, ids, sectors_ref, offsets_ref, theta_hbm, gate_ref, *refs):
    vector_refs = refs[:count]
    sent_ref, kept_ref, theta, mixer, sem, lhs = refs[count:]
    slot = pl.program_id(0)
    rows = NMAX // halves

    @pl.when(slot == 0)
    def _():
        prepare(theta_hbm, gate_ref, theta, mixer, sem)

    for n in range(count):
        for far_half in (0, 1):
            half = (ids[1] % halves) ^ (1 - far_half)
            start, live = window(ids, sectors_ref, offsets_ref, theta_hbm.shape[0], n, slot, half, rows, per_group)

            def store(at, cols, value, base=far_half * 4 * rows):
                lhs[pl.ds(base + at.start, at.size), cols] = value

            gated_window(theta, mixer, start, live, rows, store)
        out = jnp.dot(lhs[...], vector_refs[n][0], preferred_element_type=f32)
        sent_ref[0, n] = out[: 4 * rows].astype(bf16)
        kept_ref[0, n] = out[4 * rows :]


def near_product(ids, slot_sector, block_offsets, theta, gate, vectors, halves, per_group):
    slots, depth, most = vectors[0].shape
    rows = NMAX // halves
    count = len(vectors)
    out_block = (1, count, 4 * rows, most)
    return pl.pallas_call(
        functools.partial(near_body, halves, per_group, count),
        out_shape=(
            jax.ShapeDtypeStruct((slots,) + out_block[1:], bf16),
            jax.ShapeDtypeStruct((slots,) + out_block[1:], f32),
        ),
        grid_spec=pltpu.PrefetchScalarGridSpec(
            num_scalar_prefetch=3,
            grid=(slots,),
            in_specs=[
                pl.BlockSpec(memory_space=pl.ANY),
                pl.BlockSpec((CHUNK, CHUNK), lambda s, *_: (0, 0)),
            ]
            + [pl.BlockSpec((1, depth, most), lambda s, *_: (s, 0, 0))] * count,
            out_specs=(
                pl.BlockSpec(out_block, lambda s, *_: (s, 0, 0, 0)),
                pl.BlockSpec(out_block, lambda s, *_: (s, 0, 0, 0)),
            ),
            scratch_shapes=theta_scratch(theta) + [pltpu.VMEM((halves * 4 * rows, depth), bf16)],
        ),
        cost_estimate=pl.CostEstimate(
            flops=slots * count * 12 * 10**8, bytes_accessed=slots * count * 2**21, transcendentals=0
        ),
        compiler_params=pltpu.CompilerParams(vmem_limit_bytes=24 * MIB),
        name="near",
    )(ids, slot_sector, block_offsets, theta, gate, *vectors)


def gate_body(halves, per_group, first_far, ids, sectors_ref, offsets_ref, theta_hbm, gate_ref, out_ref, theta, mixer, sem):
    slot, n = pl.program_id(0), pl.program_id(1)
    rows = NMAX // halves

    @pl.when((slot == 0) & (n == 0))
    def _():
        prepare(theta_hbm, gate_ref, theta, mixer, sem)

    for far_half in (0, 1):
        half = (ids[1] % halves) ^ (1 - far_half)
        start, live = window(
            ids, sectors_ref, offsets_ref, theta_hbm.shape[0], first_far + n, slot, half, rows, per_group
        )

        def store(at, cols, value, base=far_half * 4 * rows):
            out_ref[0, 0, pl.ds(base + at.start, at.size), cols] = value

        gated_window(theta, mixer, start, live, rows, store)


def gate_rows(ids, slot_sector, block_offsets, theta, gate, count, first_far, halves, per_group):
    rows, cols = NMAX // halves, theta.shape[3]
    block = (1, 1, halves * 4 * rows, 4 * cols)
    return pl.pallas_call(
        functools.partial(gate_body, halves, per_group, first_far),
        out_shape=jax.ShapeDtypeStruct((per_group, count) + block[2:], bf16),
        grid_spec=pltpu.PrefetchScalarGridSpec(
            num_scalar_prefetch=3,
            grid=(per_group, count),
            in_specs=[
                pl.BlockSpec(memory_space=pl.ANY),
                pl.BlockSpec((CHUNK, CHUNK), lambda s, n, *_: (0, 0)),
            ],
            out_specs=pl.BlockSpec(block, lambda s, n, *_: (s, n, 0, 0)),
            scratch_shapes=theta_scratch(theta),
        ),
        cost_estimate=pl.CostEstimate(flops=4 * 10**9, bytes_accessed=8 * 2**20, transcendentals=0),
        compiler_params=pltpu.CompilerParams(vmem_limit_bytes=12 * MIB),
        name="gate_rows",
    )(ids, slot_sector, block_offsets, theta, gate)


def far_body(count, lhs_ref, *refs):
    vector_refs = refs[:count]
    sent_ref, kept_ref = refs[count:]
    rows = sent_ref.shape[2]
    for n in range(count):
        out = jnp.dot(lhs_ref[0, n], vector_refs[n][0], preferred_element_type=f32)
        sent_ref[0, n] = out[:rows].astype(bf16)
        kept_ref[0, n] = out[rows:]


def far_product(slot, gated, vectors):
    _, count, rows, depth = gated.shape
    most = vectors[0].shape[2]
    out_block = (1, count, rows // 2, most)
    return pl.pallas_call(
        functools.partial(far_body, count),
        out_shape=(jax.ShapeDtypeStruct(out_block, bf16), jax.ShapeDtypeStruct(out_block, f32)),
        grid=(1,),
        in_specs=[pl.BlockSpec((1, count, rows, depth), lambda i: (slot, 0, 0, 0))]
        + [pl.BlockSpec((1, depth, most), lambda i: (0, 0, 0))] * count,
        out_specs=(pl.BlockSpec(out_block, lambda i: (0, 0, 0, 0)),) * 2,
        cost_estimate=pl.CostEstimate(flops=8 * 10**8, bytes_accessed=5 * 2**20, transcendentals=0),
        compiler_params=pltpu.CompilerParams(vmem_limit_bytes=16 * MIB),
        name="far",
    )(gated, *vectors)


PACK = 16


def packed(diag):
    high = diag.astype(bf16)
    rest = diag - high.astype(f32)
    middle = rest.astype(bf16)
    low = (rest - middle.astype(f32)).astype(bf16)
    row = lax.broadcasted_iota(jnp.int32, (PACK, diag.shape[1]), 0)
    wide = [jnp.broadcast_to(x.astype(f32), row.shape) for x in (high, middle, low)]
    return jnp.where(row == 0, wide[0], jnp.where(row == 1, wide[1], jnp.where(row == 2, wide[2], 0.0))).astype(bf16)


def unpacked(block):
    return jnp.sum(block.astype(f32), axis=0, keepdims=True)


def bit_of(ids, which, halves):
    source, shift = which
    value = {"row": ids[0], "group": ids[1] // halves, "half": ids[1] % halves}[source]
    return (value >> shift) & 1


def corr_body(halves, ids, corr_ref, sent_ref, stays_ref, diag_ref):
    slots, count, rows, most = stays_ref.shape
    mine = ids[1] % halves
    for s in range(slots):
        diag = jnp.zeros((1, most), f32)
        for n in range(count * halves):
            i = n * rows + lax.broadcasted_iota(jnp.int32, (rows, most), 0)
            j = lax.broadcasted_iota(jnp.int32, (rows, most), 1)
            diag = diag + jnp.sum(jnp.where(i == j, corr_ref[s, n], 0.0), axis=0, keepdims=True)
        diag_ref[s] = diag
        for n in range(count):
            stays_ref[s, n] = corr_ref[s, halves * n + mine]
            sent_ref[s, pl.ds(n * rows, rows), :] = corr_ref[s, halves * n + 1 - mine].astype(bf16)
        sent_ref[s, pl.ds(count * rows, PACK), :] = packed(diag)


def corr_split(ids, corr, halves):
    slots, count, rows, most = corr.shape
    count = count // halves
    return pl.pallas_call(
        functools.partial(corr_body, halves),
        out_shape=(
            jax.ShapeDtypeStruct((slots, count * rows + PACK, most), bf16),
            jax.ShapeDtypeStruct((slots, count, rows, most), f32),
            jax.ShapeDtypeStruct((slots, 1, most), f32),
        ),
        in_specs=[SMEM, VMEM],
        out_specs=(VMEM,) * 3,
        cost_estimate=pl.CostEstimate(flops=10**6, bytes_accessed=2**21, transcendentals=0),
        compiler_params=pltpu.CompilerParams(vmem_limit_bytes=8 * MIB),
        name="corr_split",
    )(ids, corr)


def step_body(which, halves, ids, stays_in, taken_ref, diag_in, sent_ref, stays_ref, diag_ref):
    slots, count, rows, _ = stays_ref.shape
    before, block = stays_in.shape[1:3]
    mine = bit_of(ids, which, halves) if which else 0
    for s in range(slots):
        diag = diag_in[s] + unpacked(taken_ref[s, pl.ds(before * block, PACK), :])
        diag_ref[s] = diag

        def total(at, first=0):
            there = pl.multiple_of(at * block + first, rows)
            return stays_in[s, at, pl.ds(first, rows), :] + taken_ref[s, pl.ds(there, rows), :].astype(f32)

        for n in range(count):
            if not which:
                value = total(n)
                stays_ref[s, n] = value
            elif block != rows:
                stays_ref[s, n] = total(n, pl.multiple_of(mine * rows, rows))
                value = total(n, pl.multiple_of((1 - mine) * rows, rows))
            else:
                stays_ref[s, n] = total(2 * n + mine)
                value = total(2 * n + 1 - mine)
            sent_ref[s, pl.ds(n * rows, rows), :] = value.astype(bf16)
        sent_ref[s, pl.ds(count * rows, PACK), :] = packed(diag)


def step(ids, stays, taken, diag, which, halves):
    slots, count, rows, most = stays.shape
    if which and which[0] == "half":
        rows = rows // halves
    elif which:
        count = count // 2
    return pl.pallas_call(
        functools.partial(step_body, which, halves),
        out_shape=(
            jax.ShapeDtypeStruct((slots, count * rows + PACK, most), bf16),
            jax.ShapeDtypeStruct((slots, count, rows, most), f32),
            jax.ShapeDtypeStruct((slots, 1, most), f32),
        ),
        in_specs=[SMEM] + [VMEM] * 3,
        out_specs=(VMEM,) * 3,
        cost_estimate=pl.CostEstimate(flops=10**6, bytes_accessed=2**19, transcendentals=0),
        compiler_params=pltpu.CompilerParams(vmem_limit_bytes=8 * MIB),
    )(ids, stays, taken, diag)


def gram_body(parts, ids, *refs):
    projected_ref, sent_ref, stays_ref, diag_ref, gram = refs[2 * parts :]
    _, count, rows, most = stays_ref.shape
    width = most // parts
    for n in range(parts):
        part = (refs[2 * n][0, 0] + refs[2 * n + 1][0, 0].astype(f32)).astype(bf16)
        projected_ref[:, n * width : (n + 1) * width] = part
    projected = projected_ref[...]
    gram[...] = lax.dot_general(projected, projected, (((0,), (0,)), ((), ())), preferred_element_type=f32)
    wide = projected.astype(f32)
    diag = jnp.sum(wide * wide, axis=0, keepdims=True)
    diag_ref[0] = diag
    mine = ids[0] & 1
    for n in range(count):
        stays_ref[0, n] = gram[pl.ds(pl.multiple_of((2 * n + mine) * rows, rows), rows), :]
        other = gram[pl.ds(pl.multiple_of((2 * n + 1 - mine) * rows, rows), rows), :]
        sent_ref[0, pl.ds(n * rows, rows), :] = other.astype(bf16)
    sent_ref[0, pl.ds(count * rows, PACK), :] = packed(diag)


def gram_split(ids, values, groups):
    depth, most = values[0][0].shape[2:]
    most = most * len(values)
    rows, count = most // groups, groups // 2
    operands = [x for value in values for x in value]
    return pl.pallas_call(
        functools.partial(gram_body, len(values)),
        out_shape=(
            jax.ShapeDtypeStruct((depth, most), bf16),
            jax.ShapeDtypeStruct((1, count * rows + PACK, most), bf16),
            jax.ShapeDtypeStruct((1, count, rows, most), f32),
            jax.ShapeDtypeStruct((1, 1, most), f32),
        ),
        in_specs=[SMEM] + [VMEM] * len(operands),
        out_specs=(VMEM,) * 4,
        scratch_shapes=[pltpu.VMEM((most, most), f32)],
        cost_estimate=pl.CostEstimate(flops=2 * depth * most * most, bytes_accessed=2**20, transcendentals=0),
        compiler_params=pltpu.CompilerParams(vmem_limit_bytes=6 * MIB),
        name="gram_split",
    )(ids, *operands)


def refine_body(slot, halves, per_group, ids, sectors_ref, kept_ref, stays_ref, taken_ref, gdiag_ref, corr_ref, out_ref):
    rows, most = out_ref.shape
    block, col = ids[0], ids[1]
    first = (block * halves + col % halves) * rows
    rank = kept_ref[sectors_ref[(col // halves) * per_group + slot]]
    gram = stays_ref[0, 0] + taken_ref[0, pl.ds(0, rows), :].astype(f32)
    gdiag = gdiag_ref[0] + unpacked(taken_ref[0, pl.ds(rows, PACK), :])
    cdiag = unpacked(corr_ref[0, pl.ds(rows, PACK), :])
    lam = gdiag / (cdiag + 1e-06)
    i = first + lax.broadcasted_iota(jnp.int32, (rows, most), 0)
    j = lax.broadcasted_iota(jnp.int32, (rows, most), 1)
    lam_j = jnp.broadcast_to(lam, (rows, most))
    lam_i = jnp.sum(jnp.where(i == j, lam_j, 0.0), axis=1, keepdims=True)
    differ = lam_j - lam_i
    total = damping * (lam_i + lam_j)
    divisor = differ * differ + total * total + 1e-06
    offdiag = (gram - lam_j * corr_ref[0, pl.ds(0, rows), :].astype(f32)) * differ / divisor
    result = jnp.where(i == j, 0.5 * (1.0 - cdiag), offdiag)
    inside = (i < rank) & (j < rank)
    out_ref[...] = jnp.where(inside, result, 0.0).astype(bf16)


def refine(slot, ids, slot_sector, kept, stays, taken, gdiag, corr, halves, per_group):
    _, _, rows, most = stays.shape
    return pl.pallas_call(
        functools.partial(refine_body, slot, halves, per_group),
        out_shape=jax.ShapeDtypeStruct((rows, most), bf16),
        in_specs=[SMEM] * 3 + [VMEM] * 4,
        out_specs=VMEM,
        cost_estimate=pl.CostEstimate(flops=10**6, bytes_accessed=2**19, transcendentals=0),
        compiler_params=pltpu.CompilerParams(vmem_limit_bytes=4 * MIB),
        name="refine",
    )(ids, slot_sector, kept, stays, taken, gdiag, corr)


def final_body(slot, per_group, halves, pieces, ids, sectors_ref, kept_ref, vectors_ref, left_ref, *refs):
    piece_refs = refs[:pieces]
    right_out, left_out, corr = refs[-3:]
    rows, most = piece_refs[0].shape
    rank = kept_ref[sectors_ref[ids[0] * per_group + slot]]

    def finish(narrow):
        out = narrow.astype(f32) + jnp.dot(narrow, corr[...], preferred_element_type=f32)
        j = lax.broadcasted_iota(jnp.int32, out.shape, 1)
        return jnp.where(j < rank, out, 0.0)

    @pl.when(pl.program_id(0) == 0)
    def _():
        half = ids[1] % halves
        for k in range(pieces - 1):
            at = ((ids[1] // halves) ^ k) * halves
            corr[pl.ds(pl.multiple_of((at + half) * rows, rows), rows), :] = piece_refs[k][...]
            other = piece_refs[-1][pl.ds(k * rows, rows), :]
            corr[pl.ds(pl.multiple_of((at + 1 - half) * rows, rows), rows), :] = other
        out = finish(left_ref[...])
        left_out[:, 0] = out.reshape(out.shape[0] // 4, 4, most)

    right_out[0] = finish(vectors_ref[0])


def final(slot, ids, slot_sector, kept, vectors, left, pieces, carried, halves):
    per_group, depth, most = vectors.shape
    tile = depth // 2
    rows = left.shape[0] // 4
    whole = lambda shape: pl.BlockSpec(shape, lambda t, *_: (0,) * len(shape))
    right_shape = jax.ShapeDtypeStruct((per_group, depth, most), f32)
    left_shape = jax.ShapeDtypeStruct((rows, per_group, 4, most), f32)
    in_specs = [
        pl.BlockSpec((1, tile, most), lambda t, *_: (slot, t, 0)),
        whole(left.shape),
    ] + [whole(piece.shape) for piece in pieces]
    operands = [vectors, left] + list(pieces)
    aliases = {}
    if carried is not None:
        aliases = {3 + len(operands): 0, 4 + len(operands): 1}
        in_specs += [pl.BlockSpec(memory_space=pl.ANY)] * 2
        operands += list(carried)
    return pl.pallas_call(
        functools.partial(final_body, slot, per_group, halves, len(pieces)),
        out_shape=(right_shape, left_shape),
        grid_spec=pltpu.PrefetchScalarGridSpec(
            num_scalar_prefetch=3,
            grid=(depth // tile,),
            in_specs=in_specs,
            out_specs=(
                pl.BlockSpec((1, tile, most), lambda t, *_: (slot, t, 0)),
                pl.BlockSpec((rows, 1, 4, most), lambda t, *_: (0, slot, 0, 0)),
            ),
            scratch_shapes=[pltpu.VMEM((most, most), bf16)],
        ),
        input_output_aliases=aliases,
        cost_estimate=pl.CostEstimate(flops=2 * 1216 * most * most, bytes_accessed=4 * 2**20, transcendentals=0),
        compiler_params=pltpu.CompilerParams(vmem_limit_bytes=12 * MIB),
        name="final",
    )(ids, slot_sector, kept, *operands)


def halve_body(shift, halves, slot, first, ids, stays_in, taken_in, *refs):
    other, (sent_ref, stays_ref) = refs[:-2], refs[-2:]
    most = stays_ref.shape[3]
    want = (((ids[1] // halves) ^ ids[0]) >> shift) & 1
    for s in range(stays_ref.shape[0]):
        for n in range(stays_ref.shape[1]):
            if other:
                part = pl.ds(first, most)
                low = stays_in[slot, 0, :, part] + taken_in[slot, 0, :, part].astype(f32)
                high = other[0][0, 0] + other[1][0, 0].astype(f32)
                stays_ref[s, n] = jnp.where(want == 1, high, low)
                sent_ref[s, n] = jnp.where(want == 1, low, high).astype(bf16)
            else:
                at = 2 * n + want
                stays_ref[s, n] = stays_in[s, at] + taken_in[s, at].astype(f32)
                at = 2 * n + 1 - want
                sent_ref[s, n] = (stays_in[s, at] + taken_in[s, at].astype(f32)).astype(bf16)


def halve(ids, shift, halves, value, other=None, slot=0, first=0):
    slots, count, rows, most = (other or value)[0].shape
    shape = (1, 1, rows, most) if other else (slots, count // 2, rows, most)
    operands = list(value) + list(other or ())
    return pl.pallas_call(
        functools.partial(halve_body, shift, halves, slot, first),
        out_shape=(jax.ShapeDtypeStruct(shape, bf16), jax.ShapeDtypeStruct(shape, f32)),
        in_specs=[SMEM] + [VMEM] * len(operands),
        out_specs=(VMEM,) * 2,
        cost_estimate=pl.CostEstimate(flops=10**6, bytes_accessed=2**20, transcendentals=0),
        compiler_params=pltpu.CompilerParams(vmem_limit_bytes=8 * MIB),
    )(ids, *operands)


def work(theta, gate, warm_start, slot_sector, kept, block_offsets):
    groups, cols = lax.axis_size("row"), lax.axis_size("col")
    block, col = lax.axis_index("row"), lax.axis_index("col")
    halves = cols // groups
    per_group, _, bond_cols, most = warm_start.shape
    group_bits = groups.bit_length() - 1
    ids = jnp.stack([block, col]).astype(jnp.int32)
    vectors = warm_start.reshape(per_group, 4 * bond_cols, most)
    gate_matrix = gate.reshape(CHUNK, CHUNK)

    parts = [1] * (per_group - 1) + [2]

    across = {}
    remaining = vectors
    for s in range(per_group):
        width = most // parts[s]
        for p in range(parts[s]):
            own = remaining[s : s + 1, :, p * width : (p + 1) * width]
            own, remaining = lax.optimization_barrier((own, remaining))
            across[s, p] = {d: swap(own, "row", d) for d in range(2, groups, 2)}
    partner = swap(vectors, "row", 1)

    def place(b, g, h):
        return b * cols + g * halves + h

    def turned(value, k=0, hop=0):
        pairs = [
            (place(b ^ hop, g, h), place(g, b ^ k, h))
            for b in range(groups)
            for g in range(groups)
            for h in range(halves)
        ]
        return lax.ppermute(value, ("row", "col"), pairs)

    def turned_over(value):
        value = swap(value, "row", groups // 2)
        return turned(value, 0, groups // 2)

    corr = jnp.einsum("snk,snl->skl", vectors, vectors, preferred_element_type=f32)
    corr = corr.reshape(per_group, cols, most // cols, most)
    sent, stays, diag = corr_split(ids, corr, halves)
    taken = swap(sent, "col", 1)
    for t in range(group_bits):
        sent, stays, diag = step(ids, stays, taken, diag, ("group", t), halves)
        taken = swap(sent, "col", halves << t)
    sent, _, _ = step(ids, stays, taken, diag, None, halves)
    corr = []
    for s in range(per_group):
        if s == 0:
            corr.append(turned(sent[s : s + 1]))
        else:
            corr.append(turned_over(sent[s : s + 1]))

    def reduced(sent, stays):
        taken = swap(sent, "col", 1)
        for t in range(group_bits - 1):
            sent, stays = halve(ids, t, halves, (stays, taken))
            taken = swap(sent, "col", halves << t)
        return stays, taken

    near = [vectors, partner]
    for d in range(2, groups // 2, 2):
        arrived = []
        for s in range(per_group):
            arrived.append(jnp.concatenate([across[s, p][d] for p in range(parts[s])], axis=2))
        arrived = jnp.concatenate(arrived)
        near += [arrived, swap(arrived, "row", 1)]
    near = near_product(ids, slot_sector, block_offsets, theta, gate_matrix, near, halves, per_group)
    near = reduced(*near)
    gated = gate_rows(ids, slot_sector, block_offsets, theta, gate_matrix, groups // 2, groups // 2, halves, per_group)
    last = group_bits - 1
    carried = None
    for s in range(per_group):
        values = []
        for p in range(parts[s]):
            far = []
            for d in range(groups // 2, groups, 2):
                far += [across[s, p][d], swap(across[s, p][d], "row", 1)]
            far = far_product(s, gated, far)
            far = reduced(*far)
            sent, stays = halve(ids, last, halves, near, far, s, p * (most // parts[s]))
            values.append((stays, swap(sent, "col", halves << last)))
        projected, sent, stays, diag = gram_split(ids, values, groups)
        if s == per_group - 1:
            left = turned(projected)
        else:
            left = turned_over(projected)
        for t in range(1, group_bits + 1):
            taken = swap(sent, "row", 1 << (t - 1))
            which = ("row", t) if t < group_bits else ("half", 0)
            sent, stays, diag = step(ids, stays, taken, diag, which, halves)
        taken = swap(sent, "col", 1)
        piece = refine(s, ids, slot_sector, kept, stays, taken, diag, corr[s], halves, per_group)
        pieces = []
        for k in range(groups):
            pieces.append(turned(piece, k))
        pieces.append(swap(jnp.concatenate(pieces), "col", 1))
        carried = final(s, ids, slot_sector, kept, vectors, left, pieces, carried, halves)
    right, left = carried
    return left, right.reshape(warm_start.shape)


def solution(mesh):
    in_specs = (P("row", None, None, "col"), P(), P("row", None, "col", None), P(), P(), P())
    out_specs = (P("col", "row", None, None), P("row", None, "col", None))
    return jax.shard_map(work, mesh=mesh, in_specs=in_specs, out_specs=out_specs, check_vma=False)
```

```python
import functools

import jax
import jax.numpy as jnp
from jax import lax
from jax.experimental import pallas as pl
from jax.experimental.pallas import tpu as pltpu
from jax.sharding import PartitionSpec as P


NMAX = 96
CHUNK = 16
MIB = 2**20
damping = 0.25


VMEM = pl.BlockSpec(memory_space=pltpu.VMEM)
SMEM = pl.BlockSpec(memory_space=pltpu.SMEM)
f32, bf16 = jnp.float32, jnp.bfloat16


def swap(value, axis, mask):
    count = lax.axis_size(axis)
    return lax.ppermute(value, axis, [(i, i ^ mask) for i in range(count)])


def window(ids, sectors_ref, offsets_ref, block_rows, far, slot, half, rows, per_group):
    block = ids[0]
    sector = sectors_ref[(far ^ block) * per_group + slot]
    number = offsets_ref.shape[1]
    start = offsets_ref[block, sector]
    following = offsets_ref[block, jnp.minimum(sector + 1, number - 1)]
    end = jnp.where(sector + 1 < number, following, block_rows)
    start = start + half * rows
    return start, jnp.clip(end - start, 0, rows)


def prepare(theta_hbm, gate_ref, theta, mixer, sem):
    block_rows = theta_hbm.shape[0]
    size = CHUNK * CHUNK
    copy = pltpu.make_async_copy(theta_hbm, theta.at[pl.ds(0, block_rows)], sem)
    copy.start()
    theta[pl.ds(block_rows, NMAX)] = jnp.zeros((NMAX,) + theta.shape[1:], theta.dtype)
    tall_row = lax.broadcasted_iota(jnp.int32, (size, CHUNK), 0)
    tall_col = lax.broadcasted_iota(jnp.int32, (size, CHUNK), 1)
    wide_row = lax.broadcasted_iota(jnp.int32, (CHUNK, size), 0)
    wide_col = lax.broadcasted_iota(jnp.int32, (CHUNK, size), 1)
    spread = ((tall_row % 4) * 4 + tall_row // (4 * CHUNK) == tall_col).astype(bf16)
    repeat = (wide_col % CHUNK == wide_row).astype(bf16)
    tall = jnp.dot(spread, gate_ref[...], preferred_element_type=f32).astype(bf16)
    full = jnp.dot(tall, repeat, preferred_element_type=f32)
    row = lax.broadcasted_iota(jnp.int32, (size, size), 0)
    col = lax.broadcasted_iota(jnp.int32, (size, size), 1)
    mixer[...] = jnp.where((row // 4) % CHUNK == col // CHUNK, full, 0.0).astype(bf16)
    copy.wait()


def gated_window(theta, mixer, start, live, rows, store):
    size = CHUNK * CHUNK
    cols = theta.shape[3]
    for part in range(rows // CHUNK):
        first = jnp.clip(start + part * CHUNK, 0, theta.shape[0] - CHUNK)
        piece = theta[pl.ds(first, CHUNK)].reshape(size, cols)
        mixed = jnp.dot(mixer[...], piece, preferred_element_type=f32)
        place = part * CHUNK + lax.broadcasted_iota(jnp.int32, (4 * CHUNK, cols), 0) // 4
        for b in range(4):
            value = mixed[b * 4 * CHUNK : (b + 1) * 4 * CHUNK, :]
            value = jnp.where(place < live, value, 0.0).astype(bf16)
            store(pl.ds(part * 4 * CHUNK, 4 * CHUNK), pl.ds(b * cols, cols), value)


def theta_scratch(theta):
    return [
        pltpu.VMEM((theta.shape[0] + NMAX,) + theta.shape[1:], bf16),
        pltpu.VMEM((CHUNK * CHUNK, CHUNK * CHUNK), bf16),
        pltpu.SemaphoreType.DMA,
    ]


def gate_body(halves, per_group, ids, sectors_ref, offsets_ref, theta_hbm, gate_ref, out_ref, theta, mixer, sem):
    slot, n = pl.program_id(0), pl.program_id(1)
    rows = NMAX // halves

    @pl.when((slot == 0) & (n == 0))
    def _():
        prepare(theta_hbm, gate_ref, theta, mixer, sem)

    for far_half in (0, 1):
        half = (ids[1] % halves) ^ (1 - far_half)
        start, live = window(
            ids, sectors_ref, offsets_ref, theta_hbm.shape[0], n, slot, half, rows, per_group
        )

        def store(at, cols, value, base=far_half * 4 * rows):
            out_ref[0, 0, pl.ds(base + at.start, at.size), cols] = value

        gated_window(theta, mixer, start, live, rows, store)


def gate_rows(ids, slot_sector, block_offsets, theta, gate, count, halves, per_group):
    rows, cols = NMAX // halves, theta.shape[3]
    block = (1, 1, halves * 4 * rows, 4 * cols)
    return pl.pallas_call(
        functools.partial(gate_body, halves, per_group),
        out_shape=jax.ShapeDtypeStruct((per_group, count) + block[2:], bf16),
        grid_spec=pltpu.PrefetchScalarGridSpec(
            num_scalar_prefetch=3,
            grid=(per_group, count),
            in_specs=[
                pl.BlockSpec(memory_space=pl.ANY),
                pl.BlockSpec((CHUNK, CHUNK), lambda s, n, *_: (0, 0)),
            ],
            out_specs=pl.BlockSpec(block, lambda s, n, *_: (s, n, 0, 0)),
            scratch_shapes=theta_scratch(theta),
        ),
        cost_estimate=pl.CostEstimate(flops=6 * 10**9, bytes_accessed=12 * 2**20, transcendentals=0),
        compiler_params=pltpu.CompilerParams(vmem_limit_bytes=14 * MIB),
        name="gate_rows",
    )(ids, slot_sector, block_offsets, theta, gate)


def product_body(count, lhs_ref, *refs):
    vector_refs = refs[:count]
    sent_ref, kept_ref = refs[count:]
    rows = sent_ref.shape[2]
    for n in range(count):
        out = jnp.dot(lhs_ref[0, n], vector_refs[n][0], preferred_element_type=f32)
        sent_ref[0, n] = out[:rows].astype(bf16)
        kept_ref[0, n] = out[rows:]


def product(slot, chunk, gated, vectors):
    _, _, rows, depth = gated.shape
    count = len(vectors)
    most = vectors[0].shape[2]
    out_block = (1, count, rows // 2, most)
    return pl.pallas_call(
        functools.partial(product_body, count),
        out_shape=(jax.ShapeDtypeStruct(out_block, bf16), jax.ShapeDtypeStruct(out_block, f32)),
        grid=(1,),
        in_specs=[pl.BlockSpec((1, count, rows, depth), lambda i: (slot, chunk, 0, 0))]
        + [pl.BlockSpec((1, depth, most), lambda i, at=min(slot, v.shape[0] - 1): (at, 0, 0)) for v in vectors],
        out_specs=(pl.BlockSpec(out_block, lambda i: (0, 0, 0, 0)),) * 2,
        cost_estimate=pl.CostEstimate(flops=8 * 10**8, bytes_accessed=5 * 2**20, transcendentals=0),
        compiler_params=pltpu.CompilerParams(vmem_limit_bytes=16 * MIB),
    )(gated, *vectors)


PACK = 16


def packed(diag):
    high = diag.astype(bf16)
    rest = diag - high.astype(f32)
    middle = rest.astype(bf16)
    low = (rest - middle.astype(f32)).astype(bf16)
    row = lax.broadcasted_iota(jnp.int32, (PACK, diag.shape[1]), 0)
    wide = [jnp.broadcast_to(x.astype(f32), row.shape) for x in (high, middle, low)]
    return jnp.where(row == 0, wide[0], jnp.where(row == 1, wide[1], jnp.where(row == 2, wide[2], 0.0))).astype(bf16)


def unpacked(block):
    return jnp.sum(block.astype(f32), axis=0, keepdims=True)


def bit_of(ids, which, halves):
    source, shift = which
    value = {"row": ids[0], "group": ids[1] // halves, "half": ids[1] % halves}[source]
    return (value >> shift) & 1


def corr_body(halves, ids, corr_ref, sent_ref, stays_ref, diag_ref):
    slots, count, rows, most = stays_ref.shape
    mine = ids[1] % halves
    for s in range(slots):
        diag = jnp.zeros((1, most), f32)
        for n in range(count * halves):
            i = n * rows + lax.broadcasted_iota(jnp.int32, (rows, most), 0)
            j = lax.broadcasted_iota(jnp.int32, (rows, most), 1)
            diag = diag + jnp.sum(jnp.where(i == j, corr_ref[s, n], 0.0), axis=0, keepdims=True)
        diag_ref[s] = diag
        for n in range(count):
            stays_ref[s, n] = corr_ref[s, halves * n + mine]
            sent_ref[s, pl.ds(n * rows, rows), :] = corr_ref[s, halves * n + 1 - mine].astype(bf16)
        sent_ref[s, pl.ds(count * rows, PACK), :] = packed(diag)


def corr_split(ids, corr, halves):
    slots, count, rows, most = corr.shape
    count = count // halves
    return pl.pallas_call(
        functools.partial(corr_body, halves),
        out_shape=(
            jax.ShapeDtypeStruct((slots, count * rows + PACK, most), bf16),
            jax.ShapeDtypeStruct((slots, count, rows, most), f32),
            jax.ShapeDtypeStruct((slots, 1, most), f32),
        ),
        in_specs=[SMEM, VMEM],
        out_specs=(VMEM,) * 3,
        cost_estimate=pl.CostEstimate(flops=10**6, bytes_accessed=2**21, transcendentals=0),
        compiler_params=pltpu.CompilerParams(vmem_limit_bytes=8 * MIB),
        name="corr_split",
    )(ids, corr)


def step_body(which, halves, ids, stays_in, taken_ref, diag_in, sent_ref, stays_ref, diag_ref):
    slots, count, rows, _ = stays_ref.shape
    before, block = stays_in.shape[1:3]
    mine = bit_of(ids, which, halves) if which else 0
    for s in range(slots):
        diag = diag_in[s] + unpacked(taken_ref[s, pl.ds(before * block, PACK), :])
        diag_ref[s] = diag

        def total(at, first=0):
            there = pl.multiple_of(at * block + first, rows)
            return stays_in[s, at, pl.ds(first, rows), :] + taken_ref[s, pl.ds(there, rows), :].astype(f32)

        for n in range(count):
            if not which:
                value = total(n)
                stays_ref[s, n] = value
            elif block != rows:
                stays_ref[s, n] = total(n, pl.multiple_of(mine * rows, rows))
                value = total(n, pl.multiple_of((1 - mine) * rows, rows))
            else:
                stays_ref[s, n] = total(2 * n + mine)
                value = total(2 * n + 1 - mine)
            sent_ref[s, pl.ds(n * rows, rows), :] = value.astype(bf16)
        sent_ref[s, pl.ds(count * rows, PACK), :] = packed(diag)


def step(ids, stays, taken, diag, which, halves):
    slots, count, rows, most = stays.shape
    if which and which[0] == "half":
        rows = rows // halves
    elif which:
        count = count // 2
    return pl.pallas_call(
        functools.partial(step_body, which, halves),
        out_shape=(
            jax.ShapeDtypeStruct((slots, count * rows + PACK, most), bf16),
            jax.ShapeDtypeStruct((slots, count, rows, most), f32),
            jax.ShapeDtypeStruct((slots, 1, most), f32),
        ),
        in_specs=[SMEM] + [VMEM] * 3,
        out_specs=(VMEM,) * 3,
        cost_estimate=pl.CostEstimate(flops=10**6, bytes_accessed=2**19, transcendentals=0),
        compiler_params=pltpu.CompilerParams(vmem_limit_bytes=8 * MIB),
    )(ids, stays, taken, diag)


def gram_body(parts, ids, *refs):
    projected_ref, sent_ref, stays_ref, diag_ref, gram = refs[2 * parts :]
    _, count, rows, most = stays_ref.shape
    width = most // parts
    for n in range(parts):
        part = (refs[2 * n][0, 0] + refs[2 * n + 1][0, 0].astype(f32)).astype(bf16)
        projected_ref[:, n * width : (n + 1) * width] = part
    projected = projected_ref[...]
    gram[...] = lax.dot_general(projected, projected, (((0,), (0,)), ((), ())), preferred_element_type=f32)
    wide = projected.astype(f32)
    diag = jnp.sum(wide * wide, axis=0, keepdims=True)
    diag_ref[0] = diag
    mine = ids[0] & 1
    for n in range(count):
        stays_ref[0, n] = gram[pl.ds(pl.multiple_of((2 * n + mine) * rows, rows), rows), :]
        other = gram[pl.ds(pl.multiple_of((2 * n + 1 - mine) * rows, rows), rows), :]
        sent_ref[0, pl.ds(n * rows, rows), :] = other.astype(bf16)
    sent_ref[0, pl.ds(count * rows, PACK), :] = packed(diag)


def gram_split(ids, values, groups):
    depth, most = values[0][0].shape[2:]
    most = most * len(values)
    rows, count = most // groups, groups // 2
    operands = [x for value in values for x in value]
    return pl.pallas_call(
        functools.partial(gram_body, len(values)),
        out_shape=(
            jax.ShapeDtypeStruct((depth, most), bf16),
            jax.ShapeDtypeStruct((1, count * rows + PACK, most), bf16),
            jax.ShapeDtypeStruct((1, count, rows, most), f32),
            jax.ShapeDtypeStruct((1, 1, most), f32),
        ),
        in_specs=[SMEM] + [VMEM] * len(operands),
        out_specs=(VMEM,) * 4,
        scratch_shapes=[pltpu.VMEM((most, most), f32)],
        cost_estimate=pl.CostEstimate(flops=2 * depth * most * most, bytes_accessed=2**20, transcendentals=0),
        compiler_params=pltpu.CompilerParams(vmem_limit_bytes=6 * MIB),
        name="gram_split",
    )(ids, *operands)


def refine_body(slot, halves, per_group, ids, sectors_ref, kept_ref, stays_ref, taken_ref, gdiag_ref, corr_ref, out_ref):
    rows, most = out_ref.shape
    block, col = ids[0], ids[1]
    first = (block * halves + col % halves) * rows
    rank = kept_ref[sectors_ref[(col // halves) * per_group + slot]]
    gram = stays_ref[0, 0] + taken_ref[0, pl.ds(0, rows), :].astype(f32)
    gdiag = gdiag_ref[0] + unpacked(taken_ref[0, pl.ds(rows, PACK), :])
    cdiag = unpacked(corr_ref[0, pl.ds(rows, PACK), :])
    lam = gdiag / (cdiag + 1e-06)
    i = first + lax.broadcasted_iota(jnp.int32, (rows, most), 0)
    j = lax.broadcasted_iota(jnp.int32, (rows, most), 1)
    lam_j = jnp.broadcast_to(lam, (rows, most))
    lam_i = jnp.sum(jnp.where(i == j, lam_j, 0.0), axis=1, keepdims=True)
    differ = lam_j - lam_i
    total = damping * (lam_i + lam_j)
    divisor = differ * differ + total * total + 1e-06
    offdiag = (gram - lam_j * corr_ref[0, pl.ds(0, rows), :].astype(f32)) * differ / divisor
    result = jnp.where(i == j, 0.5 * (1.0 - cdiag), offdiag)
    inside = (i < rank) & (j < rank)
    out_ref[...] = jnp.where(inside, result, 0.0).astype(bf16)


def refine(slot, ids, slot_sector, kept, stays, taken, gdiag, corr, halves, per_group):
    _, _, rows, most = stays.shape
    return pl.pallas_call(
        functools.partial(refine_body, slot, halves, per_group),
        out_shape=jax.ShapeDtypeStruct((rows, most), bf16),
        in_specs=[SMEM] * 3 + [VMEM] * 4,
        out_specs=VMEM,
        cost_estimate=pl.CostEstimate(flops=10**6, bytes_accessed=2**19, transcendentals=0),
        compiler_params=pltpu.CompilerParams(vmem_limit_bytes=4 * MIB),
        name="refine",
    )(ids, slot_sector, kept, stays, taken, gdiag, corr)


def final_body(slot, per_group, halves, pieces, ids, sectors_ref, kept_ref, vectors_ref, left_ref, *refs):
    piece_refs = refs[:pieces]
    right_out, left_out, corr = refs[-3:]
    rows, most = piece_refs[0].shape
    rank = kept_ref[sectors_ref[ids[0] * per_group + slot]]

    def finish(narrow):
        out = narrow.astype(f32) + jnp.dot(narrow, corr[...], preferred_element_type=f32)
        j = lax.broadcasted_iota(jnp.int32, out.shape, 1)
        return jnp.where(j < rank, out, 0.0)

    @pl.when(pl.program_id(0) == 0)
    def _():
        half = ids[1] % halves
        for k in range(pieces - 1):
            at = ((ids[1] // halves) ^ k) * halves
            corr[pl.ds(pl.multiple_of((at + half) * rows, rows), rows), :] = piece_refs[k][...]
            other = piece_refs[-1][pl.ds(k * rows, rows), :]
            corr[pl.ds(pl.multiple_of((at + 1 - half) * rows, rows), rows), :] = other
        out = finish(left_ref[...])
        left_out[:, 0] = out.reshape(out.shape[0] // 4, 4, most)

    right_out[0] = finish(vectors_ref[0])


def final(slot, ids, slot_sector, kept, vectors, left, pieces, carried, halves):
    per_group, depth, most = vectors.shape
    tile = depth // 2
    rows = left.shape[0] // 4
    whole = lambda shape: pl.BlockSpec(shape, lambda t, *_: (0,) * len(shape))
    right_shape = jax.ShapeDtypeStruct((per_group, depth, most), f32)
    left_shape = jax.ShapeDtypeStruct((rows, per_group, 4, most), f32)
    in_specs = [
        pl.BlockSpec((1, tile, most), lambda t, *_: (slot, t, 0)),
        whole(left.shape),
    ] + [whole(piece.shape) for piece in pieces]
    operands = [vectors, left] + list(pieces)
    aliases = {}
    if carried is not None:
        aliases = {3 + len(operands): 0, 4 + len(operands): 1}
        in_specs += [pl.BlockSpec(memory_space=pl.ANY)] * 2
        operands += list(carried)
    return pl.pallas_call(
        functools.partial(final_body, slot, per_group, halves, len(pieces)),
        out_shape=(right_shape, left_shape),
        grid_spec=pltpu.PrefetchScalarGridSpec(
            num_scalar_prefetch=3,
            grid=(depth // tile,),
            in_specs=in_specs,
            out_specs=(
                pl.BlockSpec((1, tile, most), lambda t, *_: (slot, t, 0)),
                pl.BlockSpec((rows, 1, 4, most), lambda t, *_: (0, slot, 0, 0)),
            ),
            scratch_shapes=[pltpu.VMEM((most, most), bf16)],
        ),
        input_output_aliases=aliases,
        cost_estimate=pl.CostEstimate(flops=2 * 1216 * most * most, bytes_accessed=4 * 2**20, transcendentals=0),
        compiler_params=pltpu.CompilerParams(vmem_limit_bytes=12 * MIB),
        name="final",
    )(ids, slot_sector, kept, *operands)


def halve_body(shift, halves, first, ids, stays_in, taken_in, *refs):
    other, (sent_ref, stays_ref) = refs[:-2], refs[-2:]
    most = stays_ref.shape[3]
    want = (((ids[1] // halves) ^ ids[0]) >> shift) & 1
    for s in range(stays_ref.shape[0]):
        for n in range(stays_ref.shape[1]):
            if other:
                part = pl.ds(first, most)
                low = stays_in[0, 0, :, part] + taken_in[0, 0, :, part].astype(f32)
                high = other[0][0, 0] + other[1][0, 0].astype(f32)
                stays_ref[s, n] = jnp.where(want == 1, high, low)
                sent_ref[s, n] = jnp.where(want == 1, low, high).astype(bf16)
            else:
                at = 2 * n + want
                stays_ref[s, n] = stays_in[s, at] + taken_in[s, at].astype(f32)
                at = 2 * n + 1 - want
                sent_ref[s, n] = (stays_in[s, at] + taken_in[s, at].astype(f32)).astype(bf16)


def halve(ids, shift, halves, value, other=None, first=0):
    slots, count, rows, most = (other or value)[0].shape
    shape = (1, 1, rows, most) if other else (slots, count // 2, rows, most)
    operands = list(value) + list(other or ())
    return pl.pallas_call(
        functools.partial(halve_body, shift, halves, first),
        out_shape=(jax.ShapeDtypeStruct(shape, bf16), jax.ShapeDtypeStruct(shape, f32)),
        in_specs=[SMEM] + [VMEM] * len(operands),
        out_specs=(VMEM,) * 2,
        cost_estimate=pl.CostEstimate(flops=10**6, bytes_accessed=2**20, transcendentals=0),
        compiler_params=pltpu.CompilerParams(vmem_limit_bytes=8 * MIB),
    )(ids, *operands)


def work(theta, gate, warm_start, slot_sector, kept, block_offsets):
    groups, cols = lax.axis_size("row"), lax.axis_size("col")
    block, col = lax.axis_index("row"), lax.axis_index("col")
    halves = cols // groups
    per_group, _, bond_cols, most = warm_start.shape
    group_bits = groups.bit_length() - 1
    ids = jnp.stack([block, col]).astype(jnp.int32)
    vectors = warm_start.reshape(per_group, 4 * bond_cols, most)
    gate_matrix = gate.reshape(CHUNK, CHUNK)

    parts = [1] * (per_group - 1) + [2]

    across = {}
    remaining = vectors
    for s in range(per_group):
        width = most // parts[s]
        for p in range(parts[s]):
            own = remaining[s : s + 1, :, p * width : (p + 1) * width]
            own, remaining = lax.optimization_barrier((own, remaining))
            across[s, p] = {d: swap(own, "row", d) for d in range(2, groups, 2)}
    partner = swap(vectors, "row", 1)

    def place(b, g, h):
        return b * cols + g * halves + h

    def turned(value, k=0, hop=0):
        pairs = [
            (place(b ^ hop, g, h), place(g, b ^ k, h))
            for b in range(groups)
            for g in range(groups)
            for h in range(halves)
        ]
        return lax.ppermute(value, ("row", "col"), pairs)

    def turned_over(value):
        value = swap(value, "row", groups // 2)
        return turned(value, 0, groups // 2)

    corr = jnp.einsum("snk,snl->skl", vectors, vectors, preferred_element_type=f32)
    corr = corr.reshape(per_group, cols, most // cols, most)
    sent, stays, diag = corr_split(ids, corr, halves)
    taken = swap(sent, "col", 1)
    for t in range(group_bits):
        sent, stays, diag = step(ids, stays, taken, diag, ("group", t), halves)
        taken = swap(sent, "col", halves << t)
    sent, _, _ = step(ids, stays, taken, diag, None, halves)
    corr = []
    for s in range(per_group):
        if s == 0:
            corr.append(turned(sent[s : s + 1]))
        else:
            corr.append(turned_over(sent[s : s + 1]))

    def reduced(sent, stays):
        taken = swap(sent, "col", 1)
        for t in range(group_bits - 1):
            sent, stays = halve(ids, t, halves, (stays, taken))
            taken = swap(sent, "col", halves << t)
        return stays, taken

    gated = gate_rows(ids, slot_sector, block_offsets, theta, gate_matrix, groups, halves, per_group)
    near = []
    for s in range(per_group):
        operands = [vectors, partner]
        for d in range(2, groups // 2, 2):
            arrived = jnp.concatenate([across[s, p][d] for p in range(parts[s])], axis=2)
            operands += [arrived, swap(arrived, "row", 1)]
        value = product(s, 0, gated, operands)
        near.append(reduced(*value))
    last = group_bits - 1
    carried = None
    for s in range(per_group):
        values = []
        for p in range(parts[s]):
            far = []
            for d in range(groups // 2, groups, 2):
                far += [across[s, p][d], swap(across[s, p][d], "row", 1)]
            far = product(s, 1, gated, far)
            far = reduced(*far)
            sent, stays = halve(ids, last, halves, near[s], far, p * (most // parts[s]))
            values.append((stays, swap(sent, "col", halves << last)))
        projected, sent, stays, diag = gram_split(ids, values, groups)
        if s == per_group - 1:
            left = turned(projected)
        else:
            left = turned_over(projected)
        for t in range(1, group_bits + 1):
            taken = swap(sent, "row", 1 << (t - 1))
            which = ("row", t) if t < group_bits else ("half", 0)
            sent, stays, diag = step(ids, stays, taken, diag, which, halves)
        taken = swap(sent, "col", 1)
        piece = refine(s, ids, slot_sector, kept, stays, taken, diag, corr[s], halves, per_group)
        pieces = []
        for k in range(groups):
            pieces.append(turned(piece, k))
        pieces.append(swap(jnp.concatenate(pieces), "col", 1))
        carried = final(s, ids, slot_sector, kept, vectors, left, pieces, carried, halves)
    right, left = carried
    return left, right.reshape(warm_start.shape)


def solution(mesh):
    in_specs = (P("row", None, None, "col"), P(), P("row", None, "col", None), P(), P(), P())
    out_specs = (P("col", "row", None, None), P("row", None, "col", None))
    return jax.shard_map(work, mesh=mesh, in_specs=in_specs, out_specs=out_specs, check_vma=False)
```

```python
import functools

import jax
import jax.numpy as jnp
from jax import lax
from jax.experimental import pallas as pl
from jax.experimental.pallas import tpu as pltpu
from jax.sharding import PartitionSpec as P


NMAX = 96
CHUNK = 16
MIB = 2**20
damping = 0.25


VMEM = pl.BlockSpec(memory_space=pltpu.VMEM)
SMEM = pl.BlockSpec(memory_space=pltpu.SMEM)
f32, bf16 = jnp.float32, jnp.bfloat16


def swap(value, axis, mask):
    count = lax.axis_size(axis)
    return lax.ppermute(value, axis, [(i, i ^ mask) for i in range(count)])


def window(ids, sectors_ref, offsets_ref, block_rows, far, slot, half, rows, per_group):
    block = ids[0]
    sector = sectors_ref[(far ^ block) * per_group + slot]
    number = offsets_ref.shape[1]
    start = offsets_ref[block, sector]
    following = offsets_ref[block, jnp.minimum(sector + 1, number - 1)]
    end = jnp.where(sector + 1 < number, following, block_rows)
    start = start + half * rows
    return start, jnp.clip(end - start, 0, rows)


def prepare(theta_hbm, gate_ref, theta, mixer, sem):
    block_rows = theta_hbm.shape[0]
    size = CHUNK * CHUNK
    copy = pltpu.make_async_copy(theta_hbm, theta.at[pl.ds(0, block_rows)], sem)
    copy.start()
    theta[pl.ds(block_rows, NMAX)] = jnp.zeros((NMAX,) + theta.shape[1:], theta.dtype)
    tall_row = lax.broadcasted_iota(jnp.int32, (size, CHUNK), 0)
    tall_col = lax.broadcasted_iota(jnp.int32, (size, CHUNK), 1)
    wide_row = lax.broadcasted_iota(jnp.int32, (CHUNK, size), 0)
    wide_col = lax.broadcasted_iota(jnp.int32, (CHUNK, size), 1)
    spread = ((tall_row % 4) * 4 + tall_row // (4 * CHUNK) == tall_col).astype(bf16)
    repeat = (wide_col % CHUNK == wide_row).astype(bf16)
    tall = jnp.dot(spread, gate_ref[...], preferred_element_type=f32).astype(bf16)
    full = jnp.dot(tall, repeat, preferred_element_type=f32)
    row = lax.broadcasted_iota(jnp.int32, (size, size), 0)
    col = lax.broadcasted_iota(jnp.int32, (size, size), 1)
    mixer[...] = jnp.where((row // 4) % CHUNK == col // CHUNK, full, 0.0).astype(bf16)
    copy.wait()


def gated_window(theta, mixer, start, live, rows, store):
    size = CHUNK * CHUNK
    cols = theta.shape[3]
    for part in range(rows // CHUNK):
        first = jnp.clip(start + part * CHUNK, 0, theta.shape[0] - CHUNK)
        piece = theta[pl.ds(first, CHUNK)].reshape(size, cols)
        mixed = jnp.dot(mixer[...], piece, preferred_element_type=f32)
        place = part * CHUNK + lax.broadcasted_iota(jnp.int32, (4 * CHUNK, cols), 0) // 4
        for b in range(4):
            value = mixed[b * 4 * CHUNK : (b + 1) * 4 * CHUNK, :]
            value = jnp.where(place < live, value, 0.0).astype(bf16)
            store(pl.ds(part * 4 * CHUNK, 4 * CHUNK), pl.ds(b * cols, cols), value)


def theta_scratch(theta):
    return [
        pltpu.VMEM((theta.shape[0] + NMAX,) + theta.shape[1:], bf16),
        pltpu.VMEM((CHUNK * CHUNK, CHUNK * CHUNK), bf16),
        pltpu.SemaphoreType.DMA,
    ]


def gate_body(halves, per_group, ids, sectors_ref, offsets_ref, theta_hbm, gate_ref, out_ref, theta, mixer, sem):
    slot, n = pl.program_id(0), pl.program_id(1)
    rows = NMAX // halves

    @pl.when((slot == 0) & (n == 0))
    def _():
        prepare(theta_hbm, gate_ref, theta, mixer, sem)

    for far_half in (0, 1):
        half = (ids[1] % halves) ^ (1 - far_half)
        start, live = window(
            ids, sectors_ref, offsets_ref, theta_hbm.shape[0], n, slot, half, rows, per_group
        )

        def store(at, cols, value, base=far_half * 4 * rows):
            out_ref[0, 0, pl.ds(base + at.start, at.size), cols] = value

        gated_window(theta, mixer, start, live, rows, store)


def gate_rows(ids, slot_sector, block_offsets, theta, gate, count, halves, per_group):
    rows, cols = NMAX // halves, theta.shape[3]
    block = (1, 1, halves * 4 * rows, 4 * cols)
    return pl.pallas_call(
        functools.partial(gate_body, halves, per_group),
        out_shape=jax.ShapeDtypeStruct((per_group, count) + block[2:], bf16),
        grid_spec=pltpu.PrefetchScalarGridSpec(
            num_scalar_prefetch=3,
            grid=(per_group, count),
            in_specs=[
                pl.BlockSpec(memory_space=pl.ANY),
                pl.BlockSpec((CHUNK, CHUNK), lambda s, n, *_: (0, 0)),
            ],
            out_specs=pl.BlockSpec(block, lambda s, n, *_: (s, n, 0, 0)),
            scratch_shapes=theta_scratch(theta),
        ),
        cost_estimate=pl.CostEstimate(flops=6 * 10**9, bytes_accessed=12 * 2**20, transcendentals=0),
        compiler_params=pltpu.CompilerParams(vmem_limit_bytes=14 * MIB),
        name="gate_rows",
    )(ids, slot_sector, block_offsets, theta, gate)


def product_body(count, lhs_ref, *refs):
    vector_refs = refs[:count]
    sent_ref, kept_ref = refs[count:]
    rows = sent_ref.shape[2]
    for n in range(count):
        out = jnp.dot(lhs_ref[0, n], vector_refs[n][0], preferred_element_type=f32)
        sent_ref[0, n] = out[:rows].astype(bf16)
        kept_ref[0, n] = out[rows:]


def product(slot, chunk, gated, vectors):
    _, _, rows, depth = gated.shape
    count = len(vectors)
    most = vectors[0].shape[2]
    out_block = (1, count, rows // 2, most)
    return pl.pallas_call(
        functools.partial(product_body, count),
        out_shape=(jax.ShapeDtypeStruct(out_block, bf16), jax.ShapeDtypeStruct(out_block, f32)),
        grid=(1,),
        in_specs=[pl.BlockSpec((1, count, rows, depth), lambda i: (slot, chunk, 0, 0))]
        + [pl.BlockSpec((1, depth, most), lambda i, at=min(slot, v.shape[0] - 1): (at, 0, 0)) for v in vectors],
        out_specs=(pl.BlockSpec(out_block, lambda i: (0, 0, 0, 0)),) * 2,
        cost_estimate=pl.CostEstimate(flops=8 * 10**8, bytes_accessed=5 * 2**20, transcendentals=0),
        compiler_params=pltpu.CompilerParams(vmem_limit_bytes=16 * MIB),
    )(gated, *vectors)


PACK = 16


def packed(diag):
    high = diag.astype(bf16)
    rest = diag - high.astype(f32)
    middle = rest.astype(bf16)
    low = (rest - middle.astype(f32)).astype(bf16)
    row = lax.broadcasted_iota(jnp.int32, (PACK, diag.shape[1]), 0)
    wide = [jnp.broadcast_to(x.astype(f32), row.shape) for x in (high, middle, low)]
    return jnp.where(row == 0, wide[0], jnp.where(row == 1, wide[1], jnp.where(row == 2, wide[2], 0.0))).astype(bf16)


def unpacked(block):
    return jnp.sum(block.astype(f32), axis=0, keepdims=True)


def bit_of(ids, which, halves):
    source, shift = which
    value = {"row": ids[0], "group": ids[1] // halves, "half": ids[1] % halves}[source]
    return (value >> shift) & 1


def corr_body(halves, ids, corr_ref, sent_ref, stays_ref, diag_ref):
    slots, count, rows, most = stays_ref.shape
    mine = bit_of(ids, ("group", 0), halves)
    for s in range(slots):
        diag = jnp.zeros((1, most), f32)
        for n in range(2 * count):
            i = n * rows + lax.broadcasted_iota(jnp.int32, (rows, most), 0)
            j = lax.broadcasted_iota(jnp.int32, (rows, most), 1)
            diag = diag + jnp.sum(jnp.where(i == j, corr_ref[s, n], 0.0), axis=0, keepdims=True)
        diag_ref[s] = diag
        for n in range(count):
            stays_ref[s, n] = corr_ref[s, 2 * n + mine]
            sent_ref[s, pl.ds(n * rows, rows), :] = corr_ref[s, 2 * n + 1 - mine].astype(bf16)
        sent_ref[s, pl.ds(count * rows, PACK), :] = packed(diag)


def corr_split(ids, corr, halves):
    slots, count, rows, most = corr.shape
    count = count // 2
    return pl.pallas_call(
        functools.partial(corr_body, halves),
        out_shape=(
            jax.ShapeDtypeStruct((slots, count * rows + PACK, most), bf16),
            jax.ShapeDtypeStruct((slots, count, rows, most), f32),
            jax.ShapeDtypeStruct((slots, 1, most), f32),
        ),
        in_specs=[SMEM, VMEM],
        out_specs=(VMEM,) * 3,
        cost_estimate=pl.CostEstimate(flops=10**6, bytes_accessed=2**21, transcendentals=0),
        compiler_params=pltpu.CompilerParams(vmem_limit_bytes=8 * MIB),
        name="corr_split",
    )(ids, corr)


def step_body(which, halves, ids, stays_in, taken_ref, diag_in, sent_ref, stays_ref, diag_ref):
    slots, count, rows, _ = stays_ref.shape
    before, block = stays_in.shape[1:3]
    mine = bit_of(ids, which, halves) if which else 0
    for s in range(slots):
        diag = diag_in[s] + unpacked(taken_ref[s, pl.ds(before * block, PACK), :])
        diag_ref[s] = diag

        def total(at, first=0):
            there = pl.multiple_of(at * block + first, rows)
            return stays_in[s, at, pl.ds(first, rows), :] + taken_ref[s, pl.ds(there, rows), :].astype(f32)

        for n in range(count):
            if not which:
                value = total(n)
                stays_ref[s, n] = value
            elif block != rows:
                stays_ref[s, n] = total(n, pl.multiple_of(mine * rows, rows))
                value = total(n, pl.multiple_of((1 - mine) * rows, rows))
            else:
                stays_ref[s, n] = total(2 * n + mine)
                value = total(2 * n + 1 - mine)
            sent_ref[s, pl.ds(n * rows, rows), :] = value.astype(bf16)
        sent_ref[s, pl.ds(count * rows, PACK), :] = packed(diag)


def step(ids, stays, taken, diag, which, halves):
    slots, count, rows, most = stays.shape
    if which and which[0] == "half":
        rows = rows // halves
    elif which:
        count = count // 2
    return pl.pallas_call(
        functools.partial(step_body, which, halves),
        out_shape=(
            jax.ShapeDtypeStruct((slots, count * rows + PACK, most), bf16),
            jax.ShapeDtypeStruct((slots, count, rows, most), f32),
            jax.ShapeDtypeStruct((slots, 1, most), f32),
        ),
        in_specs=[SMEM] + [VMEM] * 3,
        out_specs=(VMEM,) * 3,
        cost_estimate=pl.CostEstimate(flops=10**6, bytes_accessed=2**19, transcendentals=0),
        compiler_params=pltpu.CompilerParams(vmem_limit_bytes=8 * MIB),
    )(ids, stays, taken, diag)


def gram_body(parts, ids, *refs):
    projected_ref, sent_ref, stays_ref, diag_ref, gram = refs[2 * parts :]
    _, count, rows, most = stays_ref.shape
    width = most // parts
    for n in range(parts):
        part = (refs[2 * n][0, 0] + refs[2 * n + 1][0, 0].astype(f32)).astype(bf16)
        projected_ref[:, n * width : (n + 1) * width] = part
    projected = projected_ref[...]
    gram[...] = lax.dot_general(projected, projected, (((0,), (0,)), ((), ())), preferred_element_type=f32)
    wide = projected.astype(f32)
    diag = jnp.sum(wide * wide, axis=0, keepdims=True)
    diag_ref[0] = diag
    mine = ids[0] & 1
    for n in range(count):
        stays_ref[0, n] = gram[pl.ds(pl.multiple_of((2 * n + mine) * rows, rows), rows), :]
        other = gram[pl.ds(pl.multiple_of((2 * n + 1 - mine) * rows, rows), rows), :]
        sent_ref[0, pl.ds(n * rows, rows), :] = other.astype(bf16)
    sent_ref[0, pl.ds(count * rows, PACK), :] = packed(diag)


def gram_split(ids, values, groups):
    depth, most = values[0][0].shape[2:]
    most = most * len(values)
    rows, count = most // groups, groups // 2
    operands = [x for value in values for x in value]
    return pl.pallas_call(
        functools.partial(gram_body, len(values)),
        out_shape=(
            jax.ShapeDtypeStruct((depth, most), bf16),
            jax.ShapeDtypeStruct((1, count * rows + PACK, most), bf16),
            jax.ShapeDtypeStruct((1, count, rows, most), f32),
            jax.ShapeDtypeStruct((1, 1, most), f32),
        ),
        in_specs=[SMEM] + [VMEM] * len(operands),
        out_specs=(VMEM,) * 4,
        scratch_shapes=[pltpu.VMEM((most, most), f32)],
        cost_estimate=pl.CostEstimate(flops=2 * depth * most * most, bytes_accessed=2**20, transcendentals=0),
        compiler_params=pltpu.CompilerParams(vmem_limit_bytes=6 * MIB),
        name="gram_split",
    )(ids, *operands)


def refine_body(slot, halves, per_group, ids, sectors_ref, kept_ref, stays_ref, taken_ref, gdiag_ref, corr_ref, out_ref):
    rows, most = out_ref.shape
    block, col = ids[0], ids[1]
    first = (block * halves + col % halves) * rows
    rank = kept_ref[sectors_ref[(col // halves) * per_group + slot]]
    gram = stays_ref[0, 0] + taken_ref[0, pl.ds(0, rows), :].astype(f32)
    gdiag = gdiag_ref[0] + unpacked(taken_ref[0, pl.ds(rows, PACK), :])
    cdiag = unpacked(corr_ref[0, pl.ds(rows, PACK), :])
    lam = gdiag / (cdiag + 1e-06)
    i = first + lax.broadcasted_iota(jnp.int32, (rows, most), 0)
    j = lax.broadcasted_iota(jnp.int32, (rows, most), 1)
    lam_j = jnp.broadcast_to(lam, (rows, most))
    lam_i = jnp.sum(jnp.where(i == j, lam_j, 0.0), axis=1, keepdims=True)
    differ = lam_j - lam_i
    total = damping * (lam_i + lam_j)
    divisor = differ * differ + total * total + 1e-06
    offdiag = (gram - lam_j * corr_ref[0, pl.ds(0, rows), :].astype(f32)) * differ / divisor
    result = jnp.where(i == j, 0.5 * (1.0 - cdiag), offdiag)
    inside = (i < rank) & (j < rank)
    out_ref[...] = jnp.where(inside, result, 0.0).astype(bf16)


def refine(slot, ids, slot_sector, kept, stays, taken, gdiag, corr, halves, per_group):
    _, _, rows, most = stays.shape
    return pl.pallas_call(
        functools.partial(refine_body, slot, halves, per_group),
        out_shape=jax.ShapeDtypeStruct((rows, most), bf16),
        in_specs=[SMEM] * 3 + [VMEM] * 4,
        out_specs=VMEM,
        cost_estimate=pl.CostEstimate(flops=10**6, bytes_accessed=2**19, transcendentals=0),
        compiler_params=pltpu.CompilerParams(vmem_limit_bytes=4 * MIB),
        name="refine",
    )(ids, slot_sector, kept, stays, taken, gdiag, corr)


def final_body(slot, per_group, halves, pieces, ids, sectors_ref, kept_ref, vectors_ref, left_ref, *refs):
    piece_refs = refs[:pieces]
    right_out, left_out, corr = refs[-3:]
    rows, most = piece_refs[0].shape
    rank = kept_ref[sectors_ref[ids[0] * per_group + slot]]

    def finish(narrow):
        out = narrow.astype(f32) + jnp.dot(narrow, corr[...], preferred_element_type=f32)
        j = lax.broadcasted_iota(jnp.int32, out.shape, 1)
        return jnp.where(j < rank, out, 0.0)

    @pl.when(pl.program_id(0) == 0)
    def _():
        half = ids[1] % halves
        for k in range(pieces - 1):
            at = ((ids[1] // halves) ^ k) * halves
            corr[pl.ds(pl.multiple_of((at + half) * rows, rows), rows), :] = piece_refs[k][...]
            other = piece_refs[-1][pl.ds(k * rows, rows), :]
            corr[pl.ds(pl.multiple_of((at + 1 - half) * rows, rows), rows), :] = other
        out = finish(left_ref[...])
        left_out[:, 0] = out.reshape(out.shape[0] // 4, 4, most)

    right_out[0] = finish(vectors_ref[0])


def final(slot, ids, slot_sector, kept, vectors, left, pieces, carried, halves):
    per_group, depth, most = vectors.shape
    tile = depth // 2
    rows = left.shape[0] // 4
    whole = lambda shape: pl.BlockSpec(shape, lambda t, *_: (0,) * len(shape))
    right_shape = jax.ShapeDtypeStruct((per_group, depth, most), f32)
    left_shape = jax.ShapeDtypeStruct((rows, per_group, 4, most), f32)
    in_specs = [
        pl.BlockSpec((1, tile, most), lambda t, *_: (slot, t, 0)),
        whole(left.shape),
    ] + [whole(piece.shape) for piece in pieces]
    operands = [vectors, left] + list(pieces)
    aliases = {}
    if carried is not None:
        aliases = {3 + len(operands): 0, 4 + len(operands): 1}
        in_specs += [pl.BlockSpec(memory_space=pl.ANY)] * 2
        operands += list(carried)
    return pl.pallas_call(
        functools.partial(final_body, slot, per_group, halves, len(pieces)),
        out_shape=(right_shape, left_shape),
        grid_spec=pltpu.PrefetchScalarGridSpec(
            num_scalar_prefetch=3,
            grid=(depth // tile,),
            in_specs=in_specs,
            out_specs=(
                pl.BlockSpec((1, tile, most), lambda t, *_: (slot, t, 0)),
                pl.BlockSpec((rows, 1, 4, most), lambda t, *_: (0, slot, 0, 0)),
            ),
            scratch_shapes=[pltpu.VMEM((most, most), bf16)],
        ),
        input_output_aliases=aliases,
        cost_estimate=pl.CostEstimate(flops=2 * 1216 * most * most, bytes_accessed=4 * 2**20, transcendentals=0),
        compiler_params=pltpu.CompilerParams(vmem_limit_bytes=12 * MIB),
        name="final",
    )(ids, slot_sector, kept, *operands)


def halve_body(shift, halves, first, ids, stays_in, taken_in, *refs):
    other, (sent_ref, stays_ref) = refs[:-2], refs[-2:]
    most = stays_ref.shape[3]
    want = (((ids[1] // halves) ^ ids[0]) >> shift) & 1
    for s in range(stays_ref.shape[0]):
        for n in range(stays_ref.shape[1]):
            if other:
                part = pl.ds(first, most)
                low = stays_in[0, 0, :, part] + taken_in[0, 0, :, part].astype(f32)
                high = other[0][0, 0] + other[1][0, 0].astype(f32)
                stays_ref[s, n] = jnp.where(want == 1, high, low)
                sent_ref[s, n] = jnp.where(want == 1, low, high).astype(bf16)
            else:
                at = 2 * n + want
                stays_ref[s, n] = stays_in[s, at] + taken_in[s, at].astype(f32)
                at = 2 * n + 1 - want
                sent_ref[s, n] = (stays_in[s, at] + taken_in[s, at].astype(f32)).astype(bf16)


def halve(ids, shift, halves, value, other=None, first=0):
    slots, count, rows, most = (other or value)[0].shape
    shape = (1, 1, rows, most) if other else (slots, count // 2, rows, most)
    operands = list(value) + list(other or ())
    return pl.pallas_call(
        functools.partial(halve_body, shift, halves, first),
        out_shape=(jax.ShapeDtypeStruct(shape, bf16), jax.ShapeDtypeStruct(shape, f32)),
        in_specs=[SMEM] + [VMEM] * len(operands),
        out_specs=(VMEM,) * 2,
        cost_estimate=pl.CostEstimate(flops=10**6, bytes_accessed=2**20, transcendentals=0),
        compiler_params=pltpu.CompilerParams(vmem_limit_bytes=8 * MIB),
    )(ids, *operands)


def work(theta, gate, warm_start, slot_sector, kept, block_offsets):
    groups, cols = lax.axis_size("row"), lax.axis_size("col")
    block, col = lax.axis_index("row"), lax.axis_index("col")
    halves = cols // groups
    per_group, _, bond_cols, most = warm_start.shape
    group_bits = groups.bit_length() - 1
    ids = jnp.stack([block, col]).astype(jnp.int32)
    vectors = warm_start.reshape(per_group, 4 * bond_cols, most)
    gate_matrix = gate.reshape(CHUNK, CHUNK)

    parts = [1] * (per_group - 1) + [2]

    across = {}
    remaining = vectors
    for s in range(per_group):
        width = most // parts[s]
        for p in range(parts[s]):
            own = remaining[s : s + 1, :, p * width : (p + 1) * width]
            own, remaining = lax.optimization_barrier((own, remaining))
            across[s, p] = {d: swap(own, "row", d) for d in range(2, groups, 2)}
    partner = swap(vectors, "row", 1)

    def place(b, g, h):
        return b * cols + g * halves + h

    def turned(value, k=0, hop=0):
        pairs = [
            (place(b ^ hop, g, h), place(g, b ^ k, h))
            for b in range(groups)
            for g in range(groups)
            for h in range(halves)
        ]
        return lax.ppermute(value, ("row", "col"), pairs)

    def turned_over(value):
        value = swap(value, "row", groups // 2)
        return turned(value, 0, groups // 2)

    corr = jnp.einsum("snk,snl->skl", vectors, vectors, preferred_element_type=f32)
    corr = corr.reshape(per_group, groups, most // groups, most)
    sent, stays, diag = corr_split(ids, corr, halves)
    for t in range(group_bits):
        taken = swap(sent, "col", halves << t)
        which = ("group", t + 1) if t + 1 < group_bits else ("half", 0)
        sent, stays, diag = step(ids, stays, taken, diag, which, halves)
    taken = swap(sent, "col", 1)
    sent, _, _ = step(ids, stays, taken, diag, None, halves)
    corr = []
    for s in range(per_group):
        if s == 0:
            corr.append(turned(sent[s : s + 1]))
        else:
            corr.append(turned_over(sent[s : s + 1]))

    def reduced(sent, stays):
        taken = swap(sent, "col", 1)
        for t in range(group_bits - 1):
            sent, stays = halve(ids, t, halves, (stays, taken))
            taken = swap(sent, "col", halves << t)
        return stays, taken

    gated = gate_rows(ids, slot_sector, block_offsets, theta, gate_matrix, groups, halves, per_group)
    near = []
    for s in range(per_group):
        operands = [vectors, partner]
        for d in range(2, groups // 2, 2):
            arrived = jnp.concatenate([across[s, p][d] for p in range(parts[s])], axis=2)
            operands += [arrived, swap(arrived, "row", 1)]
        value = product(s, 0, gated, operands)
        near.append(reduced(*value))
    last = group_bits - 1
    carried = None
    for s in range(per_group):
        values = []
        for p in range(parts[s]):
            far = []
            for d in range(groups // 2, groups, 2):
                far += [across[s, p][d], swap(across[s, p][d], "row", 1)]
            far = product(s, 1, gated, far)
            far = reduced(*far)
            sent, stays = halve(ids, last, halves, near[s], far, p * (most // parts[s]))
            values.append((stays, swap(sent, "col", halves << last)))
        projected, sent, stays, diag = gram_split(ids, values, groups)
        if s == per_group - 1:
            left = turned(projected)
        else:
            left = turned_over(projected)
        for t in range(1, group_bits + 1):
            taken = swap(sent, "row", 1 << (t - 1))
            which = ("row", t) if t < group_bits else ("half", 0)
            sent, stays, diag = step(ids, stays, taken, diag, which, halves)
        taken = swap(sent, "col", 1)
        piece = refine(s, ids, slot_sector, kept, stays, taken, diag, corr[s], halves, per_group)
        pieces = []
        for k in range(groups):
            pieces.append(turned(piece, k))
        pieces.append(swap(jnp.concatenate(pieces), "col", 1))
        carried = final(s, ids, slot_sector, kept, vectors, left, pieces, carried, halves)
    right, left = carried
    return left, right.reshape(warm_start.shape)


def solution(mesh):
    in_specs = (P("row", None, None, "col"), P(), P("row", None, "col", None), P(), P(), P())
    out_specs = (P("col", "row", None, None), P("row", None, "col", None))
    return jax.shard_map(work, mesh=mesh, in_specs=in_specs, out_specs=out_specs, check_vma=False)
```

```python
import functools

import jax
import jax.numpy as jnp
from jax import lax
from jax.experimental import pallas as pl
from jax.experimental.pallas import tpu as pltpu
from jax.sharding import PartitionSpec as P


NMAX = 96
CHUNK = 16
MIB = 2**20
damping = 0.25


VMEM = pl.BlockSpec(memory_space=pltpu.VMEM)
SMEM = pl.BlockSpec(memory_space=pltpu.SMEM)
f32, bf16 = jnp.float32, jnp.bfloat16


def swap(value, axis, mask):
    count = lax.axis_size(axis)
    return lax.ppermute(value, axis, [(i, i ^ mask) for i in range(count)])


def window(ids, sectors_ref, offsets_ref, block_rows, far, slot, half, rows, per_group):
    block = ids[0]
    sector = sectors_ref[(far ^ block) * per_group + slot]
    number = offsets_ref.shape[1]
    start = offsets_ref[block, sector]
    following = offsets_ref[block, jnp.minimum(sector + 1, number - 1)]
    end = jnp.where(sector + 1 < number, following, block_rows)
    start = start + half * rows
    return start, jnp.clip(end - start, 0, rows)


def prepare(theta_hbm, gate_ref, theta, mixer, sem):
    block_rows = theta_hbm.shape[0]
    size = CHUNK * CHUNK
    copy = pltpu.make_async_copy(theta_hbm, theta.at[pl.ds(0, block_rows)], sem)
    copy.start()
    theta[pl.ds(block_rows, NMAX)] = jnp.zeros((NMAX,) + theta.shape[1:], theta.dtype)
    tall_row = lax.broadcasted_iota(jnp.int32, (size, CHUNK), 0)
    tall_col = lax.broadcasted_iota(jnp.int32, (size, CHUNK), 1)
    wide_row = lax.broadcasted_iota(jnp.int32, (CHUNK, size), 0)
    wide_col = lax.broadcasted_iota(jnp.int32, (CHUNK, size), 1)
    spread = ((tall_row % 4) * 4 + tall_row // (4 * CHUNK) == tall_col).astype(bf16)
    repeat = (wide_col % CHUNK == wide_row).astype(bf16)
    tall = jnp.dot(spread, gate_ref[...], preferred_element_type=f32).astype(bf16)
    full = jnp.dot(tall, repeat, preferred_element_type=f32)
    row = lax.broadcasted_iota(jnp.int32, (size, size), 0)
    col = lax.broadcasted_iota(jnp.int32, (size, size), 1)
    mixer[...] = jnp.where((row // 4) % CHUNK == col // CHUNK, full, 0.0).astype(bf16)
    copy.wait()


def gated_window(theta, mixer, start, live, rows, store):
    size = CHUNK * CHUNK
    cols = theta.shape[3]
    for part in range(rows // CHUNK):
        first = jnp.clip(start + part * CHUNK, 0, theta.shape[0] - CHUNK)
        piece = theta[pl.ds(first, CHUNK)].reshape(size, cols)
        mixed = jnp.dot(mixer[...], piece, preferred_element_type=f32)
        place = part * CHUNK + lax.broadcasted_iota(jnp.int32, (4 * CHUNK, cols), 0) // 4
        for b in range(4):
            value = mixed[b * 4 * CHUNK : (b + 1) * 4 * CHUNK, :]
            value = jnp.where(place < live, value, 0.0).astype(bf16)
            store(pl.ds(part * 4 * CHUNK, 4 * CHUNK), pl.ds(b * cols, cols), value)


def theta_scratch(theta):
    return [
        pltpu.VMEM((theta.shape[0] + NMAX,) + theta.shape[1:], bf16),
        pltpu.VMEM((CHUNK * CHUNK, CHUNK * CHUNK), bf16),
        pltpu.SemaphoreType.DMA,
    ]


def gate_body(halves, per_group, ids, sectors_ref, offsets_ref, theta_hbm, gate_ref, out_ref, theta, mixer, sem):
    slot, n = pl.program_id(0), pl.program_id(1)
    rows = NMAX // halves

    @pl.when((slot == 0) & (n == 0))
    def _():
        prepare(theta_hbm, gate_ref, theta, mixer, sem)

    for far_half in (0, 1):
        half = (ids[1] % halves) ^ (1 - far_half)
        start, live = window(
            ids, sectors_ref, offsets_ref, theta_hbm.shape[0], n, slot, half, rows, per_group
        )

        def store(at, cols, value, base=far_half * 4 * rows):
            out_ref[0, 0, pl.ds(base + at.start, at.size), cols] = value

        gated_window(theta, mixer, start, live, rows, store)


def gate_rows(ids, slot_sector, block_offsets, theta, gate, count, halves, per_group):
    rows, cols = NMAX // halves, theta.shape[3]
    block = (1, 1, halves * 4 * rows, 4 * cols)
    return pl.pallas_call(
        functools.partial(gate_body, halves, per_group),
        out_shape=jax.ShapeDtypeStruct((per_group, count) + block[2:], bf16),
        grid_spec=pltpu.PrefetchScalarGridSpec(
            num_scalar_prefetch=3,
            grid=(per_group, count),
            in_specs=[
                pl.BlockSpec(memory_space=pltpu.HBM),
                pl.BlockSpec((CHUNK, CHUNK), lambda s, n, *_: (0, 0)),
            ],
            out_specs=pl.BlockSpec(block, lambda s, n, *_: (s, n, 0, 0)),
            scratch_shapes=theta_scratch(theta),
        ),
        cost_estimate=pl.CostEstimate(flops=6 * 10**9, bytes_accessed=12 * 2**20, transcendentals=0),
        compiler_params=pltpu.CompilerParams(vmem_limit_bytes=14 * MIB),
        name="gate_rows",
    )(ids, slot_sector, block_offsets, theta, gate)


def product_body(count, lhs_ref, *refs):
    vector_refs = refs[:count]
    sent_ref, kept_ref = refs[count:]
    rows = sent_ref.shape[2]
    for n in range(count):
        out = jnp.dot(lhs_ref[0, n], vector_refs[n][0], preferred_element_type=f32)
        sent_ref[0, n] = out[:rows].astype(bf16)
        kept_ref[0, n] = out[rows:]


def product(slot, chunk, gated, vectors):
    _, _, rows, depth = gated.shape
    count = len(vectors)
    most = vectors[0].shape[2]
    out_block = (1, count, rows // 2, most)
    return pl.pallas_call(
        functools.partial(product_body, count),
        out_shape=(jax.ShapeDtypeStruct(out_block, bf16), jax.ShapeDtypeStruct(out_block, f32)),
        grid=(1,),
        in_specs=[pl.BlockSpec((1, count, rows, depth), lambda i: (slot, chunk, 0, 0))]
        + [pl.BlockSpec((1, depth, most), lambda i, at=min(slot, v.shape[0] - 1): (at, 0, 0)) for v in vectors],
        out_specs=(pl.BlockSpec(out_block, lambda i: (0, 0, 0, 0)),) * 2,
        cost_estimate=pl.CostEstimate(flops=8 * 10**8, bytes_accessed=5 * 2**20, transcendentals=0),
        compiler_params=pltpu.CompilerParams(vmem_limit_bytes=16 * MIB),
    )(gated, *vectors)


PACK = 16


def packed(diag):
    high = diag.astype(bf16)
    rest = diag - high.astype(f32)
    middle = rest.astype(bf16)
    low = (rest - middle.astype(f32)).astype(bf16)
    row = lax.broadcasted_iota(jnp.int32, (PACK, diag.shape[1]), 0)
    wide = [jnp.broadcast_to(x.astype(f32), row.shape) for x in (high, middle, low)]
    return jnp.where(row == 0, wide[0], jnp.where(row == 1, wide[1], jnp.where(row == 2, wide[2], 0.0))).astype(bf16)


def unpacked(block):
    return jnp.sum(block.astype(f32), axis=0, keepdims=True)


def bit_of(ids, which, halves):
    source, shift = which
    value = {"row": ids[0], "group": ids[1] // halves, "half": ids[1] % halves}[source]
    return (value >> shift) & 1


def corr_body(halves, ids, corr_ref, sent_ref, stays_ref, diag_ref):
    slots, count, rows, most = stays_ref.shape
    mine = bit_of(ids, ("group", 0), halves)
    for s in range(slots):
        diag = jnp.zeros((1, most), f32)
        for n in range(2 * count):
            i = n * rows + lax.broadcasted_iota(jnp.int32, (rows, most), 0)
            j = lax.broadcasted_iota(jnp.int32, (rows, most), 1)
            diag = diag + jnp.sum(jnp.where(i == j, corr_ref[s, n], 0.0), axis=0, keepdims=True)
        diag_ref[s] = diag
        for n in range(count):
            stays_ref[s, n] = corr_ref[s, 2 * n + mine]
            sent_ref[s, pl.ds(n * rows, rows), :] = corr_ref[s, 2 * n + 1 - mine].astype(bf16)
        sent_ref[s, pl.ds(count * rows, PACK), :] = packed(diag)


def corr_split(ids, corr, halves):
    slots, count, rows, most = corr.shape
    count = count // 2
    return pl.pallas_call(
        functools.partial(corr_body, halves),
        out_shape=(
            jax.ShapeDtypeStruct((slots, count * rows + PACK, most), bf16),
            jax.ShapeDtypeStruct((slots, count, rows, most), f32),
            jax.ShapeDtypeStruct((slots, 1, most), f32),
        ),
        in_specs=[SMEM, VMEM],
        out_specs=(VMEM,) * 3,
        cost_estimate=pl.CostEstimate(flops=10**6, bytes_accessed=2**21, transcendentals=0),
        compiler_params=pltpu.CompilerParams(vmem_limit_bytes=8 * MIB),
        name="corr_split",
    )(ids, corr)


def step_body(which, halves, ids, stays_in, taken_ref, diag_in, sent_ref, stays_ref, diag_ref):
    slots, count, rows, _ = stays_ref.shape
    before, block = stays_in.shape[1:3]
    mine = bit_of(ids, which, halves) if which else 0
    for s in range(slots):
        diag = diag_in[s] + unpacked(taken_ref[s, pl.ds(before * block, PACK), :])
        diag_ref[s] = diag

        def total(at, first=0):
            there = pl.multiple_of(at * block + first, rows)
            return stays_in[s, at, pl.ds(first, rows), :] + taken_ref[s, pl.ds(there, rows), :].astype(f32)

        for n in range(count):
            if not which:
                value = total(n)
                stays_ref[s, n] = value
            elif block != rows:
                stays_ref[s, n] = total(n, pl.multiple_of(mine * rows, rows))
                value = total(n, pl.multiple_of((1 - mine) * rows, rows))
            else:
                stays_ref[s, n] = total(2 * n + mine)
                value = total(2 * n + 1 - mine)
            sent_ref[s, pl.ds(n * rows, rows), :] = value.astype(bf16)
        sent_ref[s, pl.ds(count * rows, PACK), :] = packed(diag)


def step(ids, stays, taken, diag, which, halves):
    slots, count, rows, most = stays.shape
    if which and which[0] == "half":
        rows = rows // halves
    elif which:
        count = count // 2
    return pl.pallas_call(
        functools.partial(step_body, which, halves),
        out_shape=(
            jax.ShapeDtypeStruct((slots, count * rows + PACK, most), bf16),
            jax.ShapeDtypeStruct((slots, count, rows, most), f32),
            jax.ShapeDtypeStruct((slots, 1, most), f32),
        ),
        in_specs=[SMEM] + [VMEM] * 3,
        out_specs=(VMEM,) * 3,
        cost_estimate=pl.CostEstimate(flops=10**6, bytes_accessed=2**19, transcendentals=0),
        compiler_params=pltpu.CompilerParams(vmem_limit_bytes=8 * MIB),
    )(ids, stays, taken, diag)


def gram_body(parts, ids, *refs):
    projected_ref, sent_ref, stays_ref, diag_ref, gram = refs[2 * parts :]
    _, count, rows, most = stays_ref.shape
    width = most // parts
    for n in range(parts):
        part = (refs[2 * n][0, 0] + refs[2 * n + 1][0, 0].astype(f32)).astype(bf16)
        projected_ref[:, n * width : (n + 1) * width] = part
    projected = projected_ref[...]
    gram[...] = lax.dot_general(projected, projected, (((0,), (0,)), ((), ())), preferred_element_type=f32)
    wide = projected.astype(f32)
    diag = jnp.sum(wide * wide, axis=0, keepdims=True)
    diag_ref[0] = diag
    mine = ids[0] & 1
    for n in range(count):
        stays_ref[0, n] = gram[pl.ds(pl.multiple_of((2 * n + mine) * rows, rows), rows), :]
        other = gram[pl.ds(pl.multiple_of((2 * n + 1 - mine) * rows, rows), rows), :]
        sent_ref[0, pl.ds(n * rows, rows), :] = other.astype(bf16)
    sent_ref[0, pl.ds(count * rows, PACK), :] = packed(diag)


def gram_split(ids, values, groups):
    depth, most = values[0][0].shape[2:]
    most = most * len(values)
    rows, count = most // groups, groups // 2
    operands = [x for value in values for x in value]
    return pl.pallas_call(
        functools.partial(gram_body, len(values)),
        out_shape=(
            jax.ShapeDtypeStruct((depth, most), bf16),
            jax.ShapeDtypeStruct((1, count * rows + PACK, most), bf16),
            jax.ShapeDtypeStruct((1, count, rows, most), f32),
            jax.ShapeDtypeStruct((1, 1, most), f32),
        ),
        in_specs=[SMEM] + [VMEM] * len(operands),
        out_specs=(VMEM,) * 4,
        scratch_shapes=[pltpu.VMEM((most, most), f32)],
        cost_estimate=pl.CostEstimate(flops=2 * depth * most * most, bytes_accessed=2**20, transcendentals=0),
        compiler_params=pltpu.CompilerParams(vmem_limit_bytes=6 * MIB),
        name="gram_split",
    )(ids, *operands)


def refine_body(slot, halves, per_group, ids, sectors_ref, kept_ref, stays_ref, taken_ref, gdiag_ref, corr_ref, out_ref):
    rows, most = out_ref.shape
    block, col = ids[0], ids[1]
    first = (block * halves + col % halves) * rows
    rank = kept_ref[sectors_ref[(col // halves) * per_group + slot]]
    gram = stays_ref[0, 0] + taken_ref[0, pl.ds(0, rows), :].astype(f32)
    gdiag = gdiag_ref[0] + unpacked(taken_ref[0, pl.ds(rows, PACK), :])
    cdiag = unpacked(corr_ref[0, pl.ds(rows, PACK), :])
    lam = gdiag / (cdiag + 1e-06)
    i = first + lax.broadcasted_iota(jnp.int32, (rows, most), 0)
    j = lax.broadcasted_iota(jnp.int32, (rows, most), 1)
    lam_j = jnp.broadcast_to(lam, (rows, most))
    lam_i = jnp.sum(jnp.where(i == j, lam_j, 0.0), axis=1, keepdims=True)
    differ = lam_j - lam_i
    total = damping * (lam_i + lam_j)
    divisor = differ * differ + total * total + 1e-06
    offdiag = (gram - lam_j * corr_ref[0, pl.ds(0, rows), :].astype(f32)) * differ / divisor
    result = jnp.where(i == j, 0.5 * (1.0 - cdiag), offdiag)
    inside = (i < rank) & (j < rank)
    out_ref[...] = jnp.where(inside, result, 0.0).astype(bf16)


def refine(slot, ids, slot_sector, kept, stays, taken, gdiag, corr, halves, per_group):
    _, _, rows, most = stays.shape
    return pl.pallas_call(
        functools.partial(refine_body, slot, halves, per_group),
        out_shape=jax.ShapeDtypeStruct((rows, most), bf16),
        in_specs=[SMEM] * 3 + [VMEM] * 4,
        out_specs=VMEM,
        cost_estimate=pl.CostEstimate(flops=10**6, bytes_accessed=2**19, transcendentals=0),
        compiler_params=pltpu.CompilerParams(vmem_limit_bytes=4 * MIB),
        name="refine",
    )(ids, slot_sector, kept, stays, taken, gdiag, corr)


def final_body(slot, per_group, halves, pieces, ids, sectors_ref, kept_ref, vectors_ref, left_ref, *refs):
    piece_refs = refs[:pieces]
    right_out, left_out, corr = refs[-3:]
    rows, most = piece_refs[0].shape
    rank = kept_ref[sectors_ref[ids[0] * per_group + slot]]

    def finish(narrow):
        out = narrow.astype(f32) + jnp.dot(narrow, corr[...], preferred_element_type=f32)
        j = lax.broadcasted_iota(jnp.int32, out.shape, 1)
        return jnp.where(j < rank, out, 0.0)

    @pl.when(pl.program_id(0) == 0)
    def _():
        half = ids[1] % halves
        for k in range(pieces - 1):
            at = ((ids[1] // halves) ^ k) * halves
            corr[pl.ds(pl.multiple_of((at + half) * rows, rows), rows), :] = piece_refs[k][...]
            other = piece_refs[-1][pl.ds(k * rows, rows), :]
            corr[pl.ds(pl.multiple_of((at + 1 - half) * rows, rows), rows), :] = other
        out = finish(left_ref[...])
        left_out[:, 0] = out.reshape(out.shape[0] // 4, 4, most)

    right_out[0] = finish(vectors_ref[0])


def final(slot, ids, slot_sector, kept, vectors, left, pieces, carried, halves):
    per_group, depth, most = vectors.shape
    tile = depth // 2
    rows = left.shape[0] // 4
    whole = lambda shape: pl.BlockSpec(shape, lambda t, *_: (0,) * len(shape))
    right_shape = jax.ShapeDtypeStruct((per_group, depth, most), f32)
    left_shape = jax.ShapeDtypeStruct((rows, per_group, 4, most), f32)
    in_specs = [
        pl.BlockSpec((1, tile, most), lambda t, *_: (slot, t, 0)),
        whole(left.shape),
    ] + [whole(piece.shape) for piece in pieces]
    operands = [vectors, left] + list(pieces)
    aliases = {}
    if carried is not None:
        aliases = {3 + len(operands): 0, 4 + len(operands): 1}
        in_specs += [pl.BlockSpec(memory_space=pl.ANY)] * 2
        operands += list(carried)
    return pl.pallas_call(
        functools.partial(final_body, slot, per_group, halves, len(pieces)),
        out_shape=(right_shape, left_shape),
        grid_spec=pltpu.PrefetchScalarGridSpec(
            num_scalar_prefetch=3,
            grid=(depth // tile,),
            in_specs=in_specs,
            out_specs=(
                pl.BlockSpec((1, tile, most), lambda t, *_: (slot, t, 0)),
                pl.BlockSpec((rows, 1, 4, most), lambda t, *_: (0, slot, 0, 0)),
            ),
            scratch_shapes=[pltpu.VMEM((most, most), bf16)],
        ),
        input_output_aliases=aliases,
        cost_estimate=pl.CostEstimate(flops=2 * 1216 * most * most, bytes_accessed=4 * 2**20, transcendentals=0),
        compiler_params=pltpu.CompilerParams(vmem_limit_bytes=12 * MIB),
        name="final",
    )(ids, slot_sector, kept, *operands)


def halve_body(shift, halves, first, ids, stays_in, taken_in, *refs):
    other, (sent_ref, stays_ref) = refs[:-2], refs[-2:]
    most = stays_ref.shape[3]
    want = (((ids[1] // halves) ^ ids[0]) >> shift) & 1
    for s in range(stays_ref.shape[0]):
        for n in range(stays_ref.shape[1]):
            if other:
                part = pl.ds(first, most)
                low = stays_in[0, 0, :, part] + taken_in[0, 0, :, part].astype(f32)
                high = other[0][0, 0] + other[1][0, 0].astype(f32)
                stays_ref[s, n] = jnp.where(want == 1, high, low)
                sent_ref[s, n] = jnp.where(want == 1, low, high).astype(bf16)
            else:
                at = 2 * n + want
                stays_ref[s, n] = stays_in[s, at] + taken_in[s, at].astype(f32)
                at = 2 * n + 1 - want
                sent_ref[s, n] = (stays_in[s, at] + taken_in[s, at].astype(f32)).astype(bf16)


def halve(ids, shift, halves, value, other=None, first=0):
    slots, count, rows, most = (other or value)[0].shape
    shape = (1, 1, rows, most) if other else (slots, count // 2, rows, most)
    operands = list(value) + list(other or ())
    return pl.pallas_call(
        functools.partial(halve_body, shift, halves, first),
        out_shape=(jax.ShapeDtypeStruct(shape, bf16), jax.ShapeDtypeStruct(shape, f32)),
        in_specs=[SMEM] + [VMEM] * len(operands),
        out_specs=(VMEM,) * 2,
        cost_estimate=pl.CostEstimate(flops=10**6, bytes_accessed=2**20, transcendentals=0),
        compiler_params=pltpu.CompilerParams(vmem_limit_bytes=8 * MIB),
    )(ids, *operands)


def work(theta, gate, warm_start, slot_sector, kept, block_offsets):
    groups, cols = lax.axis_size("row"), lax.axis_size("col")
    block, col = lax.axis_index("row"), lax.axis_index("col")
    halves = cols // groups
    per_group, _, bond_cols, most = warm_start.shape
    group_bits = groups.bit_length() - 1
    ids = jnp.stack([block, col]).astype(jnp.int32)
    vectors = warm_start.reshape(per_group, 4 * bond_cols, most)
    gate_matrix = gate.reshape(CHUNK, CHUNK)

    parts = [2] * per_group

    across = {}
    remaining = vectors
    for s in range(per_group):
        width = most // parts[s]
        for p in range(parts[s]):
            own = remaining[s : s + 1, :, p * width : (p + 1) * width]
            own, remaining = lax.optimization_barrier((own, remaining))
            across[s, p] = {d: swap(own, "row", d) for d in range(2, groups, 2)}
    partner = swap(vectors, "row", 1)

    def place(b, g, h):
        return b * cols + g * halves + h

    def turned(value, k=0, hop=0):
        pairs = [
            (place(b ^ hop, g, h), place(g, b ^ k, h))
            for b in range(groups)
            for g in range(groups)
            for h in range(halves)
        ]
        return lax.ppermute(value, ("row", "col"), pairs)

    def turned_over(value):
        value = swap(value, "row", groups // 2)
        return turned(value, 0, groups // 2)

    corr = jnp.einsum("snk,snl->skl", vectors, vectors, preferred_element_type=f32)
    corr = corr.reshape(per_group, groups, most // groups, most)
    sent, stays, diag = corr_split(ids, corr, halves)
    for t in range(group_bits):
        taken = swap(sent, "col", halves << t)
        which = ("group", t + 1) if t + 1 < group_bits else ("half", 0)
        sent, stays, diag = step(ids, stays, taken, diag, which, halves)
    taken = swap(sent, "col", 1)
    sent, _, _ = step(ids, stays, taken, diag, None, halves)
    corr = []
    for s in range(per_group):
        if s == 0:
            corr.append(turned(sent[s : s + 1]))
        else:
            corr.append(turned_over(sent[s : s + 1]))

    def reduced(sent, stays):
        taken = swap(sent, "col", 1)
        for t in range(group_bits - 1):
            sent, stays = halve(ids, t, halves, (stays, taken))
            taken = swap(sent, "col", halves << t)
        return stays, taken

    gated = gate_rows(ids, slot_sector, block_offsets, theta, gate_matrix, groups, halves, per_group)
    near = []
    for s in range(per_group):
        operands = [vectors, partner]
        for d in range(2, groups // 2, 2):
            arrived = jnp.concatenate([across[s, p][d] for p in range(parts[s])], axis=2)
            operands += [arrived, swap(arrived, "row", 1)]
        value = product(s, 0, gated, operands)
        near.append(reduced(*value))
    last = group_bits - 1
    carried = None
    for s in range(per_group):
        values = []
        for p in range(parts[s]):
            far = []
            for d in range(groups // 2, groups, 2):
                far += [across[s, p][d], swap(across[s, p][d], "row", 1)]
            far = product(s, 1, gated, far)
            far = reduced(*far)
            sent, stays = halve(ids, last, halves, near[s], far, p * (most // parts[s]))
            values.append((stays, swap(sent, "col", halves << last)))
        projected, sent, stays, diag = gram_split(ids, values, groups)
        left = turned(projected)
        for t in range(1, group_bits + 1):
            taken = swap(sent, "row", 1 << (t - 1))
            which = ("row", t) if t < group_bits else ("half", 0)
            sent, stays, diag = step(ids, stays, taken, diag, which, halves)
        taken = swap(sent, "col", 1)
        piece = refine(s, ids, slot_sector, kept, stays, taken, diag, corr[s], halves, per_group)
        pieces = []
        for k in range(groups):
            pieces.append(turned(piece, k))
        pieces.append(swap(jnp.concatenate(pieces), "col", 1))
        carried = final(s, ids, slot_sector, kept, vectors, left, pieces, carried, halves)
    right, left = carried
    return left, right.reshape(warm_start.shape)


def solution(mesh):
    in_specs = (P("row", None, None, "col"), P(), P("row", None, "col", None), P(), P(), P())
    out_specs = (P("col", "row", None, None), P("row", None, "col", None))
    return jax.shard_map(work, mesh=mesh, in_specs=in_specs, out_specs=out_specs, check_vma=False)
```

```python
import functools

import jax
import jax.numpy as jnp
from jax import lax
from jax.experimental import pallas as pl
from jax.experimental.pallas import tpu as pltpu
from jax.sharding import PartitionSpec as P


NMAX = 96
CHUNK = 16
MIB = 2**20
damping = 0.25


VMEM = pl.BlockSpec(memory_space=pltpu.VMEM)
SMEM = pl.BlockSpec(memory_space=pltpu.SMEM)
f32, bf16 = jnp.float32, jnp.bfloat16


def swap(value, axis, mask):
    count = lax.axis_size(axis)
    return lax.ppermute(value, axis, [(i, i ^ mask) for i in range(count)])


def window(ids, sectors_ref, offsets_ref, block_rows, far, slot, half, rows, per_group):
    block = ids[0]
    sector = sectors_ref[(far ^ block) * per_group + slot]
    number = offsets_ref.shape[1]
    start = offsets_ref[block, sector]
    following = offsets_ref[block, jnp.minimum(sector + 1, number - 1)]
    end = jnp.where(sector + 1 < number, following, block_rows)
    start = start + half * rows
    return start, jnp.clip(end - start, 0, rows)


def prepare(theta_hbm, gate_ref, theta, mixer, sem):
    block_rows = theta_hbm.shape[0]
    size = CHUNK * CHUNK
    copy = pltpu.make_async_copy(theta_hbm, theta.at[pl.ds(0, block_rows)], sem)
    copy.start()
    theta[pl.ds(block_rows, NMAX)] = jnp.zeros((NMAX,) + theta.shape[1:], theta.dtype)
    tall_row = lax.broadcasted_iota(jnp.int32, (size, CHUNK), 0)
    tall_col = lax.broadcasted_iota(jnp.int32, (size, CHUNK), 1)
    wide_row = lax.broadcasted_iota(jnp.int32, (CHUNK, size), 0)
    wide_col = lax.broadcasted_iota(jnp.int32, (CHUNK, size), 1)
    spread = ((tall_row % 4) * 4 + tall_row // (4 * CHUNK) == tall_col).astype(bf16)
    repeat = (wide_col % CHUNK == wide_row).astype(bf16)
    tall = jnp.dot(spread, gate_ref[...], preferred_element_type=f32).astype(bf16)
    full = jnp.dot(tall, repeat, preferred_element_type=f32)
    row = lax.broadcasted_iota(jnp.int32, (size, size), 0)
    col = lax.broadcasted_iota(jnp.int32, (size, size), 1)
    mixer[...] = jnp.where((row // 4) % CHUNK == col // CHUNK, full, 0.0).astype(bf16)
    copy.wait()


def gated_window(theta, mixer, start, live, rows, store):
    size = CHUNK * CHUNK
    cols = theta.shape[3]
    for part in range(rows // CHUNK):
        first = jnp.clip(start + part * CHUNK, 0, theta.shape[0] - CHUNK)
        piece = theta[pl.ds(first, CHUNK)].reshape(size, cols)
        mixed = jnp.dot(mixer[...], piece, preferred_element_type=f32)
        place = part * CHUNK + lax.broadcasted_iota(jnp.int32, (4 * CHUNK, cols), 0) // 4
        for b in range(4):
            value = mixed[b * 4 * CHUNK : (b + 1) * 4 * CHUNK, :]
            value = jnp.where(place < live, value, 0.0).astype(bf16)
            store(pl.ds(part * 4 * CHUNK, 4 * CHUNK), pl.ds(b * cols, cols), value)


def theta_scratch(theta):
    return [
        pltpu.VMEM((theta.shape[0] + NMAX,) + theta.shape[1:], bf16),
        pltpu.VMEM((CHUNK * CHUNK, CHUNK * CHUNK), bf16),
        pltpu.SemaphoreType.DMA,
    ]


def gate_body(halves, per_group, ids, sectors_ref, offsets_ref, theta_hbm, gate_ref, out_ref, theta, mixer, sem):
    slot, n = pl.program_id(0), pl.program_id(1)
    rows = NMAX // halves

    @pl.when((slot == 0) & (n == 0))
    def _():
        prepare(theta_hbm, gate_ref, theta, mixer, sem)

    for far_half in (0, 1):
        half = (ids[1] % halves) ^ (1 - far_half)
        start, live = window(
            ids, sectors_ref, offsets_ref, theta_hbm.shape[0], n, slot, half, rows, per_group
        )

        def store(at, cols, value, base=far_half * 4 * rows):
            out_ref[0, 0, pl.ds(base + at.start, at.size), cols] = value

        gated_window(theta, mixer, start, live, rows, store)


def gate_rows(ids, slot_sector, block_offsets, theta, gate, count, halves, per_group):
    rows, cols = NMAX // halves, theta.shape[3]
    block = (1, 1, halves * 4 * rows, 4 * cols)
    return pl.pallas_call(
        functools.partial(gate_body, halves, per_group),
        out_shape=jax.ShapeDtypeStruct((per_group, count) + block[2:], bf16),
        grid_spec=pltpu.PrefetchScalarGridSpec(
            num_scalar_prefetch=3,
            grid=(per_group, count),
            in_specs=[
                pl.BlockSpec(memory_space=pltpu.HBM),
                pl.BlockSpec((CHUNK, CHUNK), lambda s, n, *_: (0, 0)),
            ],
            out_specs=pl.BlockSpec(block, lambda s, n, *_: (s, n, 0, 0)),
            scratch_shapes=theta_scratch(theta),
        ),
        cost_estimate=pl.CostEstimate(flops=6 * 10**9, bytes_accessed=12 * 2**20, transcendentals=0),
        compiler_params=pltpu.CompilerParams(vmem_limit_bytes=14 * MIB),
        name="gate_rows",
    )(ids, slot_sector, block_offsets, theta, gate)


def product_body(count, lhs_ref, *refs):
    vector_refs = refs[:count]
    sent_ref, kept_ref = refs[count:]
    rows = sent_ref.shape[2]
    for n in range(count):
        out = jnp.dot(lhs_ref[0, n], vector_refs[n][0], preferred_element_type=f32)
        sent_ref[0, n] = out[:rows].astype(bf16)
        kept_ref[0, n] = out[rows:]


def product(slot, chunk, gated, vectors):
    _, _, rows, depth = gated.shape
    count = len(vectors)
    most = vectors[0].shape[2]
    out_block = (1, count, rows // 2, most)
    return pl.pallas_call(
        functools.partial(product_body, count),
        out_shape=(jax.ShapeDtypeStruct(out_block, bf16), jax.ShapeDtypeStruct(out_block, f32)),
        grid=(1,),
        in_specs=[pl.BlockSpec((1, count, rows, depth), lambda i: (slot, chunk, 0, 0))]
        + [pl.BlockSpec((1, depth, most), lambda i, at=min(slot, v.shape[0] - 1): (at, 0, 0)) for v in vectors],
        out_specs=(pl.BlockSpec(out_block, lambda i: (0, 0, 0, 0)),) * 2,
        cost_estimate=pl.CostEstimate(flops=8 * 10**8, bytes_accessed=5 * 2**20, transcendentals=0),
        compiler_params=pltpu.CompilerParams(vmem_limit_bytes=16 * MIB),
    )(gated, *vectors)


PACK = 16


def packed(diag):
    high = diag.astype(bf16)
    rest = diag - high.astype(f32)
    middle = rest.astype(bf16)
    low = (rest - middle.astype(f32)).astype(bf16)
    row = lax.broadcasted_iota(jnp.int32, (PACK, diag.shape[1]), 0)
    wide = [jnp.broadcast_to(x.astype(f32), row.shape) for x in (high, middle, low)]
    return jnp.where(row == 0, wide[0], jnp.where(row == 1, wide[1], jnp.where(row == 2, wide[2], 0.0))).astype(bf16)


def unpacked(block):
    return jnp.sum(block.astype(f32), axis=0, keepdims=True)


def bit_of(ids, which, halves):
    source, shift = which
    value = {"row": ids[0], "group": ids[1] // halves, "half": ids[1] % halves}[source]
    return (value >> shift) & 1


def corr_body(halves, ids, corr_ref, sent_ref, stays_ref, diag_ref):
    slots, count, rows, most = stays_ref.shape
    mine = bit_of(ids, ("group", 0), halves)
    for s in range(slots):
        diag = jnp.zeros((1, most), f32)
        for n in range(2 * count):
            i = n * rows + lax.broadcasted_iota(jnp.int32, (rows, most), 0)
            j = lax.broadcasted_iota(jnp.int32, (rows, most), 1)
            diag = diag + jnp.sum(jnp.where(i == j, corr_ref[s, n], 0.0), axis=0, keepdims=True)
        diag_ref[s] = diag
        for n in range(count):
            stays_ref[s, n] = corr_ref[s, 2 * n + mine]
            sent_ref[s, pl.ds(n * rows, rows), :] = corr_ref[s, 2 * n + 1 - mine].astype(bf16)
        sent_ref[s, pl.ds(count * rows, PACK), :] = packed(diag)


def corr_split(ids, corr, halves):
    slots, count, rows, most = corr.shape
    count = count // 2
    return pl.pallas_call(
        functools.partial(corr_body, halves),
        out_shape=(
            jax.ShapeDtypeStruct((slots, count * rows + PACK, most), bf16),
            jax.ShapeDtypeStruct((slots, count, rows, most), f32),
            jax.ShapeDtypeStruct((slots, 1, most), f32),
        ),
        in_specs=[SMEM, VMEM],
        out_specs=(VMEM,) * 3,
        cost_estimate=pl.CostEstimate(flops=10**6, bytes_accessed=2**21, transcendentals=0),
        compiler_params=pltpu.CompilerParams(vmem_limit_bytes=8 * MIB),
        name="corr_split",
    )(ids, corr)


def step_body(which, halves, ids, stays_in, taken_ref, diag_in, sent_ref, stays_ref, diag_ref):
    slots, count, rows, _ = stays_ref.shape
    before, block = stays_in.shape[1:3]
    mine = bit_of(ids, which, halves) if which else 0
    for s in range(slots):
        diag = diag_in[s] + unpacked(taken_ref[s, pl.ds(before * block, PACK), :])
        diag_ref[s] = diag

        def total(at, first=0):
            there = pl.multiple_of(at * block + first, rows)
            return stays_in[s, at, pl.ds(first, rows), :] + taken_ref[s, pl.ds(there, rows), :].astype(f32)

        for n in range(count):
            if not which:
                value = total(n)
                stays_ref[s, n] = value
            elif block != rows:
                stays_ref[s, n] = total(n, pl.multiple_of(mine * rows, rows))
                value = total(n, pl.multiple_of((1 - mine) * rows, rows))
            else:
                stays_ref[s, n] = total(2 * n + mine)
                value = total(2 * n + 1 - mine)
            sent_ref[s, pl.ds(n * rows, rows), :] = value.astype(bf16)
        sent_ref[s, pl.ds(count * rows, PACK), :] = packed(diag)


def step(ids, stays, taken, diag, which, halves):
    slots, count, rows, most = stays.shape
    if which and which[0] == "half":
        rows = rows // halves
    elif which:
        count = count // 2
    return pl.pallas_call(
        functools.partial(step_body, which, halves),
        out_shape=(
            jax.ShapeDtypeStruct((slots, count * rows + PACK, most), bf16),
            jax.ShapeDtypeStruct((slots, count, rows, most), f32),
            jax.ShapeDtypeStruct((slots, 1, most), f32),
        ),
        in_specs=[SMEM] + [VMEM] * 3,
        out_specs=(VMEM,) * 3,
        cost_estimate=pl.CostEstimate(flops=10**6, bytes_accessed=2**19, transcendentals=0),
        compiler_params=pltpu.CompilerParams(vmem_limit_bytes=8 * MIB),
    )(ids, stays, taken, diag)


def gram_body(parts, ids, *refs):
    projected_ref, sent_ref, stays_ref, diag_ref, gram = refs[2 * parts :]
    _, count, rows, most = stays_ref.shape
    width = most // parts
    for n in range(parts):
        part = (refs[2 * n][0, 0] + refs[2 * n + 1][0, 0].astype(f32)).astype(bf16)
        projected_ref[:, n * width : (n + 1) * width] = part
    projected = projected_ref[...]
    gram[...] = lax.dot_general(projected, projected, (((0,), (0,)), ((), ())), preferred_element_type=f32)
    wide = projected.astype(f32)
    diag = jnp.sum(wide * wide, axis=0, keepdims=True)
    diag_ref[0] = diag
    mine = ids[0] & 1
    for n in range(count):
        stays_ref[0, n] = gram[pl.ds(pl.multiple_of((2 * n + mine) * rows, rows), rows), :]
        other = gram[pl.ds(pl.multiple_of((2 * n + 1 - mine) * rows, rows), rows), :]
        sent_ref[0, pl.ds(n * rows, rows), :] = other.astype(bf16)
    sent_ref[0, pl.ds(count * rows, PACK), :] = packed(diag)


def gram_split(ids, values, groups):
    depth, most = values[0][0].shape[2:]
    most = most * len(values)
    rows, count = most // groups, groups // 2
    operands = [x for value in values for x in value]
    return pl.pallas_call(
        functools.partial(gram_body, len(values)),
        out_shape=(
            jax.ShapeDtypeStruct((depth, most), bf16),
            jax.ShapeDtypeStruct((1, count * rows + PACK, most), bf16),
            jax.ShapeDtypeStruct((1, count, rows, most), f32),
            jax.ShapeDtypeStruct((1, 1, most), f32),
        ),
        in_specs=[SMEM] + [VMEM] * len(operands),
        out_specs=(VMEM,) * 4,
        scratch_shapes=[pltpu.VMEM((most, most), f32)],
        cost_estimate=pl.CostEstimate(flops=2 * depth * most * most, bytes_accessed=2**20, transcendentals=0),
        compiler_params=pltpu.CompilerParams(vmem_limit_bytes=6 * MIB),
        name="gram_split",
    )(ids, *operands)


def refine_body(slot, halves, per_group, ids, sectors_ref, kept_ref, stays_ref, taken_ref, gdiag_ref, corr_ref, out_ref):
    rows, most = out_ref.shape
    block, col = ids[0], ids[1]
    first = (block * halves + col % halves) * rows
    rank = kept_ref[sectors_ref[(col // halves) * per_group + slot]]
    gram = stays_ref[0, 0] + taken_ref[0, pl.ds(0, rows), :].astype(f32)
    gdiag = gdiag_ref[0] + unpacked(taken_ref[0, pl.ds(rows, PACK), :])
    cdiag = unpacked(corr_ref[slot, pl.ds(rows, PACK), :])
    lam = gdiag / (cdiag + 1e-06)
    i = first + lax.broadcasted_iota(jnp.int32, (rows, most), 0)
    j = lax.broadcasted_iota(jnp.int32, (rows, most), 1)
    lam_j = jnp.broadcast_to(lam, (rows, most))
    lam_i = jnp.sum(jnp.where(i == j, lam_j, 0.0), axis=1, keepdims=True)
    differ = lam_j - lam_i
    total = damping * (lam_i + lam_j)
    divisor = differ * differ + total * total + 1e-06
    offdiag = (gram - lam_j * corr_ref[slot, pl.ds(0, rows), :].astype(f32)) * differ / divisor
    result = jnp.where(i == j, 0.5 * (1.0 - cdiag), offdiag)
    inside = (i < rank) & (j < rank)
    out_ref[...] = jnp.where(inside, result, 0.0).astype(bf16)


def refine(slot, ids, slot_sector, kept, stays, taken, gdiag, corr, halves, per_group):
    _, _, rows, most = stays.shape
    return pl.pallas_call(
        functools.partial(refine_body, slot, halves, per_group),
        out_shape=jax.ShapeDtypeStruct((rows, most), bf16),
        in_specs=[SMEM] * 3 + [VMEM] * 4,
        out_specs=VMEM,
        cost_estimate=pl.CostEstimate(flops=10**6, bytes_accessed=2**19, transcendentals=0),
        compiler_params=pltpu.CompilerParams(vmem_limit_bytes=4 * MIB),
        name="refine",
    )(ids, slot_sector, kept, stays, taken, gdiag, corr)


def final_body(slot, per_group, halves, order, ids, sectors_ref, kept_ref, vectors_ref, left_ref, own_ref, other_ref, *refs):
    right_out, left_out, corr = refs[-3:]
    rows, most = own_ref.shape[0] // len(order), own_ref.shape[1]
    rank = kept_ref[sectors_ref[ids[0] * per_group + slot]]

    def finish(narrow):
        out = narrow.astype(f32) + jnp.dot(narrow, corr[...], preferred_element_type=f32)
        j = lax.broadcasted_iota(jnp.int32, out.shape, 1)
        return jnp.where(j < rank, out, 0.0)

    @pl.when(pl.program_id(0) == 0)
    def _():
        half = ids[1] % halves
        for n, k in enumerate(order):
            at = ((ids[1] // halves) ^ k) * halves
            mine, others = pl.multiple_of((at + half) * rows, rows), pl.multiple_of((at + 1 - half) * rows, rows)
            corr[pl.ds(mine, rows), :] = own_ref[pl.ds(n * rows, rows), :]
            corr[pl.ds(others, rows), :] = other_ref[pl.ds(n * rows, rows), :]
        out = finish(left_ref[...])
        left_out[:, 0] = out.reshape(out.shape[0] // 4, 4, most)

    right_out[0] = finish(vectors_ref[0])


def final(slot, ids, slot_sector, kept, vectors, left, own, other, order, carried, halves):
    per_group, depth, most = vectors.shape
    tile = depth // 2
    rows = left.shape[0] // 4
    whole = lambda shape: pl.BlockSpec(shape, lambda t, *_: (0,) * len(shape))
    right_shape = jax.ShapeDtypeStruct((per_group, depth, most), f32)
    left_shape = jax.ShapeDtypeStruct((rows, per_group, 4, most), f32)
    in_specs = [
        pl.BlockSpec((1, tile, most), lambda t, *_: (slot, t, 0)),
        whole(left.shape),
        whole(own.shape),
        whole(other.shape),
    ]
    operands = [vectors, left, own, other]
    aliases = {}
    if carried is not None:
        aliases = {3 + len(operands): 0, 4 + len(operands): 1}
        in_specs += [pl.BlockSpec(memory_space=pl.ANY)] * 2
        operands += list(carried)
    return pl.pallas_call(
        functools.partial(final_body, slot, per_group, halves, order),
        out_shape=(right_shape, left_shape),
        grid_spec=pltpu.PrefetchScalarGridSpec(
            num_scalar_prefetch=3,
            grid=(depth // tile,),
            in_specs=in_specs,
            out_specs=(
                pl.BlockSpec((1, tile, most), lambda t, *_: (slot, t, 0)),
                pl.BlockSpec((rows, 1, 4, most), lambda t, *_: (0, slot, 0, 0)),
            ),
            scratch_shapes=[pltpu.VMEM((most, most), bf16)],
        ),
        input_output_aliases=aliases,
        cost_estimate=pl.CostEstimate(flops=2 * 1216 * most * most, bytes_accessed=4 * 2**20, transcendentals=0),
        compiler_params=pltpu.CompilerParams(vmem_limit_bytes=12 * MIB),
        name="final",
    )(ids, slot_sector, kept, *operands)


def halve_body(shift, halves, first, ids, stays_in, taken_in, *refs):
    other, (sent_ref, stays_ref) = refs[:-2], refs[-2:]
    most = stays_ref.shape[3]
    want = (((ids[1] // halves) ^ ids[0]) >> shift) & 1
    for s in range(stays_ref.shape[0]):
        for n in range(stays_ref.shape[1]):
            if other:
                part = pl.ds(first, most)
                low = stays_in[0, 0, :, part] + taken_in[0, 0, :, part].astype(f32)
                high = other[0][0, 0] + other[1][0, 0].astype(f32)
                stays_ref[s, n] = jnp.where(want == 1, high, low)
                sent_ref[s, n] = jnp.where(want == 1, low, high).astype(bf16)
            else:
                at = 2 * n + want
                stays_ref[s, n] = stays_in[s, at] + taken_in[s, at].astype(f32)
                at = 2 * n + 1 - want
                sent_ref[s, n] = (stays_in[s, at] + taken_in[s, at].astype(f32)).astype(bf16)


def halve(ids, shift, halves, value, other=None, first=0):
    slots, count, rows, most = (other or value)[0].shape
    shape = (1, 1, rows, most) if other else (slots, count // 2, rows, most)
    operands = list(value) + list(other or ())
    return pl.pallas_call(
        functools.partial(halve_body, shift, halves, first),
        out_shape=(jax.ShapeDtypeStruct(shape, bf16), jax.ShapeDtypeStruct(shape, f32)),
        in_specs=[SMEM] + [VMEM] * len(operands),
        out_specs=(VMEM,) * 2,
        cost_estimate=pl.CostEstimate(flops=10**6, bytes_accessed=2**20, transcendentals=0),
        compiler_params=pltpu.CompilerParams(vmem_limit_bytes=8 * MIB),
    )(ids, *operands)


def work(theta, gate, warm_start, slot_sector, kept, block_offsets):
    groups, cols = lax.axis_size("row"), lax.axis_size("col")
    block, col = lax.axis_index("row"), lax.axis_index("col")
    halves = cols // groups
    per_group, _, bond_cols, most = warm_start.shape
    group_bits = groups.bit_length() - 1
    ids = jnp.stack([block, col]).astype(jnp.int32)
    vectors = warm_start.reshape(per_group, 4 * bond_cols, most)
    gate_matrix = gate.reshape(CHUNK, CHUNK)

    parts = [1] * (per_group - 1) + [2]

    across = {}
    remaining = vectors
    for s in range(per_group):
        width = most // parts[s]
        for p in range(parts[s]):
            own = remaining[s : s + 1, :, p * width : (p + 1) * width]
            own, remaining = lax.optimization_barrier((own, remaining))
            across[s, p] = {d: swap(own, "row", d) for d in range(2, groups, 2)}
    partner = swap(vectors, "row", 1)

    def place(b, g, h):
        return b * cols + g * halves + h

    def turned(value, k=0):
        pairs = [
            (place(b, g, h), place(g, b ^ k, h))
            for b in range(groups)
            for g in range(groups)
            for h in range(halves)
        ]
        return lax.ppermute(value, ("row", "col"), pairs)

    corr = jnp.einsum("snk,snl->skl", vectors, vectors, preferred_element_type=f32)
    corr = corr.reshape(per_group, groups, most // groups, most)
    sent, stays, diag = corr_split(ids, corr, halves)
    for t in range(group_bits):
        taken = swap(sent, "col", halves << t)
        which = ("group", t + 1) if t + 1 < group_bits else ("half", 0)
        sent, stays, diag = step(ids, stays, taken, diag, which, halves)
    taken = swap(sent, "col", 1)
    sent, _, _ = step(ids, stays, taken, diag, None, halves)
    corr = turned(sent)

    def reduced(sent, stays):
        taken = swap(sent, "col", 1)
        for t in range(group_bits - 1):
            sent, stays = halve(ids, t, halves, (stays, taken))
            taken = swap(sent, "col", halves << t)
        return stays, taken

    gated = gate_rows(ids, slot_sector, block_offsets, theta, gate_matrix, groups, halves, per_group)
    near = []
    for s in range(per_group):
        operands = [vectors, partner]
        for d in range(2, groups // 2, 2):
            arrived = jnp.concatenate([across[s, p][d] for p in range(parts[s])], axis=2)
            operands += [arrived, swap(arrived, "row", 1)]
        value = product(s, 0, gated, operands)
        near.append(reduced(*value))
    last = group_bits - 1
    carried = None
    for s in range(per_group):
        values = []
        for p in range(parts[s]):
            far = []
            for d in range(groups // 2, groups, 2):
                far += [across[s, p][d], swap(across[s, p][d], "row", 1)]
            far = product(s, 1, gated, far)
            far = reduced(*far)
            sent, stays = halve(ids, last, halves, near[s], far, p * (most // parts[s]))
            values.append((stays, swap(sent, "col", halves << last)))
        projected, sent, stays, diag = gram_split(ids, values, groups)
        left = turned(projected)
        for t in range(1, group_bits + 1):
            taken = swap(sent, "row", 1 << (t - 1))
            which = ("row", t) if t < group_bits else ("half", 0)
            sent, stays, diag = step(ids, stays, taken, diag, which, halves)
        taken = swap(sent, "col", 1)
        piece = refine(s, ids, slot_sector, kept, stays, taken, diag, corr, halves, per_group)
        if s == per_group - 1:
            order = list(range(groups))
            pieces = []
            for k in order:
                pieces.append(turned(piece, k))
            own = jnp.concatenate(pieces)
        else:
            order = [0]
            own = turned(piece)
            for t in reversed(range(group_bits)):
                own = jnp.concatenate([own, swap(own, "col", halves << t)])
                order += [k ^ (1 << t) for k in order]
        other = swap(own, "col", 1)
        carried = final(s, ids, slot_sector, kept, vectors, left, own, other, order, carried, halves)
    right, left = carried
    return left, right.reshape(warm_start.shape)


def solution(mesh):
    in_specs = (P("row", None, None, "col"), P(), P("row", None, "col", None), P(), P(), P())
    out_specs = (P("col", "row", None, None), P("row", None, "col", None))
    return jax.shard_map(work, mesh=mesh, in_specs=in_specs, out_specs=out_specs, check_vma=False)
```

```python
import functools

import jax
import jax.numpy as jnp
from jax import lax
from jax.experimental import pallas as pl
from jax.experimental.pallas import tpu as pltpu
from jax.sharding import PartitionSpec as P


NMAX = 96
CHUNK = 16
MIB = 2**20
damping = 0.25


VMEM = pl.BlockSpec(memory_space=pltpu.VMEM)
SMEM = pl.BlockSpec(memory_space=pltpu.SMEM)
f32, bf16 = jnp.float32, jnp.bfloat16


def swap(value, axis, mask):
    count = lax.axis_size(axis)
    return lax.ppermute(value, axis, [(i, i ^ mask) for i in range(count)])


def window(ids, sectors_ref, offsets_ref, block_rows, far, slot, half, rows, per_group):
    block = ids[0]
    sector = sectors_ref[(far ^ block) * per_group + slot]
    number = offsets_ref.shape[1]
    start = offsets_ref[block, sector]
    following = offsets_ref[block, jnp.minimum(sector + 1, number - 1)]
    end = jnp.where(sector + 1 < number, following, block_rows)
    start = start + half * rows
    return start, jnp.clip(end - start, 0, rows)


def prepare(theta_hbm, gate_ref, theta, mixer, sem):
    block_rows = theta_hbm.shape[0]
    size = CHUNK * CHUNK
    copy = pltpu.make_async_copy(theta_hbm, theta.at[pl.ds(0, block_rows)], sem)
    copy.start()
    theta[pl.ds(block_rows, NMAX)] = jnp.zeros((NMAX,) + theta.shape[1:], theta.dtype)
    tall_row = lax.broadcasted_iota(jnp.int32, (size, CHUNK), 0)
    tall_col = lax.broadcasted_iota(jnp.int32, (size, CHUNK), 1)
    wide_row = lax.broadcasted_iota(jnp.int32, (CHUNK, size), 0)
    wide_col = lax.broadcasted_iota(jnp.int32, (CHUNK, size), 1)
    spread = ((tall_row % 4) * 4 + tall_row // (4 * CHUNK) == tall_col).astype(bf16)
    repeat = (wide_col % CHUNK == wide_row).astype(bf16)
    tall = jnp.dot(spread, gate_ref[...], preferred_element_type=f32).astype(bf16)
    full = jnp.dot(tall, repeat, preferred_element_type=f32)
    row = lax.broadcasted_iota(jnp.int32, (size, size), 0)
    col = lax.broadcasted_iota(jnp.int32, (size, size), 1)
    mixer[...] = jnp.where((row // 4) % CHUNK == col // CHUNK, full, 0.0).astype(bf16)
    copy.wait()


def gated_window(theta, mixer, start, live, rows, store):
    size = CHUNK * CHUNK
    cols = theta.shape[3]
    for part in range(rows // CHUNK):
        first = jnp.clip(start + part * CHUNK, 0, theta.shape[0] - CHUNK)
        piece = theta[pl.ds(first, CHUNK)].reshape(size, cols)
        mixed = jnp.dot(mixer[...], piece, preferred_element_type=f32)
        place = part * CHUNK + lax.broadcasted_iota(jnp.int32, (4 * CHUNK, cols), 0) // 4
        for b in range(4):
            value = mixed[b * 4 * CHUNK : (b + 1) * 4 * CHUNK, :]
            value = jnp.where(place < live, value, 0.0).astype(bf16)
            store(pl.ds(part * 4 * CHUNK, 4 * CHUNK), pl.ds(b * cols, cols), value)


def theta_scratch(theta):
    return [
        pltpu.VMEM((theta.shape[0] + NMAX,) + theta.shape[1:], bf16),
        pltpu.VMEM((CHUNK * CHUNK, CHUNK * CHUNK), bf16),
        pltpu.SemaphoreType.DMA,
    ]


def gate_body(halves, per_group, ids, sectors_ref, offsets_ref, theta_hbm, gate_ref, out_ref, theta, mixer, sem):
    slot, n = pl.program_id(0), pl.program_id(1)
    rows = NMAX // halves

    @pl.when((slot == 0) & (n == 0))
    def _():
        prepare(theta_hbm, gate_ref, theta, mixer, sem)

    for far_half in (0, 1):
        half = (ids[1] % halves) ^ (1 - far_half)
        start, live = window(
            ids, sectors_ref, offsets_ref, theta_hbm.shape[0], n, slot, half, rows, per_group
        )

        def store(at, cols, value, base=far_half * 4 * rows):
            out_ref[0, 0, pl.ds(base + at.start, at.size), cols] = value

        gated_window(theta, mixer, start, live, rows, store)


def gate_rows(ids, slot_sector, block_offsets, theta, gate, count, halves, per_group):
    rows, cols = NMAX // halves, theta.shape[3]
    block = (1, 1, halves * 4 * rows, 4 * cols)
    return pl.pallas_call(
        functools.partial(gate_body, halves, per_group),
        out_shape=jax.ShapeDtypeStruct((per_group, count) + block[2:], bf16),
        grid_spec=pltpu.PrefetchScalarGridSpec(
            num_scalar_prefetch=3,
            grid=(per_group, count),
            in_specs=[
                pl.BlockSpec(memory_space=pltpu.HBM),
                pl.BlockSpec((CHUNK, CHUNK), lambda s, n, *_: (0, 0)),
            ],
            out_specs=pl.BlockSpec(block, lambda s, n, *_: (s, n, 0, 0)),
            scratch_shapes=theta_scratch(theta),
        ),
        cost_estimate=pl.CostEstimate(flops=6 * 10**9, bytes_accessed=12 * 2**20, transcendentals=0),
        compiler_params=pltpu.CompilerParams(vmem_limit_bytes=14 * MIB),
        name="gate_rows",
    )(ids, slot_sector, block_offsets, theta, gate)


def product_body(count, lhs_ref, *refs):
    vector_refs = refs[:count]
    sent_ref, kept_ref = refs[count:]
    rows = sent_ref.shape[2]
    for n in range(count):
        out = jnp.dot(lhs_ref[0, n], vector_refs[n][0], preferred_element_type=f32)
        sent_ref[0, n] = out[:rows].astype(bf16)
        kept_ref[0, n] = out[rows:]


def product(slot, chunk, gated, vectors):
    _, _, rows, depth = gated.shape
    count = len(vectors)
    most = vectors[0].shape[2]
    out_block = (1, count, rows // 2, most)
    return pl.pallas_call(
        functools.partial(product_body, count),
        out_shape=(jax.ShapeDtypeStruct(out_block, bf16), jax.ShapeDtypeStruct(out_block, f32)),
        grid=(1,),
        in_specs=[pl.BlockSpec((1, count, rows, depth), lambda i: (slot, chunk, 0, 0))]
        + [pl.BlockSpec((1, depth, most), lambda i, at=min(slot, v.shape[0] - 1): (at, 0, 0)) for v in vectors],
        out_specs=(pl.BlockSpec(out_block, lambda i: (0, 0, 0, 0)),) * 2,
        cost_estimate=pl.CostEstimate(flops=8 * 10**8, bytes_accessed=5 * 2**20, transcendentals=0),
        compiler_params=pltpu.CompilerParams(vmem_limit_bytes=16 * MIB),
    )(gated, *vectors)


PACK = 16


def packed(diag):
    high = diag.astype(bf16)
    rest = diag - high.astype(f32)
    middle = rest.astype(bf16)
    low = (rest - middle.astype(f32)).astype(bf16)
    row = lax.broadcasted_iota(jnp.int32, (PACK, diag.shape[1]), 0)
    wide = [jnp.broadcast_to(x.astype(f32), row.shape) for x in (high, middle, low)]
    return jnp.where(row == 0, wide[0], jnp.where(row == 1, wide[1], jnp.where(row == 2, wide[2], 0.0))).astype(bf16)


def unpacked(block):
    return jnp.sum(block.astype(f32), axis=0, keepdims=True)


def bit_of(ids, which, halves):
    source, shift = which
    value = {"row": ids[0], "group": ids[1] // halves, "half": ids[1] % halves}[source]
    return (value >> shift) & 1


def corr_body(halves, ids, corr_ref, sent_ref, stays_ref, diag_ref):
    slots, count, rows, most = stays_ref.shape
    mine = bit_of(ids, ("group", 0), halves)
    for s in range(slots):
        diag = jnp.zeros((1, most), f32)
        for n in range(2 * count):
            i = n * rows + lax.broadcasted_iota(jnp.int32, (rows, most), 0)
            j = lax.broadcasted_iota(jnp.int32, (rows, most), 1)
            diag = diag + jnp.sum(jnp.where(i == j, corr_ref[s, n], 0.0), axis=0, keepdims=True)
        diag_ref[s] = diag
        for n in range(count):
            stays_ref[s, n] = corr_ref[s, 2 * n + mine]
            sent_ref[s, pl.ds(n * rows, rows), :] = corr_ref[s, 2 * n + 1 - mine].astype(bf16)
        sent_ref[s, pl.ds(count * rows, PACK), :] = packed(diag)


def corr_split(ids, corr, halves):
    slots, count, rows, most = corr.shape
    count = count // 2
    return pl.pallas_call(
        functools.partial(corr_body, halves),
        out_shape=(
            jax.ShapeDtypeStruct((slots, count * rows + PACK, most), bf16),
            jax.ShapeDtypeStruct((slots, count, rows, most), f32),
            jax.ShapeDtypeStruct((slots, 1, most), f32),
        ),
        in_specs=[SMEM, VMEM],
        out_specs=(VMEM,) * 3,
        cost_estimate=pl.CostEstimate(flops=10**6, bytes_accessed=2**21, transcendentals=0),
        compiler_params=pltpu.CompilerParams(vmem_limit_bytes=8 * MIB),
        name="corr_split",
    )(ids, corr)


def step_body(which, halves, ids, stays_in, taken_ref, diag_in, sent_ref, stays_ref, diag_ref):
    slots, count, rows, _ = stays_ref.shape
    before, block = stays_in.shape[1:3]
    mine = bit_of(ids, which, halves) if which else 0
    for s in range(slots):
        diag = diag_in[s] + unpacked(taken_ref[s, pl.ds(before * block, PACK), :])
        diag_ref[s] = diag

        def total(at, first=0):
            there = pl.multiple_of(at * block + first, rows)
            return stays_in[s, at, pl.ds(first, rows), :] + taken_ref[s, pl.ds(there, rows), :].astype(f32)

        for n in range(count):
            if not which:
                value = total(n)
                stays_ref[s, n] = value
            elif block != rows:
                stays_ref[s, n] = total(n, pl.multiple_of(mine * rows, rows))
                value = total(n, pl.multiple_of((1 - mine) * rows, rows))
            else:
                stays_ref[s, n] = total(2 * n + mine)
                value = total(2 * n + 1 - mine)
            sent_ref[s, pl.ds(n * rows, rows), :] = value.astype(bf16)
        sent_ref[s, pl.ds(count * rows, PACK), :] = packed(diag)


def step(ids, stays, taken, diag, which, halves):
    slots, count, rows, most = stays.shape
    if which and which[0] == "half":
        rows = rows // halves
    elif which:
        count = count // 2
    return pl.pallas_call(
        functools.partial(step_body, which, halves),
        out_shape=(
            jax.ShapeDtypeStruct((slots, count * rows + PACK, most), bf16),
            jax.ShapeDtypeStruct((slots, count, rows, most), f32),
            jax.ShapeDtypeStruct((slots, 1, most), f32),
        ),
        in_specs=[SMEM] + [VMEM] * 3,
        out_specs=(VMEM,) * 3,
        cost_estimate=pl.CostEstimate(flops=10**6, bytes_accessed=2**19, transcendentals=0),
        compiler_params=pltpu.CompilerParams(vmem_limit_bytes=8 * MIB),
    )(ids, stays, taken, diag)


def gram_body(parts, ids, *refs):
    projected_ref, sent_ref, stays_ref, diag_ref, gram = refs[2 * parts :]
    _, count, rows, most = stays_ref.shape
    width = most // parts
    for n in range(parts):
        part = (refs[2 * n][0, 0] + refs[2 * n + 1][0, 0].astype(f32)).astype(bf16)
        projected_ref[:, n * width : (n + 1) * width] = part
    projected = projected_ref[...]
    gram[...] = lax.dot_general(projected, projected, (((0,), (0,)), ((), ())), preferred_element_type=f32)
    wide = projected.astype(f32)
    diag = jnp.sum(wide * wide, axis=0, keepdims=True)
    diag_ref[0] = diag
    mine = ids[0] & 1
    for n in range(count):
        stays_ref[0, n] = gram[pl.ds(pl.multiple_of((2 * n + mine) * rows, rows), rows), :]
        other = gram[pl.ds(pl.multiple_of((2 * n + 1 - mine) * rows, rows), rows), :]
        sent_ref[0, pl.ds(n * rows, rows), :] = other.astype(bf16)
    sent_ref[0, pl.ds(count * rows, PACK), :] = packed(diag)


def gram_split(ids, values, groups):
    depth, most = values[0][0].shape[2:]
    most = most * len(values)
    rows, count = most // groups, groups // 2
    operands = [x for value in values for x in value]
    return pl.pallas_call(
        functools.partial(gram_body, len(values)),
        out_shape=(
            jax.ShapeDtypeStruct((depth, most), bf16),
            jax.ShapeDtypeStruct((1, count * rows + PACK, most), bf16),
            jax.ShapeDtypeStruct((1, count, rows, most), f32),
            jax.ShapeDtypeStruct((1, 1, most), f32),
        ),
        in_specs=[SMEM] + [VMEM] * len(operands),
        out_specs=(VMEM,) * 4,
        scratch_shapes=[pltpu.VMEM((most, most), f32)],
        cost_estimate=pl.CostEstimate(flops=2 * depth * most * most, bytes_accessed=2**20, transcendentals=0),
        compiler_params=pltpu.CompilerParams(vmem_limit_bytes=6 * MIB),
        name="gram_split",
    )(ids, *operands)


def refine_body(slot, per_group, ids, sectors_ref, kept_ref, gram_ref, corr_ref, cdiag_ref, out_ref):
    rows, most = out_ref.shape
    first = ids[1] * rows
    rank = kept_ref[sectors_ref[ids[0] * per_group + slot]]
    gram = gram_ref[0, pl.ds(0, rows), :].astype(f32)
    gdiag = unpacked(gram_ref[0, pl.ds(rows, PACK), :])
    cdiag = cdiag_ref[slot]
    lam = gdiag / (cdiag + 1e-06)
    i = first + lax.broadcasted_iota(jnp.int32, (rows, most), 0)
    j = lax.broadcasted_iota(jnp.int32, (rows, most), 1)
    lam_j = jnp.broadcast_to(lam, (rows, most))
    lam_i = jnp.sum(jnp.where(i == j, lam_j, 0.0), axis=1, keepdims=True)
    differ = lam_j - lam_i
    total = damping * (lam_i + lam_j)
    divisor = differ * differ + total * total + 1e-06
    offdiag = (gram - lam_j * corr_ref[slot, 0]) * differ / divisor
    result = jnp.where(i == j, 0.5 * (1.0 - cdiag), offdiag)
    inside = (i < rank) & (j < rank)
    out_ref[...] = jnp.where(inside, result, 0.0).astype(bf16)


def refine(slot, ids, slot_sector, kept, gram, corr, cdiag, per_group):
    _, _, rows, most = corr.shape
    return pl.pallas_call(
        functools.partial(refine_body, slot, per_group),
        out_shape=jax.ShapeDtypeStruct((rows, most), bf16),
        in_specs=[SMEM] * 3 + [VMEM] * 3,
        out_specs=VMEM,
        cost_estimate=pl.CostEstimate(flops=10**6, bytes_accessed=2**19, transcendentals=0),
        compiler_params=pltpu.CompilerParams(vmem_limit_bytes=4 * MIB),
        name="refine",
    )(ids, slot_sector, kept, gram, corr, cdiag)


def final_body(slot, per_group, halves, order, ids, sectors_ref, kept_ref, vectors_ref, left_ref, own_ref, other_ref, *refs):
    right_out, left_out, corr = refs[-3:]
    rows, most = own_ref.shape[0] // len(order), own_ref.shape[1]
    rank = kept_ref[sectors_ref[ids[0] * per_group + slot]]

    def finish(narrow):
        out = narrow.astype(f32) + jnp.dot(narrow, corr[...], preferred_element_type=f32)
        j = lax.broadcasted_iota(jnp.int32, out.shape, 1)
        return jnp.where(j < rank, out, 0.0)

    @pl.when(pl.program_id(0) == 0)
    def _():
        half = ids[1] % halves
        for n, k in enumerate(order):
            at = ((ids[1] // halves) ^ k) * halves
            mine, others = pl.multiple_of((at + half) * rows, rows), pl.multiple_of((at + 1 - half) * rows, rows)
            corr[pl.ds(mine, rows), :] = own_ref[pl.ds(n * rows, rows), :]
            corr[pl.ds(others, rows), :] = other_ref[pl.ds(n * rows, rows), :]
        out = finish(left_ref[...])
        left_out[:, 0] = out.reshape(out.shape[0] // 4, 4, most)

    right_out[0] = finish(vectors_ref[0])


def final(slot, ids, slot_sector, kept, vectors, left, own, other, order, carried, halves):
    per_group, depth, most = vectors.shape
    tile = depth // 2
    rows = left.shape[0] // 4
    whole = lambda shape: pl.BlockSpec(shape, lambda t, *_: (0,) * len(shape))
    right_shape = jax.ShapeDtypeStruct((per_group, depth, most), f32)
    left_shape = jax.ShapeDtypeStruct((rows, per_group, 4, most), f32)
    in_specs = [
        pl.BlockSpec((1, tile, most), lambda t, *_: (slot, t, 0)),
        whole(left.shape),
        whole(own.shape),
        whole(other.shape),
    ]
    operands = [vectors, left, own, other]
    aliases = {}
    if carried is not None:
        aliases = {3 + len(operands): 0, 4 + len(operands): 1}
        in_specs += [pl.BlockSpec(memory_space=pl.ANY)] * 2
        operands += list(carried)
    return pl.pallas_call(
        functools.partial(final_body, slot, per_group, halves, order),
        out_shape=(right_shape, left_shape),
        grid_spec=pltpu.PrefetchScalarGridSpec(
            num_scalar_prefetch=3,
            grid=(depth // tile,),
            in_specs=in_specs,
            out_specs=(
                pl.BlockSpec((1, tile, most), lambda t, *_: (slot, t, 0)),
                pl.BlockSpec((rows, 1, 4, most), lambda t, *_: (0, slot, 0, 0)),
            ),
            scratch_shapes=[pltpu.VMEM((most, most), bf16)],
        ),
        input_output_aliases=aliases,
        cost_estimate=pl.CostEstimate(flops=2 * 1216 * most * most, bytes_accessed=4 * 2**20, transcendentals=0),
        compiler_params=pltpu.CompilerParams(vmem_limit_bytes=12 * MIB),
        name="final",
    )(ids, slot_sector, kept, *operands)


def halve_body(shift, halves, first, ids, stays_in, taken_in, *refs):
    other, (sent_ref, stays_ref) = refs[:-2], refs[-2:]
    most = stays_ref.shape[3]
    want = (((ids[1] // halves) ^ ids[0]) >> shift) & 1
    for s in range(stays_ref.shape[0]):
        for n in range(stays_ref.shape[1]):
            if other:
                part = pl.ds(first, most)
                low = stays_in[0, 0, :, part] + taken_in[0, 0, :, part].astype(f32)
                high = other[0][0, 0] + other[1][0, 0].astype(f32)
                stays_ref[s, n] = jnp.where(want == 1, high, low)
                sent_ref[s, n] = jnp.where(want == 1, low, high).astype(bf16)
            else:
                at = 2 * n + want
                stays_ref[s, n] = stays_in[s, at] + taken_in[s, at].astype(f32)
                at = 2 * n + 1 - want
                sent_ref[s, n] = (stays_in[s, at] + taken_in[s, at].astype(f32)).astype(bf16)


def halve(ids, shift, halves, value, other=None, first=0):
    slots, count, rows, most = (other or value)[0].shape
    shape = (1, 1, rows, most) if other else (slots, count // 2, rows, most)
    operands = list(value) + list(other or ())
    return pl.pallas_call(
        functools.partial(halve_body, shift, halves, first),
        out_shape=(jax.ShapeDtypeStruct(shape, bf16), jax.ShapeDtypeStruct(shape, f32)),
        in_specs=[SMEM] + [VMEM] * len(operands),
        out_specs=(VMEM,) * 2,
        cost_estimate=pl.CostEstimate(flops=10**6, bytes_accessed=2**20, transcendentals=0),
        compiler_params=pltpu.CompilerParams(vmem_limit_bytes=8 * MIB),
    )(ids, *operands)


def work(theta, gate, warm_start, slot_sector, kept, block_offsets):
    groups, cols = lax.axis_size("row"), lax.axis_size("col")
    block, col = lax.axis_index("row"), lax.axis_index("col")
    halves = cols // groups
    per_group, _, bond_cols, most = warm_start.shape
    group_bits = groups.bit_length() - 1
    ids = jnp.stack([block, col]).astype(jnp.int32)
    vectors = warm_start.reshape(per_group, 4 * bond_cols, most)
    gate_matrix = gate.reshape(CHUNK, CHUNK)

    parts = [1] * (per_group - 1) + [2]

    across = {}
    remaining = vectors
    for s in range(per_group):
        width = most // parts[s]
        for p in range(parts[s]):
            own = remaining[s : s + 1, :, p * width : (p + 1) * width]
            own, remaining = lax.optimization_barrier((own, remaining))
            across[s, p] = {d: swap(own, "row", d) for d in range(2, groups, 2)}
    partner = swap(vectors, "row", 1)

    def place(b, g, h):
        return b * cols + g * halves + h

    def turned(value):
        pairs = [
            (place(b, g, h), place(g, b, h))
            for b in range(groups)
            for g in range(groups)
            for h in range(halves)
        ]
        return lax.ppermute(value, ("row", "col"), pairs)

    corr = jnp.einsum("snk,snl->skl", vectors, vectors, preferred_element_type=f32)
    corr = corr.reshape(per_group, groups, most // groups, most)
    sent, stays, diag = corr_split(ids, corr, halves)
    for t in range(group_bits):
        taken = swap(sent, "col", halves << t)
        which = ("group", t + 1) if t + 1 < group_bits else ("half", 0)
        sent, stays, diag = step(ids, stays, taken, diag, which, halves)
    taken = swap(sent, "col", 1)
    _, corr, cdiag = step(ids, stays, taken, diag, None, halves)

    def reduced(sent, stays):
        taken = swap(sent, "col", 1)
        for t in range(group_bits - 1):
            sent, stays = halve(ids, t, halves, (stays, taken))
            taken = swap(sent, "col", halves << t)
        return stays, taken

    gated = gate_rows(ids, slot_sector, block_offsets, theta, gate_matrix, groups, halves, per_group)
    near = []
    for s in range(per_group):
        operands = [vectors, partner]
        for d in range(2, groups // 2, 2):
            arrived = jnp.concatenate([across[s, p][d] for p in range(parts[s])], axis=2)
            operands += [arrived, swap(arrived, "row", 1)]
        value = product(s, 0, gated, operands)
        near.append(reduced(*value))
    last = group_bits - 1
    carried = None
    for s in range(per_group):
        values = []
        for p in range(parts[s]):
            far = []
            for d in range(groups // 2, groups, 2):
                far += [across[s, p][d], swap(across[s, p][d], "row", 1)]
            far = product(s, 1, gated, far)
            far = reduced(*far)
            sent, stays = halve(ids, last, halves, near[s], far, p * (most // parts[s]))
            values.append((stays, swap(sent, "col", halves << last)))
        projected, sent, stays, diag = gram_split(ids, values, groups)
        left = turned(projected)
        for t in range(1, group_bits + 1):
            taken = swap(sent, "row", 1 << (t - 1))
            which = ("row", t) if t < group_bits else ("half", 0)
            sent, stays, diag = step(ids, stays, taken, diag, which, halves)
        taken = swap(sent, "col", 1)
        sent, _, _ = step(ids, stays, taken, diag, None, halves)
        gram = turned(sent)
        piece = refine(s, ids, slot_sector, kept, gram, corr, cdiag, per_group)
        order = list(range(groups))
        pieces = [piece]
        for k in order[1:]:
            pieces.append(swap(piece, "col", halves * k))
        own = jnp.concatenate(pieces)
        other = swap(own, "col", 1)
        carried = final(s, ids, slot_sector, kept, vectors, left, own, other, order, carried, halves)
    right, left = carried
    return left, right.reshape(warm_start.shape)


def solution(mesh):
    in_specs = (P("row", None, None, "col"), P(), P("row", None, "col", None), P(), P(), P())
    out_specs = (P("col", "row", None, None), P("row", None, "col", None))
    return jax.shard_map(work, mesh=mesh, in_specs=in_specs, out_specs=out_specs, check_vma=False)
```

```python
import functools

import jax
import jax.numpy as jnp
from jax import lax
from jax.experimental import pallas as pl
from jax.experimental.pallas import tpu as pltpu
from jax.sharding import PartitionSpec as P


NMAX = 96
CHUNK = 16
MIB = 2**20
damping = 0.25


VMEM = pl.BlockSpec(memory_space=pltpu.VMEM)
SMEM = pl.BlockSpec(memory_space=pltpu.SMEM)
f32, bf16 = jnp.float32, jnp.bfloat16


def swap(value, axis, mask):
    count = lax.axis_size(axis)
    return lax.ppermute(value, axis, [(i, i ^ mask) for i in range(count)])


def window(ids, sectors_ref, offsets_ref, block_rows, far, slot, half, rows, per_group):
    block = ids[0]
    sector = sectors_ref[(far ^ block) * per_group + slot]
    number = offsets_ref.shape[1]
    start = offsets_ref[block, sector]
    following = offsets_ref[block, jnp.minimum(sector + 1, number - 1)]
    end = jnp.where(sector + 1 < number, following, block_rows)
    start = start + half * rows
    return start, jnp.clip(end - start, 0, rows)


def prepare(theta_hbm, gate_ref, theta, mixer, sem):
    block_rows = theta_hbm.shape[0]
    size = CHUNK * CHUNK
    copy = pltpu.make_async_copy(theta_hbm, theta.at[pl.ds(0, block_rows)], sem)
    copy.start()
    theta[pl.ds(block_rows, NMAX)] = jnp.zeros((NMAX,) + theta.shape[1:], theta.dtype)
    tall_row = lax.broadcasted_iota(jnp.int32, (size, CHUNK), 0)
    tall_col = lax.broadcasted_iota(jnp.int32, (size, CHUNK), 1)
    wide_row = lax.broadcasted_iota(jnp.int32, (CHUNK, size), 0)
    wide_col = lax.broadcasted_iota(jnp.int32, (CHUNK, size), 1)
    spread = ((tall_row % 4) * 4 + tall_row // (4 * CHUNK) == tall_col).astype(bf16)
    repeat = (wide_col % CHUNK == wide_row).astype(bf16)
    tall = jnp.dot(spread, gate_ref[...], preferred_element_type=f32).astype(bf16)
    full = jnp.dot(tall, repeat, preferred_element_type=f32)
    row = lax.broadcasted_iota(jnp.int32, (size, size), 0)
    col = lax.broadcasted_iota(jnp.int32, (size, size), 1)
    mixer[...] = jnp.where((row // 4) % CHUNK == col // CHUNK, full, 0.0).astype(bf16)
    copy.wait()


def gated_window(theta, mixer, start, live, rows, store):
    size = CHUNK * CHUNK
    cols = theta.shape[3]
    for part in range(rows // CHUNK):
        first = jnp.clip(start + part * CHUNK, 0, theta.shape[0] - CHUNK)
        piece = theta[pl.ds(first, CHUNK)].reshape(size, cols)
        mixed = jnp.dot(mixer[...], piece, preferred_element_type=f32)
        place = part * CHUNK + lax.broadcasted_iota(jnp.int32, (4 * CHUNK, cols), 0) // 4
        for b in range(4):
            value = mixed[b * 4 * CHUNK : (b + 1) * 4 * CHUNK, :]
            value = jnp.where(place < live, value, 0.0).astype(bf16)
            store(pl.ds(part * 4 * CHUNK, 4 * CHUNK), pl.ds(b * cols, cols), value)


def theta_scratch(theta):
    return [
        pltpu.VMEM((theta.shape[0] + NMAX,) + theta.shape[1:], bf16),
        pltpu.VMEM((CHUNK * CHUNK, CHUNK * CHUNK), bf16),
        pltpu.SemaphoreType.DMA,
    ]


def gate_body(halves, per_group, ids, sectors_ref, offsets_ref, theta_hbm, gate_ref, out_ref, theta, mixer, sem):
    slot, n = pl.program_id(0), pl.program_id(1)
    rows = NMAX // halves

    @pl.when((slot == 0) & (n == 0))
    def _():
        prepare(theta_hbm, gate_ref, theta, mixer, sem)

    for far_half in (0, 1):
        half = (ids[1] % halves) ^ (1 - far_half)
        start, live = window(
            ids, sectors_ref, offsets_ref, theta_hbm.shape[0], n, slot, half, rows, per_group
        )

        def store(at, cols, value, base=far_half * 4 * rows):
            out_ref[0, 0, pl.ds(base + at.start, at.size), cols] = value

        gated_window(theta, mixer, start, live, rows, store)


def gate_rows(ids, slot_sector, block_offsets, theta, gate, count, halves, per_group):
    rows, cols = NMAX // halves, theta.shape[3]
    block = (1, 1, halves * 4 * rows, 4 * cols)
    return pl.pallas_call(
        functools.partial(gate_body, halves, per_group),
        out_shape=jax.ShapeDtypeStruct((per_group, count) + block[2:], bf16),
        grid_spec=pltpu.PrefetchScalarGridSpec(
            num_scalar_prefetch=3,
            grid=(per_group, count),
            in_specs=[
                pl.BlockSpec(memory_space=pltpu.HBM),
                pl.BlockSpec((CHUNK, CHUNK), lambda s, n, *_: (0, 0)),
            ],
            out_specs=pl.BlockSpec(block, lambda s, n, *_: (s, n, 0, 0)),
            scratch_shapes=theta_scratch(theta),
        ),
        cost_estimate=pl.CostEstimate(flops=6 * 10**9, bytes_accessed=12 * 2**20, transcendentals=0),
        compiler_params=pltpu.CompilerParams(vmem_limit_bytes=14 * MIB),
        name="gate_rows",
    )(ids, slot_sector, block_offsets, theta, gate)


def product_body(count, lhs_ref, *refs):
    vector_refs = refs[:count]
    sent_ref, kept_ref = refs[count:]
    rows = sent_ref.shape[2]
    for n in range(count):
        out = jnp.dot(lhs_ref[0, n], vector_refs[n][0], preferred_element_type=f32)
        sent_ref[0, n] = out[:rows].astype(bf16)
        kept_ref[0, n] = out[rows:]


def product(slot, chunk, gated, vectors):
    _, _, rows, depth = gated.shape
    count = len(vectors)
    most = vectors[0].shape[2]
    out_block = (1, count, rows // 2, most)
    return pl.pallas_call(
        functools.partial(product_body, count),
        out_shape=(jax.ShapeDtypeStruct(out_block, bf16), jax.ShapeDtypeStruct(out_block, f32)),
        grid=(1,),
        in_specs=[pl.BlockSpec((1, count, rows, depth), lambda i: (slot, chunk, 0, 0))]
        + [pl.BlockSpec((1, depth, most), lambda i, at=min(slot, v.shape[0] - 1): (at, 0, 0)) for v in vectors],
        out_specs=(pl.BlockSpec(out_block, lambda i: (0, 0, 0, 0)),) * 2,
        cost_estimate=pl.CostEstimate(flops=8 * 10**8, bytes_accessed=5 * 2**20, transcendentals=0),
        compiler_params=pltpu.CompilerParams(vmem_limit_bytes=16 * MIB),
    )(gated, *vectors)


PACK = 16


def packed(diag):
    high = diag.astype(bf16)
    rest = diag - high.astype(f32)
    middle = rest.astype(bf16)
    low = (rest - middle.astype(f32)).astype(bf16)
    row = lax.broadcasted_iota(jnp.int32, (PACK, diag.shape[1]), 0)
    wide = [jnp.broadcast_to(x.astype(f32), row.shape) for x in (high, middle, low)]
    return jnp.where(row == 0, wide[0], jnp.where(row == 1, wide[1], jnp.where(row == 2, wide[2], 0.0))).astype(bf16)


def unpacked(block):
    return jnp.sum(block.astype(f32), axis=0, keepdims=True)


def bit_of(ids, which, halves):
    source, shift = which
    value = {"row": ids[0], "group": ids[1] // halves, "half": ids[1] % halves}[source]
    return (value >> shift) & 1


def corr_body(halves, ids, corr_ref, sent_ref, stays_ref, diag_ref):
    slots, count, rows, most = stays_ref.shape
    mine = bit_of(ids, ("group", 0), halves)
    for s in range(slots):
        diag = jnp.zeros((1, most), f32)
        for n in range(2 * count):
            i = n * rows + lax.broadcasted_iota(jnp.int32, (rows, most), 0)
            j = lax.broadcasted_iota(jnp.int32, (rows, most), 1)
            diag = diag + jnp.sum(jnp.where(i == j, corr_ref[s, n], 0.0), axis=0, keepdims=True)
        diag_ref[s] = diag
        for n in range(count):
            stays_ref[s, n] = corr_ref[s, 2 * n + mine]
            sent_ref[s, pl.ds(n * rows, rows), :] = corr_ref[s, 2 * n + 1 - mine].astype(bf16)
        sent_ref[s, pl.ds(count * rows, PACK), :] = packed(diag)


def corr_split(ids, corr, halves):
    slots, count, rows, most = corr.shape
    count = count // 2
    return pl.pallas_call(
        functools.partial(corr_body, halves),
        out_shape=(
            jax.ShapeDtypeStruct((slots, count * rows + PACK, most), bf16),
            jax.ShapeDtypeStruct((slots, count, rows, most), f32),
            jax.ShapeDtypeStruct((slots, 1, most), f32),
        ),
        in_specs=[SMEM, VMEM],
        out_specs=(VMEM,) * 3,
        cost_estimate=pl.CostEstimate(flops=10**6, bytes_accessed=2**21, transcendentals=0),
        compiler_params=pltpu.CompilerParams(vmem_limit_bytes=8 * MIB),
        name="corr_split",
    )(ids, corr)


def step_body(which, halves, ids, stays_in, taken_ref, diag_in, sent_ref, stays_ref, diag_ref):
    slots, count, rows, _ = stays_ref.shape
    before, block = stays_in.shape[1:3]
    mine = bit_of(ids, which, halves) if which else 0
    for s in range(slots):
        diag = diag_in[s] + unpacked(taken_ref[s, pl.ds(before * block, PACK), :])
        diag_ref[s] = diag

        def total(at, first=0):
            there = pl.multiple_of(at * block + first, rows)
            return stays_in[s, at, pl.ds(first, rows), :] + taken_ref[s, pl.ds(there, rows), :].astype(f32)

        for n in range(count):
            if not which:
                value = total(n)
                stays_ref[s, n] = value
            elif block != rows:
                stays_ref[s, n] = total(n, pl.multiple_of(mine * rows, rows))
                value = total(n, pl.multiple_of((1 - mine) * rows, rows))
            else:
                stays_ref[s, n] = total(2 * n + mine)
                value = total(2 * n + 1 - mine)
            sent_ref[s, pl.ds(n * rows, rows), :] = value.astype(bf16)
        sent_ref[s, pl.ds(count * rows, PACK), :] = packed(diag)


def step(ids, stays, taken, diag, which, halves):
    slots, count, rows, most = stays.shape
    if which and which[0] == "half":
        rows = rows // halves
    elif which:
        count = count // 2
    return pl.pallas_call(
        functools.partial(step_body, which, halves),
        out_shape=(
            jax.ShapeDtypeStruct((slots, count * rows + PACK, most), bf16),
            jax.ShapeDtypeStruct((slots, count, rows, most), f32),
            jax.ShapeDtypeStruct((slots, 1, most), f32),
        ),
        in_specs=[SMEM] + [VMEM] * 3,
        out_specs=(VMEM,) * 3,
        cost_estimate=pl.CostEstimate(flops=10**6, bytes_accessed=2**19, transcendentals=0),
        compiler_params=pltpu.CompilerParams(vmem_limit_bytes=8 * MIB),
    )(ids, stays, taken, diag)


def total_body(message, stays_in, taken_ref, diag_in, *refs):
    slots, _, rows, _ = stays_in.shape
    for s in range(slots):
        diag = diag_in[s] + unpacked(taken_ref[s, pl.ds(rows, PACK), :])
        value = stays_in[s, 0] + taken_ref[s, pl.ds(0, rows), :].astype(f32)
        if message:
            refs[0][s, pl.ds(0, rows), :] = value.astype(bf16)
            refs[0][s, pl.ds(rows, PACK), :] = packed(diag)
        else:
            refs[0][s, 0] = value
            refs[1][s] = diag


def total(stays, taken, diag, message):
    shapes = (
        (jax.ShapeDtypeStruct(taken.shape, bf16),)
        if message
        else (jax.ShapeDtypeStruct(stays.shape, f32), jax.ShapeDtypeStruct(diag.shape, f32))
    )
    return pl.pallas_call(
        functools.partial(total_body, message),
        out_shape=shapes,
        in_specs=[VMEM] * 3,
        out_specs=(VMEM,) * len(shapes),
        cost_estimate=pl.CostEstimate(flops=10**6, bytes_accessed=2**19, transcendentals=0),
        compiler_params=pltpu.CompilerParams(vmem_limit_bytes=4 * MIB),
    )(stays, taken, diag)


def pick_body(parts, vectors_ref, *refs):
    at = 0
    for s, count in enumerate(parts):
        width = vectors_ref.shape[2] // count
        for p in range(count):
            refs[at][0] = vectors_ref[s, :, p * width : (p + 1) * width]
            at += 1


def pick(vectors, parts):
    _, depth, most = vectors.shape
    shapes = [jax.ShapeDtypeStruct((1, depth, most // n), bf16) for n in parts for _ in range(n)]
    return pl.pallas_call(
        functools.partial(pick_body, parts),
        out_shape=tuple(shapes),
        in_specs=[VMEM],
        out_specs=(VMEM,) * len(shapes),
        cost_estimate=pl.CostEstimate(flops=0, bytes_accessed=2**23, transcendentals=0),
        compiler_params=pltpu.CompilerParams(vmem_limit_bytes=8 * MIB),
        name="pick",
    )(vectors)


def gram_body(parts, ids, *refs):
    projected_ref, sent_ref, stays_ref, diag_ref, gram = refs[2 * parts :]
    _, count, rows, most = stays_ref.shape
    width = most // parts
    for n in range(parts):
        part = (refs[2 * n][0, 0] + refs[2 * n + 1][0, 0].astype(f32)).astype(bf16)
        projected_ref[:, n * width : (n + 1) * width] = part
    projected = projected_ref[...]
    gram[...] = lax.dot_general(projected, projected, (((0,), (0,)), ((), ())), preferred_element_type=f32)
    wide = projected.astype(f32)
    diag = jnp.sum(wide * wide, axis=0, keepdims=True)
    diag_ref[0] = diag
    mine = ids[0] & 1
    for n in range(count):
        stays_ref[0, n] = gram[pl.ds(pl.multiple_of((2 * n + mine) * rows, rows), rows), :]
        other = gram[pl.ds(pl.multiple_of((2 * n + 1 - mine) * rows, rows), rows), :]
        sent_ref[0, pl.ds(n * rows, rows), :] = other.astype(bf16)
    sent_ref[0, pl.ds(count * rows, PACK), :] = packed(diag)


def gram_split(ids, values, groups):
    depth, most = values[0][0].shape[2:]
    most = most * len(values)
    rows, count = most // groups, groups // 2
    operands = [x for value in values for x in value]
    return pl.pallas_call(
        functools.partial(gram_body, len(values)),
        out_shape=(
            jax.ShapeDtypeStruct((depth, most), bf16),
            jax.ShapeDtypeStruct((1, count * rows + PACK, most), bf16),
            jax.ShapeDtypeStruct((1, count, rows, most), f32),
            jax.ShapeDtypeStruct((1, 1, most), f32),
        ),
        in_specs=[SMEM] + [VMEM] * len(operands),
        out_specs=(VMEM,) * 4,
        scratch_shapes=[pltpu.VMEM((most, most), f32)],
        cost_estimate=pl.CostEstimate(flops=2 * depth * most * most, bytes_accessed=2**20, transcendentals=0),
        compiler_params=pltpu.CompilerParams(vmem_limit_bytes=6 * MIB),
        name="gram_split",
    )(ids, *operands)


def refine_body(slot, per_group, ids, sectors_ref, kept_ref, gram_ref, corr_ref, cdiag_ref, out_ref):
    rows, most = out_ref.shape
    first = ids[1] * rows
    rank = kept_ref[sectors_ref[ids[0] * per_group + slot]]
    gram = gram_ref[0, pl.ds(0, rows), :].astype(f32)
    gdiag = unpacked(gram_ref[0, pl.ds(rows, PACK), :])
    cdiag = cdiag_ref[slot]
    lam = gdiag / (cdiag + 1e-06)
    i = first + lax.broadcasted_iota(jnp.int32, (rows, most), 0)
    j = lax.broadcasted_iota(jnp.int32, (rows, most), 1)
    lam_j = jnp.broadcast_to(lam, (rows, most))
    lam_i = jnp.sum(jnp.where(i == j, lam_j, 0.0), axis=1, keepdims=True)
    differ = lam_j - lam_i
    total = damping * (lam_i + lam_j)
    divisor = differ * differ + total * total + 1e-06
    offdiag = (gram - lam_j * corr_ref[slot, 0]) * differ / divisor
    result = jnp.where(i == j, 0.5 * (1.0 - cdiag), offdiag)
    inside = (i < rank) & (j < rank)
    out_ref[...] = jnp.where(inside, result, 0.0).astype(bf16)


def refine(slot, ids, slot_sector, kept, gram, corr, cdiag, per_group):
    _, _, rows, most = corr.shape
    return pl.pallas_call(
        functools.partial(refine_body, slot, per_group),
        out_shape=jax.ShapeDtypeStruct((rows, most), bf16),
        in_specs=[SMEM] * 3 + [VMEM] * 3,
        out_specs=VMEM,
        cost_estimate=pl.CostEstimate(flops=10**6, bytes_accessed=2**19, transcendentals=0),
        compiler_params=pltpu.CompilerParams(vmem_limit_bytes=4 * MIB),
        name="refine",
    )(ids, slot_sector, kept, gram, corr, cdiag)


def final_body(slot, per_group, halves, order, ids, sectors_ref, kept_ref, vectors_ref, left_ref, own_ref, other_ref, *refs):
    right_out, left_out, corr = refs[-3:]
    rows, most = own_ref.shape[0] // len(order), own_ref.shape[1]
    rank = kept_ref[sectors_ref[ids[0] * per_group + slot]]

    def finish(narrow):
        out = narrow.astype(f32) + jnp.dot(narrow, corr[...], preferred_element_type=f32)
        j = lax.broadcasted_iota(jnp.int32, out.shape, 1)
        return jnp.where(j < rank, out, 0.0)

    @pl.when(pl.program_id(0) == 0)
    def _():
        half = ids[1] % halves
        for n, k in enumerate(order):
            at = ((ids[1] // halves) ^ k) * halves
            mine, others = pl.multiple_of((at + half) * rows, rows), pl.multiple_of((at + 1 - half) * rows, rows)
            corr[pl.ds(mine, rows), :] = own_ref[pl.ds(n * rows, rows), :]
            corr[pl.ds(others, rows), :] = other_ref[pl.ds(n * rows, rows), :]
        out = finish(left_ref[...])
        left_out[:, 0] = out.reshape(out.shape[0] // 4, 4, most)

    right_out[0] = finish(vectors_ref[0])


def final(slot, ids, slot_sector, kept, vectors, left, own, other, order, carried, halves):
    per_group, depth, most = vectors.shape
    tile = depth // 2
    rows = left.shape[0] // 4
    whole = lambda shape: pl.BlockSpec(shape, lambda t, *_: (0,) * len(shape))
    right_shape = jax.ShapeDtypeStruct((per_group, depth, most), f32)
    left_shape = jax.ShapeDtypeStruct((rows, per_group, 4, most), f32)
    in_specs = [
        pl.BlockSpec((1, tile, most), lambda t, *_: (slot, t, 0)),
        whole(left.shape),
        whole(own.shape),
        whole(other.shape),
    ]
    operands = [vectors, left, own, other]
    aliases = {}
    if carried is not None:
        aliases = {3 + len(operands): 0, 4 + len(operands): 1}
        in_specs += [pl.BlockSpec(memory_space=pl.ANY)] * 2
        operands += list(carried)
    return pl.pallas_call(
        functools.partial(final_body, slot, per_group, halves, order),
        out_shape=(right_shape, left_shape),
        grid_spec=pltpu.PrefetchScalarGridSpec(
            num_scalar_prefetch=3,
            grid=(depth // tile,),
            in_specs=in_specs,
            out_specs=(
                pl.BlockSpec((1, tile, most), lambda t, *_: (slot, t, 0)),
                pl.BlockSpec((rows, 1, 4, most), lambda t, *_: (0, slot, 0, 0)),
            ),
            scratch_shapes=[pltpu.VMEM((most, most), bf16)],
        ),
        input_output_aliases=aliases,
        cost_estimate=pl.CostEstimate(flops=2 * 1216 * most * most, bytes_accessed=4 * 2**20, transcendentals=0),
        compiler_params=pltpu.CompilerParams(vmem_limit_bytes=12 * MIB),
        name="final",
    )(ids, slot_sector, kept, *operands)


def halve_body(shift, halves, first, ids, stays_in, taken_in, *refs):
    other, (sent_ref, stays_ref) = refs[:-2], refs[-2:]
    most = stays_ref.shape[3]
    want = (((ids[1] // halves) ^ ids[0]) >> shift) & 1
    for s in range(stays_ref.shape[0]):
        for n in range(stays_ref.shape[1]):
            if other:
                part = pl.ds(first, most)
                low = stays_in[0, 0, :, part] + taken_in[0, 0, :, part].astype(f32)
                high = other[0][0, 0] + other[1][0, 0].astype(f32)
                stays_ref[s, n] = jnp.where(want == 1, high, low)
                sent_ref[s, n] = jnp.where(want == 1, low, high).astype(bf16)
            else:
                at = 2 * n + want
                stays_ref[s, n] = stays_in[s, at] + taken_in[s, at].astype(f32)
                at = 2 * n + 1 - want
                sent_ref[s, n] = (stays_in[s, at] + taken_in[s, at].astype(f32)).astype(bf16)


def halve(ids, shift, halves, value, other=None, first=0):
    slots, count, rows, most = (other or value)[0].shape
    shape = (1, 1, rows, most) if other else (slots, count // 2, rows, most)
    operands = list(value) + list(other or ())
    return pl.pallas_call(
        functools.partial(halve_body, shift, halves, first),
        out_shape=(jax.ShapeDtypeStruct(shape, bf16), jax.ShapeDtypeStruct(shape, f32)),
        in_specs=[SMEM] + [VMEM] * len(operands),
        out_specs=(VMEM,) * 2,
        cost_estimate=pl.CostEstimate(flops=10**6, bytes_accessed=2**20, transcendentals=0),
        compiler_params=pltpu.CompilerParams(vmem_limit_bytes=8 * MIB),
    )(ids, *operands)


def work(theta, gate, warm_start, slot_sector, kept, block_offsets):
    groups, cols = lax.axis_size("row"), lax.axis_size("col")
    block, col = lax.axis_index("row"), lax.axis_index("col")
    halves = cols // groups
    per_group, _, bond_cols, most = warm_start.shape
    group_bits = groups.bit_length() - 1
    ids = jnp.stack([block, col]).astype(jnp.int32)
    vectors = warm_start.reshape(per_group, 4 * bond_cols, most)
    gate_matrix = gate.reshape(CHUNK, CHUNK)

    parts = [1] * (per_group - 1) + [2]

    across = {}
    picked = iter(pick(vectors, parts))
    for s in range(per_group):
        for p in range(parts[s]):
            own = next(picked)
            across[s, p] = {d: swap(own, "row", d) for d in range(2, groups, 2)}
    partner = swap(vectors, "row", 1)

    def place(b, g, h):
        return b * cols + g * halves + h

    def turned(value):
        pairs = [
            (place(b, g, h), place(g, b, h))
            for b in range(groups)
            for g in range(groups)
            for h in range(halves)
        ]
        return lax.ppermute(value, ("row", "col"), pairs)

    corr = jnp.einsum("snk,snl->skl", vectors, vectors, preferred_element_type=f32)
    corr = corr.reshape(per_group, groups, most // groups, most)
    sent, stays, diag = corr_split(ids, corr, halves)
    for t in range(group_bits):
        taken = swap(sent, "col", halves << t)
        which = ("group", t + 1) if t + 1 < group_bits else ("half", 0)
        sent, stays, diag = step(ids, stays, taken, diag, which, halves)
    taken = swap(sent, "col", 1)
    corr, cdiag = total(stays, taken, diag, False)

    def reduced(sent, stays):
        taken = swap(sent, "col", 1)
        for t in range(group_bits - 1):
            sent, stays = halve(ids, t, halves, (stays, taken))
            taken = swap(sent, "col", halves << t)
        return stays, taken

    gated = gate_rows(ids, slot_sector, block_offsets, theta, gate_matrix, groups, halves, per_group)
    near = []
    for s in range(per_group):
        operands = [vectors, partner]
        for d in range(2, groups // 2, 2):
            arrived = jnp.concatenate([across[s, p][d] for p in range(parts[s])], axis=2)
            operands += [arrived, swap(arrived, "row", 1)]
        value = product(s, 0, gated, operands)
        near.append(reduced(*value))
    last = group_bits - 1
    carried = None
    for s in range(per_group):
        values = []
        for p in range(parts[s]):
            far = []
            for d in range(groups // 2, groups, 2):
                far += [across[s, p][d], swap(across[s, p][d], "row", 1)]
            far = product(s, 1, gated, far)
            far = reduced(*far)
            sent, stays = halve(ids, last, halves, near[s], far, p * (most // parts[s]))
            values.append((stays, swap(sent, "col", halves << last)))
        projected, sent, stays, diag = gram_split(ids, values, groups)
        left = turned(projected)
        for t in range(1, group_bits + 1):
            taken = swap(sent, "row", 1 << (t - 1))
            which = ("row", t) if t < group_bits else ("half", 0)
            sent, stays, diag = step(ids, stays, taken, diag, which, halves)
        taken = swap(sent, "col", 1)
        (sent,) = total(stays, taken, diag, True)
        gram = turned(sent)
        piece = refine(s, ids, slot_sector, kept, gram, corr, cdiag, per_group)
        order = list(range(groups))
        pieces = [piece]
        for k in order[1:]:
            pieces.append(swap(piece, "col", halves * k))
        own = jnp.concatenate(pieces)
        other = swap(own, "col", 1)
        carried = final(s, ids, slot_sector, kept, vectors, left, own, other, order, carried, halves)
    right, left = carried
    return left, right.reshape(warm_start.shape)


def solution(mesh):
    in_specs = (P("row", None, None, "col"), P(), P("row", None, "col", None), P(), P(), P())
    out_specs = (P("col", "row", None, None), P("row", None, "col", None))
    return jax.shard_map(work, mesh=mesh, in_specs=in_specs, out_specs=out_specs, check_vma=False)
```

```python
import functools

import jax
import jax.numpy as jnp
from jax import lax
from jax.experimental import pallas as pl
from jax.experimental.pallas import tpu as pltpu
from jax.sharding import PartitionSpec as P


NMAX = 96
CHUNK = 16
MIB = 2**20
damping = 0.25


VMEM = pl.BlockSpec(memory_space=pltpu.VMEM)
SMEM = pl.BlockSpec(memory_space=pltpu.SMEM)
f32, bf16 = jnp.float32, jnp.bfloat16


def swap(value, axis, mask):
    count = lax.axis_size(axis)
    return lax.ppermute(value, axis, [(i, i ^ mask) for i in range(count)])


def window(ids, sectors_ref, offsets_ref, block_rows, far, slot, half, rows, per_group):
    block = ids[0]
    sector = sectors_ref[(far ^ block) * per_group + slot]
    number = offsets_ref.shape[1]
    start = offsets_ref[block, sector]
    following = offsets_ref[block, jnp.minimum(sector + 1, number - 1)]
    end = jnp.where(sector + 1 < number, following, block_rows)
    start = start + half * rows
    return start, jnp.clip(end - start, 0, rows)


def prepare(theta_hbm, gate_ref, theta, mixer, sem):
    block_rows = theta_hbm.shape[0]
    size = CHUNK * CHUNK
    copy = pltpu.make_async_copy(theta_hbm, theta.at[pl.ds(0, block_rows)], sem)
    copy.start()
    theta[pl.ds(block_rows, NMAX)] = jnp.zeros((NMAX,) + theta.shape[1:], theta.dtype)
    tall_row = lax.broadcasted_iota(jnp.int32, (size, CHUNK), 0)
    tall_col = lax.broadcasted_iota(jnp.int32, (size, CHUNK), 1)
    wide_row = lax.broadcasted_iota(jnp.int32, (CHUNK, size), 0)
    wide_col = lax.broadcasted_iota(jnp.int32, (CHUNK, size), 1)
    spread = ((tall_row % 4) * 4 + tall_row // (4 * CHUNK) == tall_col).astype(bf16)
    repeat = (wide_col % CHUNK == wide_row).astype(bf16)
    tall = jnp.dot(spread, gate_ref[...], preferred_element_type=f32).astype(bf16)
    full = jnp.dot(tall, repeat, preferred_element_type=f32)
    row = lax.broadcasted_iota(jnp.int32, (size, size), 0)
    col = lax.broadcasted_iota(jnp.int32, (size, size), 1)
    mixer[...] = jnp.where((row // 4) % CHUNK == col // CHUNK, full, 0.0).astype(bf16)
    copy.wait()


def gated_window(theta, mixer, start, live, rows, store):
    size = CHUNK * CHUNK
    cols = theta.shape[3]
    for part in range(rows // CHUNK):
        first = jnp.clip(start + part * CHUNK, 0, theta.shape[0] - CHUNK)
        piece = theta[pl.ds(first, CHUNK)].reshape(size, cols)
        mixed = jnp.dot(mixer[...], piece, preferred_element_type=f32)
        place = part * CHUNK + lax.broadcasted_iota(jnp.int32, (4 * CHUNK, cols), 0) // 4
        for b in range(4):
            value = mixed[b * 4 * CHUNK : (b + 1) * 4 * CHUNK, :]
            value = jnp.where(place < live, value, 0.0).astype(bf16)
            store(pl.ds(part * 4 * CHUNK, 4 * CHUNK), pl.ds(b * cols, cols), value)


def theta_scratch(theta):
    return [
        pltpu.VMEM((theta.shape[0] + NMAX,) + theta.shape[1:], bf16),
        pltpu.VMEM((CHUNK * CHUNK, CHUNK * CHUNK), bf16),
        pltpu.SemaphoreType.DMA,
    ]


def gate_body(halves, per_group, ids, sectors_ref, offsets_ref, theta_hbm, gate_ref, out_ref, theta, mixer, sem):
    slot, n = pl.program_id(0), pl.program_id(1)
    rows = NMAX // halves

    @pl.when((slot == 0) & (n == 0))
    def _():
        prepare(theta_hbm, gate_ref, theta, mixer, sem)

    for far_half in (0, 1):
        half = (ids[1] % halves) ^ (1 - far_half)
        start, live = window(
            ids, sectors_ref, offsets_ref, theta_hbm.shape[0], n, slot, half, rows, per_group
        )

        def store(at, cols, value, base=far_half * 4 * rows):
            out_ref[0, 0, pl.ds(base + at.start, at.size), cols] = value

        gated_window(theta, mixer, start, live, rows, store)


def gate_rows(ids, slot_sector, block_offsets, theta, gate, count, halves, per_group):
    rows, cols = NMAX // halves, theta.shape[3]
    block = (1, 1, halves * 4 * rows, 4 * cols)
    return pl.pallas_call(
        functools.partial(gate_body, halves, per_group),
        out_shape=jax.ShapeDtypeStruct((per_group, count) + block[2:], bf16),
        grid_spec=pltpu.PrefetchScalarGridSpec(
            num_scalar_prefetch=3,
            grid=(per_group, count),
            in_specs=[
                pl.BlockSpec(memory_space=pltpu.HBM),
                pl.BlockSpec((CHUNK, CHUNK), lambda s, n, *_: (0, 0)),
            ],
            out_specs=pl.BlockSpec(block, lambda s, n, *_: (s, n, 0, 0)),
            scratch_shapes=theta_scratch(theta),
        ),
        cost_estimate=pl.CostEstimate(flops=6 * 10**9, bytes_accessed=12 * 2**20, transcendentals=0),
        compiler_params=pltpu.CompilerParams(vmem_limit_bytes=14 * MIB),
        name="gate_rows",
    )(ids, slot_sector, block_offsets, pltpu.with_memory_space_constraint(theta, pltpu.HBM), gate)


def product_body(count, lhs_ref, *refs):
    vector_refs = refs[:count]
    sent_ref, kept_ref = refs[count:]
    rows = sent_ref.shape[2]
    for n in range(count):
        out = jnp.dot(lhs_ref[0, n], vector_refs[n][0], preferred_element_type=f32)
        sent_ref[0, n] = out[:rows].astype(bf16)
        kept_ref[0, n] = out[rows:]


def product(slot, chunk, gated, vectors):
    _, _, rows, depth = gated.shape
    count = len(vectors)
    most = vectors[0].shape[2]
    out_block = (1, count, rows // 2, most)
    return pl.pallas_call(
        functools.partial(product_body, count),
        out_shape=(jax.ShapeDtypeStruct(out_block, bf16), jax.ShapeDtypeStruct(out_block, f32)),
        grid=(1,),
        in_specs=[pl.BlockSpec((1, count, rows, depth), lambda i: (slot, chunk, 0, 0))]
        + [pl.BlockSpec((1, depth, most), lambda i, at=min(slot, v.shape[0] - 1): (at, 0, 0)) for v in vectors],
        out_specs=(pl.BlockSpec(out_block, lambda i: (0, 0, 0, 0)),) * 2,
        cost_estimate=pl.CostEstimate(flops=8 * 10**8, bytes_accessed=5 * 2**20, transcendentals=0),
        compiler_params=pltpu.CompilerParams(vmem_limit_bytes=16 * MIB),
    )(gated, *vectors)


PACK = 16


def packed(diag):
    high = diag.astype(bf16)
    rest = diag - high.astype(f32)
    middle = rest.astype(bf16)
    low = (rest - middle.astype(f32)).astype(bf16)
    row = lax.broadcasted_iota(jnp.int32, (PACK, diag.shape[1]), 0)
    wide = [jnp.broadcast_to(x.astype(f32), row.shape) for x in (high, middle, low)]
    return jnp.where(row == 0, wide[0], jnp.where(row == 1, wide[1], jnp.where(row == 2, wide[2], 0.0))).astype(bf16)


def unpacked(block):
    return jnp.sum(block.astype(f32), axis=0, keepdims=True)


def bit_of(ids, which, halves):
    source, shift = which
    value = {"row": ids[0], "group": ids[1] // halves, "half": ids[1] % halves}[source]
    return (value >> shift) & 1


def corr_body(halves, ids, corr_ref, sent_ref, stays_ref, diag_ref):
    slots, count, rows, most = stays_ref.shape
    mine = bit_of(ids, ("group", 0), halves)
    for s in range(slots):
        diag = jnp.zeros((1, most), f32)
        for n in range(2 * count):
            i = n * rows + lax.broadcasted_iota(jnp.int32, (rows, most), 0)
            j = lax.broadcasted_iota(jnp.int32, (rows, most), 1)
            diag = diag + jnp.sum(jnp.where(i == j, corr_ref[s, n], 0.0), axis=0, keepdims=True)
        diag_ref[s] = diag
        for n in range(count):
            stays_ref[s, n] = corr_ref[s, 2 * n + mine]
            sent_ref[s, pl.ds(n * rows, rows), :] = corr_ref[s, 2 * n + 1 - mine].astype(bf16)
        sent_ref[s, pl.ds(count * rows, PACK), :] = packed(diag)


def corr_split(ids, corr, halves):
    slots, count, rows, most = corr.shape
    count = count // 2
    return pl.pallas_call(
        functools.partial(corr_body, halves),
        out_shape=(
            jax.ShapeDtypeStruct((slots, count * rows + PACK, most), bf16),
            jax.ShapeDtypeStruct((slots, count, rows, most), f32),
            jax.ShapeDtypeStruct((slots, 1, most), f32),
        ),
        in_specs=[SMEM, VMEM],
        out_specs=(VMEM,) * 3,
        cost_estimate=pl.CostEstimate(flops=10**6, bytes_accessed=2**21, transcendentals=0),
        compiler_params=pltpu.CompilerParams(vmem_limit_bytes=8 * MIB),
        name="corr_split",
    )(ids, corr)


def step_body(which, halves, ids, stays_in, taken_ref, diag_in, sent_ref, stays_ref, diag_ref):
    slots, count, rows, _ = stays_ref.shape
    before, block = stays_in.shape[1:3]
    mine = bit_of(ids, which, halves) if which else 0
    for s in range(slots):
        diag = diag_in[s] + unpacked(taken_ref[s, pl.ds(before * block, PACK), :])
        diag_ref[s] = diag

        def total(at, first=0):
            there = pl.multiple_of(at * block + first, rows)
            return stays_in[s, at, pl.ds(first, rows), :] + taken_ref[s, pl.ds(there, rows), :].astype(f32)

        for n in range(count):
            if not which:
                value = total(n)
                stays_ref[s, n] = value
            elif block != rows:
                stays_ref[s, n] = total(n, pl.multiple_of(mine * rows, rows))
                value = total(n, pl.multiple_of((1 - mine) * rows, rows))
            else:
                stays_ref[s, n] = total(2 * n + mine)
                value = total(2 * n + 1 - mine)
            sent_ref[s, pl.ds(n * rows, rows), :] = value.astype(bf16)
        sent_ref[s, pl.ds(count * rows, PACK), :] = packed(diag)


def step(ids, stays, taken, diag, which, halves):
    slots, count, rows, most = stays.shape
    if which and which[0] == "half":
        rows = rows // halves
    elif which:
        count = count // 2
    return pl.pallas_call(
        functools.partial(step_body, which, halves),
        out_shape=(
            jax.ShapeDtypeStruct((slots, count * rows + PACK, most), bf16),
            jax.ShapeDtypeStruct((slots, count, rows, most), f32),
            jax.ShapeDtypeStruct((slots, 1, most), f32),
        ),
        in_specs=[SMEM] + [VMEM] * 3,
        out_specs=(VMEM,) * 3,
        cost_estimate=pl.CostEstimate(flops=10**6, bytes_accessed=2**19, transcendentals=0),
        compiler_params=pltpu.CompilerParams(vmem_limit_bytes=8 * MIB),
    )(ids, stays, taken, diag)


def total_body(message, stays_in, taken_ref, diag_in, *refs):
    slots, _, rows, _ = stays_in.shape
    for s in range(slots):
        diag = diag_in[s] + unpacked(taken_ref[s, pl.ds(rows, PACK), :])
        value = stays_in[s, 0] + taken_ref[s, pl.ds(0, rows), :].astype(f32)
        if message:
            refs[0][s, pl.ds(0, rows), :] = value.astype(bf16)
            refs[0][s, pl.ds(rows, PACK), :] = packed(diag)
        else:
            refs[0][s, 0] = value
            refs[1][s] = diag


def total(stays, taken, diag, message):
    shapes = (
        (jax.ShapeDtypeStruct(taken.shape, bf16),)
        if message
        else (jax.ShapeDtypeStruct(stays.shape, f32), jax.ShapeDtypeStruct(diag.shape, f32))
    )
    return pl.pallas_call(
        functools.partial(total_body, message),
        out_shape=shapes,
        in_specs=[VMEM] * 3,
        out_specs=(VMEM,) * len(shapes),
        cost_estimate=pl.CostEstimate(flops=10**6, bytes_accessed=2**19, transcendentals=0),
        compiler_params=pltpu.CompilerParams(vmem_limit_bytes=4 * MIB),
    )(stays, taken, diag)


def gram_body(parts, ids, *refs):
    projected_ref, sent_ref, stays_ref, diag_ref, gram = refs[2 * parts :]
    _, count, rows, most = stays_ref.shape
    width = most // parts
    for n in range(parts):
        part = (refs[2 * n][0, 0] + refs[2 * n + 1][0, 0].astype(f32)).astype(bf16)
        projected_ref[:, n * width : (n + 1) * width] = part
    projected = projected_ref[...]
    gram[...] = lax.dot_general(projected, projected, (((0,), (0,)), ((), ())), preferred_element_type=f32)
    wide = projected.astype(f32)
    diag = jnp.sum(wide * wide, axis=0, keepdims=True)
    diag_ref[0] = diag
    mine = ids[0] & 1
    for n in range(count):
        stays_ref[0, n] = gram[pl.ds(pl.multiple_of((2 * n + mine) * rows, rows), rows), :]
        other = gram[pl.ds(pl.multiple_of((2 * n + 1 - mine) * rows, rows), rows), :]
        sent_ref[0, pl.ds(n * rows, rows), :] = other.astype(bf16)
    sent_ref[0, pl.ds(count * rows, PACK), :] = packed(diag)


def gram_split(ids, values, groups):
    depth, most = values[0][0].shape[2:]
    most = most * len(values)
    rows, count = most // groups, groups // 2
    operands = [x for value in values for x in value]
    return pl.pallas_call(
        functools.partial(gram_body, len(values)),
        out_shape=(
            jax.ShapeDtypeStruct((depth, most), bf16),
            jax.ShapeDtypeStruct((1, count * rows + PACK, most), bf16),
            jax.ShapeDtypeStruct((1, count, rows, most), f32),
            jax.ShapeDtypeStruct((1, 1, most), f32),
        ),
        in_specs=[SMEM] + [VMEM] * len(operands),
        out_specs=(VMEM,) * 4,
        scratch_shapes=[pltpu.VMEM((most, most), f32)],
        cost_estimate=pl.CostEstimate(flops=2 * depth * most * most, bytes_accessed=2**20, transcendentals=0),
        compiler_params=pltpu.CompilerParams(vmem_limit_bytes=6 * MIB),
        name="gram_split",
    )(ids, *operands)


def refine_body(slot, per_group, ids, sectors_ref, kept_ref, gram_ref, corr_ref, cdiag_ref, out_ref):
    rows, most = out_ref.shape
    first = ids[1] * rows
    rank = kept_ref[sectors_ref[ids[0] * per_group + slot]]
    gram = gram_ref[0, pl.ds(0, rows), :].astype(f32)
    gdiag = unpacked(gram_ref[0, pl.ds(rows, PACK), :])
    cdiag = cdiag_ref[slot]
    lam = gdiag / (cdiag + 1e-06)
    i = first + lax.broadcasted_iota(jnp.int32, (rows, most), 0)
    j = lax.broadcasted_iota(jnp.int32, (rows, most), 1)
    lam_j = jnp.broadcast_to(lam, (rows, most))
    lam_i = jnp.sum(jnp.where(i == j, lam_j, 0.0), axis=1, keepdims=True)
    differ = lam_j - lam_i
    total = damping * (lam_i + lam_j)
    divisor = differ * differ + total * total + 1e-06
    offdiag = (gram - lam_j * corr_ref[slot, 0]) * differ / divisor
    result = jnp.where(i == j, 0.5 * (1.0 - cdiag), offdiag)
    inside = (i < rank) & (j < rank)
    out_ref[...] = jnp.where(inside, result, 0.0).astype(bf16)


def refine(slot, ids, slot_sector, kept, gram, corr, cdiag, per_group):
    _, _, rows, most = corr.shape
    return pl.pallas_call(
        functools.partial(refine_body, slot, per_group),
        out_shape=jax.ShapeDtypeStruct((rows, most), bf16),
        in_specs=[SMEM] * 3 + [VMEM] * 3,
        out_specs=VMEM,
        cost_estimate=pl.CostEstimate(flops=10**6, bytes_accessed=2**19, transcendentals=0),
        compiler_params=pltpu.CompilerParams(vmem_limit_bytes=4 * MIB),
        name="refine",
    )(ids, slot_sector, kept, gram, corr, cdiag)


def final_body(slot, per_group, halves, order, ids, sectors_ref, kept_ref, vectors_ref, left_ref, own_ref, other_ref, *refs):
    right_out, left_out, corr = refs[-3:]
    rows, most = own_ref.shape[0] // len(order), own_ref.shape[1]
    rank = kept_ref[sectors_ref[ids[0] * per_group + slot]]

    def finish(narrow):
        out = narrow.astype(f32) + jnp.dot(narrow, corr[...], preferred_element_type=f32)
        j = lax.broadcasted_iota(jnp.int32, out.shape, 1)
        return jnp.where(j < rank, out, 0.0)

    @pl.when(pl.program_id(0) == 0)
    def _():
        half = ids[1] % halves
        for n, k in enumerate(order):
            at = ((ids[1] // halves) ^ k) * halves
            mine, others = pl.multiple_of((at + half) * rows, rows), pl.multiple_of((at + 1 - half) * rows, rows)
            corr[pl.ds(mine, rows), :] = own_ref[pl.ds(n * rows, rows), :]
            corr[pl.ds(others, rows), :] = other_ref[pl.ds(n * rows, rows), :]
        out = finish(left_ref[...])
        left_out[:, 0] = out.reshape(out.shape[0] // 4, 4, most)

    right_out[0] = finish(vectors_ref[0])


def final(slot, ids, slot_sector, kept, vectors, left, own, other, order, carried, halves):
    per_group, depth, most = vectors.shape
    tile = depth // 2
    rows = left.shape[0] // 4
    whole = lambda shape: pl.BlockSpec(shape, lambda t, *_: (0,) * len(shape))
    right_shape = jax.ShapeDtypeStruct((per_group, depth, most), f32)
    left_shape = jax.ShapeDtypeStruct((rows, per_group, 4, most), f32)
    in_specs = [
        pl.BlockSpec((1, tile, most), lambda t, *_: (slot, t, 0)),
        whole(left.shape),
        whole(own.shape),
        whole(other.shape),
    ]
    operands = [vectors, left, own, other]
    aliases = {}
    if carried is not None:
        aliases = {3 + len(operands): 0, 4 + len(operands): 1}
        in_specs += [pl.BlockSpec(memory_space=pl.ANY)] * 2
        operands += list(carried)
    return pl.pallas_call(
        functools.partial(final_body, slot, per_group, halves, order),
        out_shape=(right_shape, left_shape),
        grid_spec=pltpu.PrefetchScalarGridSpec(
            num_scalar_prefetch=3,
            grid=(depth // tile,),
            in_specs=in_specs,
            out_specs=(
                pl.BlockSpec((1, tile, most), lambda t, *_: (slot, t, 0)),
                pl.BlockSpec((rows, 1, 4, most), lambda t, *_: (0, slot, 0, 0)),
            ),
            scratch_shapes=[pltpu.VMEM((most, most), bf16)],
        ),
        input_output_aliases=aliases,
        cost_estimate=pl.CostEstimate(flops=2 * 1216 * most * most, bytes_accessed=4 * 2**20, transcendentals=0),
        compiler_params=pltpu.CompilerParams(vmem_limit_bytes=12 * MIB),
        name="final",
    )(ids, slot_sector, kept, *operands)


def halve_body(shift, halves, first, ids, stays_in, taken_in, *refs):
    other, (sent_ref, stays_ref) = refs[:-2], refs[-2:]
    most = stays_ref.shape[3]
    want = (((ids[1] // halves) ^ ids[0]) >> shift) & 1
    for s in range(stays_ref.shape[0]):
        for n in range(stays_ref.shape[1]):
            if other:
                part = pl.ds(first, most)
                low = stays_in[0, 0, :, part] + taken_in[0, 0, :, part].astype(f32)
                high = other[0][0, 0] + other[1][0, 0].astype(f32)
                stays_ref[s, n] = jnp.where(want == 1, high, low)
                sent_ref[s, n] = jnp.where(want == 1, low, high).astype(bf16)
            else:
                at = 2 * n + want
                stays_ref[s, n] = stays_in[s, at] + taken_in[s, at].astype(f32)
                at = 2 * n + 1 - want
                sent_ref[s, n] = (stays_in[s, at] + taken_in[s, at].astype(f32)).astype(bf16)


def halve(ids, shift, halves, value, other=None, first=0):
    slots, count, rows, most = (other or value)[0].shape
    shape = (1, 1, rows, most) if other else (slots, count // 2, rows, most)
    operands = list(value) + list(other or ())
    return pl.pallas_call(
        functools.partial(halve_body, shift, halves, first),
        out_shape=(jax.ShapeDtypeStruct(shape, bf16), jax.ShapeDtypeStruct(shape, f32)),
        in_specs=[SMEM] + [VMEM] * len(operands),
        out_specs=(VMEM,) * 2,
        cost_estimate=pl.CostEstimate(flops=10**6, bytes_accessed=2**20, transcendentals=0),
        compiler_params=pltpu.CompilerParams(vmem_limit_bytes=8 * MIB),
    )(ids, *operands)


def work(theta, gate, warm_start, slot_sector, kept, block_offsets):
    groups, cols = lax.axis_size("row"), lax.axis_size("col")
    block, col = lax.axis_index("row"), lax.axis_index("col")
    halves = cols // groups
    per_group, _, bond_cols, most = warm_start.shape
    group_bits = groups.bit_length() - 1
    ids = jnp.stack([block, col]).astype(jnp.int32)
    vectors = warm_start.reshape(per_group, 4 * bond_cols, most)
    gate_matrix = gate.reshape(CHUNK, CHUNK)

    parts = [1] * (per_group - 1) + [2]

    across = {}
    remaining = vectors
    for s in range(per_group):
        width = most // parts[s]
        for p in range(parts[s]):
            own = remaining[s : s + 1, :, p * width : (p + 1) * width]
            own, remaining = lax.optimization_barrier((own, remaining))
            across[s, p] = {d: swap(own, "row", d) for d in range(2, groups, 2)}
    partner = swap(vectors, "row", 1)

    def place(b, g, h):
        return b * cols + g * halves + h

    def turned(value):
        pairs = [
            (place(b, g, h), place(g, b, h))
            for b in range(groups)
            for g in range(groups)
            for h in range(halves)
        ]
        return lax.ppermute(value, ("row", "col"), pairs)

    corr = jnp.einsum("snk,snl->skl", vectors, vectors, preferred_element_type=f32)
    corr = corr.reshape(per_group, groups, most // groups, most)
    sent, stays, diag = corr_split(ids, corr, halves)
    for t in range(group_bits):
        taken = swap(sent, "col", halves << t)
        which = ("group", t + 1) if t + 1 < group_bits else ("half", 0)
        sent, stays, diag = step(ids, stays, taken, diag, which, halves)
    taken = swap(sent, "col", 1)
    corr, cdiag = total(stays, taken, diag, False)

    def reduced(sent, stays):
        taken = swap(sent, "col", 1)
        for t in range(group_bits - 1):
            sent, stays = halve(ids, t, halves, (stays, taken))
            taken = swap(sent, "col", halves << t)
        return stays, taken

    gated = gate_rows(ids, slot_sector, block_offsets, theta, gate_matrix, groups, halves, per_group)
    near = []
    for s in range(per_group):
        operands = [vectors, partner]
        for d in range(2, groups // 2, 2):
            arrived = jnp.concatenate([across[s, p][d] for p in range(parts[s])], axis=2)
            operands += [arrived, swap(arrived, "row", 1)]
        value = product(s, 0, gated, operands)
        near.append(reduced(*value))
    last = group_bits - 1
    carried = None
    for s in range(per_group):
        values = []
        for p in range(parts[s]):
            far = []
            for d in range(groups // 2, groups, 2):
                far += [across[s, p][d], swap(across[s, p][d], "row", 1)]
            far = product(s, 1, gated, far)
            far = reduced(*far)
            sent, stays = halve(ids, last, halves, near[s], far, p * (most // parts[s]))
            values.append((stays, swap(sent, "col", halves << last)))
        projected, sent, stays, diag = gram_split(ids, values, groups)
        left = turned(projected)
        for t in range(1, group_bits + 1):
            taken = swap(sent, "row", 1 << (t - 1))
            which = ("row", t) if t < group_bits else ("half", 0)
            sent, stays, diag = step(ids, stays, taken, diag, which, halves)
        taken = swap(sent, "col", 1)
        (sent,) = total(stays, taken, diag, True)
        gram = turned(sent)
        piece = refine(s, ids, slot_sector, kept, gram, corr, cdiag, per_group)
        order = list(range(groups))
        pieces = [piece]
        for k in order[1:]:
            pieces.append(swap(piece, "col", halves * k))
        own = jnp.concatenate(pieces)
        other = swap(own, "col", 1)
        carried = final(s, ids, slot_sector, kept, vectors, left, own, other, order, carried, halves)
    right, left = carried
    return left, right.reshape(warm_start.shape)


def solution(mesh):
    in_specs = (P("row", None, None, "col"), P(), P("row", None, "col", None), P(), P(), P())
    out_specs = (P("col", "row", None, None), P("row", None, "col", None))
    return jax.shard_map(work, mesh=mesh, in_specs=in_specs, out_specs=out_specs, check_vma=False)
```
